128 devices in a mesh: req: 16 (over y, z), head: 8 (over x, core).
Axes of the slice: x: 4, y: 4, z: 4, core: 2. Of those that a mesh axis runs over, the one named last changes fastest.
Arguments:
- hidden: bfloat16 [2048, 6144], P('req'), may hold values from -15 to 15
- attn_norm_gain: float32 [6144], replicated, may hold values from 0.3 to 3
- attn_norm_bias: float32 [6144], replicated, may hold values from -4 to 4
- mlp_norm_gain: float32 [6144], replicated, may hold values from 0.3 to 3
- mlp_norm_bias: float32 [6144], replicated, may hold values from -4 to 4
- qkv_weight: bfloat16 [6144, 9216], P('req', 'head'), may hold values from -0.078125 to 0.078125
- qkv_bias: float32 [9216], P('head'), may hold values from -3 to 3
- out_weight: bfloat16 [3072, 6144], P('head', 'req'), may hold values from -0.625 to 0.625
- out_bias: float32 [6144], replicated, may hold values from -3 to 3
- up_weight: bfloat16 [6144, 12288], P('req', 'head'), may hold values from -0.078125 to 0.078125
- up_bias: float32 [12288], P('head'), may hold values from -3 to 3
- down_weight: bfloat16 [12288, 6144], P('head', 'req'), may hold values from -0.0546875 to 0.0546875
- down_bias: float32 [6144], replicated, may hold values from -3 to 3
- cache_keys: bfloat16 [16, 4096, 3072], P('req', None, 'head'), may hold values from -1300 to 1300
- cache_values: bfloat16 [16, 4096, 3072], P('req', None, 'head'), may hold values from -6 to 6
- cached_len: int32 [16], P('req'), may hold values from 128 to 4096, as said below
Outputs:
- hidden_out: bfloat16 [2048, 6144], P('req')
- new_keys: bfloat16 [16, 128, 3072], P('req', None, 'head')
- new_values: bfloat16 [16, 128, 3072], P('req', None, 'head')
The draws below stay inside these ranges and needn't reach their ends.
Inputs may be any that keep to these rules, and one draw needn't show every extreme that they name: `cached_len`: each entry is 128 or 4096, and both values occur.
All inputs are finite; a program needn't handle non-finite values.
Results may differ from the reference program's by a relative error of at most 0.0085.
The reference program's roundings to bfloat16 on the way count: a program that leaves them out, or rounds other values in their place, can miss the bound.
Values may be sent and summed in bfloat16 or wider, within the bound.
A program may use at most 128 MiB of HBM per device.

```python
import math
import jax
import jax.numpy as jnp
from jax import lax

D = 6144
HEADS = 32
DH = 96
ROT = 24
FF = 12288
NEW = 128
CACHE = 4096
SHORT = 128
REQS = 16
TOKENS = 2048


def draw_hidden(key, part):
    base_key = jax.random.fold_in(key, 11)
    key_main, key_rows, key_cols = jax.random.split(base_key, 3)
    rows_scale = 0.1 * jnp.exp(jax.random.uniform(key_rows, (TOKENS, 1), jnp.float32) * jnp.log(10.0))
    cols_scale = 0.3 * jnp.exp(jax.random.uniform(key_cols, (1, D), jnp.float32) * jnp.log(10.0))
    base_values = jax.random.normal(key_main, (TOKENS, D), jnp.float32)
    return (jnp.clip(base_values, -5.0, 5.0) * rows_scale * cols_scale).astype(jnp.bfloat16)


def draw_cache_keys(key, part):
    base_key = jax.random.fold_in(key, 23)
    key_main = jax.random.fold_in(base_key, 0)
    base_values = jnp.clip(jax.random.normal(key_main, (REQS, CACHE, HEADS * DH), jnp.float32), -6.0, 6.0)
    return base_values.astype(jnp.bfloat16)


def draw_cached_len(key, part):
    base_key = jax.random.fold_in(key, 37)
    key_long, key_pick = jax.random.split(base_key, 2)
    request_index = jnp.arange(REQS, dtype=jnp.int32)
    chosen = jax.random.randint(key_pick, (), 0, REQS, dtype=jnp.int32)
    long_ones = jax.random.randint(key_long, (REQS,), 0, 4, dtype=jnp.int32) == 0
    long_ones = jnp.logical_or(long_ones, request_index == chosen)
    long_ones = jnp.logical_and(long_ones, request_index != (chosen + 1) % REQS)
    return jnp.where(long_ones, CACHE, SHORT).astype(jnp.int32)


def block_levels(key, extent, cuts, low, largest):
    level = 1.0
    for axis_at, parts in cuts:
        heights = jax.random.uniform(jax.random.fold_in(jax.random.fold_in(key, 6), axis_at), (parts,), jnp.float32, low / len(cuts), largest / len(cuts))
        level = level * jnp.repeat(jnp.exp(heights), extent[axis_at] // parts).reshape((-1,) + (1,) * (len(extent) - 1 - axis_at))
    return level


def noise(rng, extent, scale, most, pieces=(), kind=jnp.bfloat16):
    drawn = jax.random.normal(rng, extent, jnp.float32) * scale
    if len(pieces) > 0:
        drawn = block_levels(rng, extent, pieces, -0.22, 0.18) * drawn
    return jnp.clip(drawn, min=-most, max=most).astype(kind)


def setup_inputs(seed: int = 0) -> dict:
    splits = jax.random.split(jax.random.key(seed), 17)
    hidden = draw_hidden(jax.random.fold_in(splits[16], 71), 0)
    attn_norm_gain = jnp.clip(jnp.exp(jax.random.uniform(splits[1], (D,), jnp.float32, math.log(0.3), math.log(3.0))), 0.3, 3.0)
    attn_norm_bias = noise(splits[2], (D,), 1.0, 4.0, (), jnp.float32)
    mlp_norm_gain = jnp.clip(jnp.exp(jax.random.uniform(splits[3], (D,), jnp.float32, math.log(0.3), math.log(3.0))), 0.3, 3.0)
    mlp_norm_bias = noise(splits[4], (D,), 1.0, 4.0, (), jnp.float32)
    qkv_weight = noise(splits[5], (D, HEADS * 3 * DH), D ** -0.5, 0.078125, ((0, 16), (1, 8)))
    qkv_bias = noise(splits[6], (HEADS * 3 * DH,), 0.5, 3.0, ((0, 8),), jnp.float32)
    out_weight = noise(splits[7], (HEADS * DH, D), DH ** -0.5, 0.625, ((0, 8), (1, 16)))
    out_bias = noise(splits[8], (D,), 0.5, 3.0, (), jnp.float32)
    up_weight = noise(splits[9], (D, FF), D ** -0.5, 0.078125, ((0, 16), (1, 8)))
    up_bias = noise(splits[10], (FF,), 0.5, 3.0, ((0, 8),), jnp.float32)
    down_weight = noise(splits[11], (FF, D), FF ** -0.5, 0.0546875, ((0, 8), (1, 16)))
    down_bias = noise(splits[12], (D,), 0.5, 3.0, (), jnp.float32)
    cache_keys = draw_cache_keys(jax.random.fold_in(splits[16], 71), 0)
    cache_values = noise(splits[14], (REQS, CACHE, HEADS * DH), 1.0, 6.0, ((0, 16), (2, 8)))
    cached_len = draw_cached_len(jax.random.fold_in(splits[16], 71), 0)
    return dict(hidden=hidden, attn_norm_gain=attn_norm_gain, attn_norm_bias=attn_norm_bias, mlp_norm_gain=mlp_norm_gain, mlp_norm_bias=mlp_norm_bias, qkv_weight=qkv_weight, qkv_bias=qkv_bias, out_weight=out_weight, out_bias=out_bias, up_weight=up_weight, up_bias=up_bias, down_weight=down_weight, down_bias=down_bias, cache_keys=cache_keys, cache_values=cache_values, cached_len=cached_len)


def normalize(values, norm_gain, norm_shift):
    widened = values.astype(jnp.float32)
    center = lax.optimization_barrier(jnp.mean(widened, axis=-1, keepdims=True))
    spread = lax.optimization_barrier(jnp.mean(jnp.square(widened - center), axis=-1, keepdims=True))
    return ((widened - center) * lax.rsqrt(spread + 1e-05) * norm_gain + norm_shift).astype(jnp.bfloat16)

def rotate(values, position):
    halfway = ROT // 2
    exponent = jnp.arange(halfway, dtype=jnp.float32) * (2.0 / ROT)
    frequency = jnp.power(10000.0, -exponent)
    angle = position[:, None] * frequency[None, :]
    cosine = jnp.cos(angle)[:, None, :]
    sine_part = jnp.sin(angle)[:, None, :]
    lower_half = values[..., :halfway]
    upper_half = values[..., halfway:ROT]
    return jnp.concatenate([lower_half * cosine - upper_half * sine_part, upper_half * cosine + lower_half * sine_part, values[..., ROT:]], axis=-1)

def attend_one(inputs):
    qkv_rows, keys_old, values_old, length = inputs
    position = length.astype(jnp.float32) + jnp.arange(NEW, dtype=jnp.float32)
    queries = rotate(qkv_rows[:, :, 0], position).astype(jnp.bfloat16)
    key_new = rotate(qkv_rows[:, :, 1], position).astype(jnp.bfloat16)
    value_new = qkv_rows[:, :, 2].astype(jnp.bfloat16)
    all_keys = jnp.concatenate([keys_old, key_new], axis=0).astype(jnp.float32)
    all_values = jnp.concatenate([values_old, value_new], axis=0).astype(jnp.float32)
    scores = jnp.einsum('qhd,khd->hqk', queries.astype(jnp.float32), all_keys) * (1.0 / math.sqrt(DH))
    key_index = jnp.arange(CACHE + NEW, dtype=jnp.int32)
    query_index = jnp.arange(NEW, dtype=jnp.int32)
    visible = jnp.where(key_index[None, :] < CACHE, key_index[None, :] < length, key_index[None, :] - CACHE <= query_index[:, None])
    scores = jnp.where(visible[None], scores, -1e+30)
    highest = lax.optimization_barrier(jnp.max(scores, axis=-1, keepdims=True))
    weights = jnp.exp(scores - highest)
    totals = lax.optimization_barrier(jnp.sum(weights, axis=-1))
    rounded = lax.optimization_barrier(weights.astype(jnp.bfloat16)).astype(jnp.float32)
    mixed = jnp.einsum('hqk,khd->qhd', rounded, all_values) / jnp.transpose(totals)[:, :, None]
    return (mixed.astype(jnp.bfloat16).reshape(NEW, HEADS * DH), key_new.reshape(NEW, HEADS * DH), value_new.reshape(NEW, HEADS * DH))

def reference(hidden, attn_norm_gain, attn_norm_bias, mlp_norm_gain, mlp_norm_bias, qkv_weight, qkv_bias, out_weight, out_bias, up_weight, up_bias, down_weight, down_bias, cache_keys, cache_values, cached_len):
    attn_normed = normalize(hidden, attn_norm_gain, attn_norm_bias)
    mlp_normed = normalize(hidden, mlp_norm_gain, mlp_norm_bias)
    qkv = jnp.dot(attn_normed, qkv_weight, preferred_element_type=jnp.float32) + qkv_bias
    up_sum = jnp.dot(mlp_normed, up_weight, preferred_element_type=jnp.float32) + up_bias
    units = jax.nn.gelu(up_sum, approximate=True).astype(jnp.bfloat16)
    per_request = qkv.reshape(REQS, NEW, HEADS, 3, DH)
    keys_old = cache_keys.reshape(REQS, CACHE, HEADS, DH)
    values_old = cache_values.reshape(REQS, CACHE, HEADS, DH)
    attended, new_keys, new_values = lax.map(attend_one, (per_request, keys_old, values_old, cached_len))
    attended = attended.reshape(TOKENS, HEADS * DH)
    attention = jnp.dot(attended, out_weight, preferred_element_type=jnp.float32)
    feed_forward = jnp.dot(units, down_weight, preferred_element_type=jnp.float32)
    hidden_out = (hidden.astype(jnp.float32) + attention + out_bias + feed_forward + down_bias).astype(jnp.bfloat16)
    return (hidden_out, new_keys, new_values)
```

```python
import functools
import math

import jax
import jax.numpy as jnp
from jax import lax
from jax.experimental import pallas as pl
from jax.experimental.pallas import tpu as pltpu
from jax.sharding import PartitionSpec as P

DH = 96
ROT = 24
NEW = 128
CACHE = 4096
KB = 512
NT = (((1,), (1,)), ((), ()))


def normalize(values, norm_gain, norm_shift):
    widened = values.astype(jnp.float32)
    center = jnp.mean(widened, axis=-1, keepdims=True)
    spread = jnp.mean(jnp.square(widened - center), axis=-1, keepdims=True)
    return ((widened - center) * lax.rsqrt(spread + 1e-05) * norm_gain + norm_shift).astype(
        jnp.bfloat16
    )


def rotation_tables(length):
    position = length.astype(jnp.float32) + jnp.arange(NEW, dtype=jnp.float32)
    halfway = ROT // 2
    exponent = jnp.arange(halfway, dtype=jnp.float32) * (2.0 / ROT)
    frequency = jnp.power(10000.0, -exponent)
    angle = position[None, :] * frequency[:, None]
    cosine, sine = jnp.cos(angle), jnp.sin(angle)
    return jnp.concatenate([cosine, cosine], 0), jnp.concatenate([-sine, sine], 0)


def attention_kernel(
    heads, len_ref, qkv_ref, bias_ref, cos_ref, sin_ref, k_hbm, v_hbm,
    att_ref, nk_ref, nv_ref, kbuf, vbuf, sbuf, qexp, ksem, vsem,
):
    scale = 1.0 / math.sqrt(DH)
    length = len_ref[0]
    width = heads * DH
    blocks = CACHE // KB
    used = (length + KB - 1) // KB

    def fetch(i, hbm, buf, sem):
        rows = pl.ds(pl.multiple_of(i * KB, KB), KB)
        return pltpu.make_async_copy(hbm.at[rows], buf.at[rows], sem.at[i])

    for hbm, buf, sem in ((k_hbm, kbuf, ksem), (v_hbm, vbuf, vsem)):
        @pl.loop(0, used)
        def _(i):
            fetch(i, hbm, buf, sem).start()

    cosine, sine = cos_ref[...], sin_ref[...]

    def turned(rows):
        low = rows[:ROT]
        swapped = jnp.concatenate([low[ROT // 2:], low[: ROT // 2]], axis=0)
        return jnp.concatenate([low * cosine + swapped * sine, rows[ROT:]], axis=0)

    def block(j, part):
        at = pl.ds((3 * j + part) * DH, DH)
        return qkv_ref[at, :] + bias_ref[at, :]

    queries = jnp.concatenate([turned(block(j, 0)) for j in range(heads)], 0).T.astype(jnp.bfloat16)
    keys = jnp.concatenate([turned(block(j, 1)) for j in range(heads)], 0).T.astype(jnp.bfloat16)
    values = jnp.concatenate([block(j, 2) for j in range(heads)], 0).T.astype(jnp.bfloat16)
    nk_ref[...] = keys
    nv_ref[...] = values
    lane_head = lax.broadcasted_iota(jnp.int32, (NEW, width), 1) // DH
    for j in range(heads):
        qexp[pl.ds(j * NEW, NEW), :] = jnp.where(lane_head == j, queries, jnp.zeros_like(queries))
    rows = heads * NEW
    fresh = lax.dot_general(qexp[...], keys, NT, preferred_element_type=jnp.float32) * scale
    row_at = lax.broadcasted_iota(jnp.int32, (rows, NEW), 0) % NEW
    col_at = lax.broadcasted_iota(jnp.int32, (rows, NEW), 1)
    fresh = jnp.where(col_at <= row_at, fresh, -1e30)

    def score(i, top):
        fetch(i, k_hbm, kbuf, ksem).wait()
        at = pl.ds(pl.multiple_of(i * KB, KB), KB)
        part = lax.dot_general(qexp[...], kbuf[at, :], NT, preferred_element_type=jnp.float32) * scale
        col = lax.broadcasted_iota(jnp.int32, (rows, KB), 1) + i * KB
        part = jnp.where(col < length, part, -1e30)
        sbuf[:, at] = part
        for t in range(KB // NEW):
            top = jnp.maximum(top, part[:, t * NEW:(t + 1) * NEW])
        return top

    top = lax.fori_loop(0, used, score, fresh)
    highest = jnp.max(top, axis=1, keepdims=True)
    fresh_weights = jnp.exp(fresh - highest)
    mixed = jnp.dot(fresh_weights.astype(jnp.bfloat16), values, preferred_element_type=jnp.float32)

    def weigh(i, carry):
        mixed, total = carry
        fetch(i, v_hbm, vbuf, vsem).wait()
        at = pl.ds(pl.multiple_of(i * KB, KB), KB)
        weights = jnp.exp(sbuf[:, at] - highest)
        for t in range(KB // NEW):
            total = total + weights[:, t * NEW:(t + 1) * NEW]
        mixed = mixed + jnp.dot(weights.astype(jnp.bfloat16), vbuf[at, :], preferred_element_type=jnp.float32)
        return mixed, total

    mixed, total = lax.fori_loop(0, used, weigh, (mixed, fresh_weights))
    total = jnp.sum(total, axis=1, keepdims=True)
    out = jnp.zeros((NEW, width), jnp.float32)
    for j in range(heads):
        at = slice(j * NEW, (j + 1) * NEW)
        out = jnp.where(lane_head == j, mixed[at] / total[at], out)
    att_ref[...] = out.astype(jnp.bfloat16)


def attention(qkv_t, bias, length, keys_old, values_old):
    heads = qkv_t.shape[0] // (3 * DH)
    width = heads * DH
    cosine, sine = rotation_tables(length[0])
    vmem = pl.BlockSpec(memory_space=pltpu.VMEM)
    hbm = pl.BlockSpec(memory_space=pl.ANY)
    out = jax.ShapeDtypeStruct((NEW, width), jnp.bfloat16)
    return pl.pallas_call(
        functools.partial(attention_kernel, heads),
        out_shape=(out, out, out),
        in_specs=[pl.BlockSpec(memory_space=pltpu.SMEM), vmem, vmem, vmem, vmem, hbm, hbm],
        out_specs=(vmem, vmem, vmem),
        scratch_shapes=[
            pltpu.VMEM((CACHE, width), jnp.bfloat16),
            pltpu.VMEM((CACHE, width), jnp.bfloat16),
            pltpu.VMEM((heads * NEW, CACHE), jnp.float32),
            pltpu.VMEM((heads * NEW, width), jnp.bfloat16),
            pltpu.SemaphoreType.DMA((CACHE // KB,)),
            pltpu.SemaphoreType.DMA((CACHE // KB,)),
        ],
        compiler_params=pltpu.CompilerParams(vmem_limit_bytes=60 * 2**20),
        name="attention",
    )(length, qkv_t, bias[:, None], cosine, sine, keys_old, values_old)


def body(
    hidden,
    attn_norm_gain,
    attn_norm_bias,
    mlp_norm_gain,
    mlp_norm_bias,
    qkv_weight,
    qkv_bias,
    out_weight,
    out_bias,
    up_weight,
    up_bias,
    down_weight,
    down_bias,
    cache_keys,
    cache_values,
    cached_len,
):
    qkv_cols = qkv_weight.shape[1]
    attn_normed = normalize(hidden, attn_norm_gain, attn_norm_bias)
    mlp_normed = normalize(hidden, mlp_norm_gain, mlp_norm_bias)
    attn_blocks, mlp_blocks = (
        lax.all_to_all(attn_normed, "req", split_axis=1, concat_axis=0, tiled=True),
        lax.all_to_all(mlp_normed, "req", split_axis=1, concat_axis=0, tiled=True),
    )
    qkv_term = jnp.dot(attn_blocks, qkv_weight, preferred_element_type=jnp.float32)
    up_term = jnp.dot(mlp_blocks, up_weight, preferred_element_type=jnp.float32)
    summed = lax.psum_scatter(
        jnp.concatenate([qkv_term, up_term], axis=1), "req", scatter_dimension=0, tiled=True
    )
    qkv_sum = summed[:, :qkv_cols]
    up_sum = summed[:, qkv_cols:]
    units = jax.nn.gelu(up_sum + up_bias, approximate=True).astype(jnp.bfloat16)
    attended_rows, key_rows, value_rows = attention(
        qkv_sum.T, qkv_bias, cached_len, cache_keys[0], cache_values[0]
    )
    new_keys, new_values = key_rows[None], value_rows[None]
    joined = jnp.concatenate([attended_rows, units], axis=1)
    head_width = attended_rows.shape[1]
    shard_rows = lax.all_gather(joined, "req", axis=0, tiled=True)
    attention_part = jnp.dot(
        shard_rows[:, :head_width], out_weight, preferred_element_type=jnp.float32
    )
    partial_out = attention_part + jnp.dot(
        shard_rows[:, head_width:], down_weight, preferred_element_type=jnp.float32
    )
    bias_total = out_bias + down_bias
    spread_out = lax.all_to_all(partial_out, "req", split_axis=0, concat_axis=1, tiled=True)
    summed_out = lax.psum(spread_out, "head")
    result = (hidden.astype(jnp.float32) + summed_out + bias_total).astype(jnp.bfloat16)
    return (result, new_keys, new_values)


def solution(mesh):
    return jax.shard_map(
        body,
        mesh=mesh,
        in_specs=(
            P("req", None),
            P(),
            P(),
            P(),
            P(),
            P("req", "head"),
            P("head"),
            P("head", "req"),
            P(),
            P("req", "head"),
            P("head"),
            P("head", "req"),
            P(),
            P("req", None, "head"),
            P("req", None, "head"),
            P("req"),
        ),
        out_specs=(P("req", None), P("req", None, "head"), P("req", None, "head")),
        check_vma=False,
    )
```

```python
import functools
import math

import jax
import jax.numpy as jnp
from jax import lax
from jax.experimental import pallas as pl
from jax.experimental.pallas import tpu as pltpu
from jax.sharding import PartitionSpec as P

DH = 96
ROT = 24
NEW = 128
CACHE = 4096
KB = 512
NT = (((1,), (1,)), ((), ()))


def rotation_tables(length):
    position = length.astype(jnp.float32) + jnp.arange(NEW, dtype=jnp.float32)
    halfway = ROT // 2
    exponent = jnp.arange(halfway, dtype=jnp.float32) * (2.0 / ROT)
    frequency = jnp.power(10000.0, -exponent)
    angle = position[None, :] * frequency[:, None]
    cosine, sine = jnp.cos(angle), jnp.sin(angle)
    return jnp.concatenate([cosine, cosine], 0), jnp.concatenate([-sine, sine], 0)


def attention_kernel(
    heads, len_ref, qkv_ref, bias_ref, cos_ref, sin_ref, k_hbm, v_hbm,
    att_ref, nk_ref, nv_ref, kbuf, vbuf, sbuf, qexp, ksem, vsem,
):
    scale = 1.0 / math.sqrt(DH)
    length = len_ref[0]
    width = heads * DH
    blocks = CACHE // KB
    used = (length + KB - 1) // KB

    def fetch(i, hbm, buf, sem):
        rows = pl.ds(pl.multiple_of(i * KB, KB), KB)
        return pltpu.make_async_copy(hbm.at[rows], buf.at[rows], sem.at[i])

    for hbm, buf, sem in ((k_hbm, kbuf, ksem), (v_hbm, vbuf, vsem)):
        @pl.loop(0, used)
        def _(i):
            fetch(i, hbm, buf, sem).start()

    cosine, sine = cos_ref[...], sin_ref[...]

    def turned(rows):
        low = rows[:ROT]
        swapped = jnp.concatenate([low[ROT // 2:], low[: ROT // 2]], axis=0)
        return jnp.concatenate([low * cosine + swapped * sine, rows[ROT:]], axis=0)

    def block(j, part):
        at = pl.ds((3 * j + part) * DH, DH)
        return qkv_ref[at, :] + bias_ref[at, :]

    queries = jnp.concatenate([turned(block(j, 0)) for j in range(heads)], 0).T.astype(jnp.bfloat16)
    keys = jnp.concatenate([turned(block(j, 1)) for j in range(heads)], 0).T.astype(jnp.bfloat16)
    values = jnp.concatenate([block(j, 2) for j in range(heads)], 0).T.astype(jnp.bfloat16)
    nk_ref[...] = keys
    nv_ref[...] = values
    lane_head = lax.broadcasted_iota(jnp.int32, (NEW, width), 1) // DH
    for j in range(heads):
        qexp[pl.ds(j * NEW, NEW), :] = jnp.where(lane_head == j, queries, jnp.zeros_like(queries))
    rows = heads * NEW
    fresh = lax.dot_general(qexp[...], keys, NT, preferred_element_type=jnp.float32) * scale
    row_at = lax.broadcasted_iota(jnp.int32, (rows, NEW), 0) % NEW
    col_at = lax.broadcasted_iota(jnp.int32, (rows, NEW), 1)
    fresh = jnp.where(col_at <= row_at, fresh, -1e30)

    def score(i, top):
        fetch(i, k_hbm, kbuf, ksem).wait()
        at = pl.ds(pl.multiple_of(i * KB, KB), KB)
        part = lax.dot_general(qexp[...], kbuf[at, :], NT, preferred_element_type=jnp.float32) * scale
        col = lax.broadcasted_iota(jnp.int32, (rows, KB), 1) + i * KB
        part = jnp.where(col < length, part, -1e30)
        sbuf[:, at] = part
        for t in range(KB // NEW):
            top = jnp.maximum(top, part[:, t * NEW:(t + 1) * NEW])
        return top

    top = lax.fori_loop(0, used, score, fresh)
    highest = jnp.max(top, axis=1, keepdims=True)
    fresh_weights = jnp.exp(fresh - highest)
    mixed = jnp.dot(fresh_weights.astype(jnp.bfloat16), values, preferred_element_type=jnp.float32)

    def weigh(i, carry):
        mixed, total = carry
        fetch(i, v_hbm, vbuf, vsem).wait()
        at = pl.ds(pl.multiple_of(i * KB, KB), KB)
        weights = jnp.exp(sbuf[:, at] - highest)
        for t in range(KB // NEW):
            total = total + weights[:, t * NEW:(t + 1) * NEW]
        mixed = mixed + jnp.dot(weights.astype(jnp.bfloat16), vbuf[at, :], preferred_element_type=jnp.float32)
        return mixed, total

    mixed, total = lax.fori_loop(0, used, weigh, (mixed, fresh_weights))
    total = jnp.sum(total, axis=1, keepdims=True)
    out = jnp.zeros((NEW, width), jnp.float32)
    for j in range(heads):
        at = slice(j * NEW, (j + 1) * NEW)
        out = jnp.where(lane_head == j, mixed[at] / total[at], out)
    att_ref[...] = out.astype(jnp.bfloat16)


def attention(qkv_t, bias, length, keys_old, values_old):
    heads = qkv_t.shape[0] // (3 * DH)
    width = heads * DH
    cosine, sine = rotation_tables(length[0])
    vmem = pl.BlockSpec(memory_space=pltpu.VMEM)
    hbm = pl.BlockSpec(memory_space=pl.ANY)
    out = jax.ShapeDtypeStruct((NEW, width), jnp.bfloat16)
    return pl.pallas_call(
        functools.partial(attention_kernel, heads),
        out_shape=(out, out, out),
        in_specs=[pl.BlockSpec(memory_space=pltpu.SMEM), vmem, vmem, vmem, vmem, hbm, hbm],
        out_specs=(vmem, vmem, vmem),
        scratch_shapes=[
            pltpu.VMEM((CACHE, width), jnp.bfloat16),
            pltpu.VMEM((CACHE, width), jnp.bfloat16),
            pltpu.VMEM((heads * NEW, CACHE), jnp.float32),
            pltpu.VMEM((heads * NEW, width), jnp.bfloat16),
            pltpu.SemaphoreType.DMA((CACHE // KB,)),
            pltpu.SemaphoreType.DMA((CACHE // KB,)),
        ],
        compiler_params=pltpu.CompilerParams(vmem_limit_bytes=60 * 2**20),
        name="attention",
    )(length, qkv_t, bias[:, None], cosine, sine, keys_old, values_old)


MESH = pl.DeviceIdType.MESH
SIDE = 4
HALF = 3072
PART = 1536
EXT = PART + 128
VMEM_LIMIT = 62 * 2**20


def place():
    req, head = lax.axis_index("req"), lax.axis_index("head")
    return req // SIDE, req % SIDE, head // 2, head % 2


def meet(barrier, others):
    for count, target, alone in others:
        @pl.loop(0, count)
        def _(i):
            @pl.when(alone(i))
            def _():
                pl.semaphore_signal(barrier, inc=1, device_id=target(i), device_id_type=MESH)


def ring_units(y, z, x, core, own, slot, part, send_sem, recv_sem):
    def send(colour, dp, ds, half, along, step):
        to = [dp, ds]
        to[along] = (to[along] + step) % SIDE if isinstance(to[along], int) else lax.rem(
            to[along] + step + SIDE, SIDE)
        on_z = (colour == 0) == (along == 0)
        dev_y = y if on_z else lax.rem(y + step + SIDE, SIDE)
        dev_z = lax.rem(z + step + SIDE, SIDE) if on_z else z
        is_own = isinstance(dp, int) and isinstance(ds, int) and dp == 0 and ds == 0
        src = own(colour, half) if is_own else part(slot(colour, dp, ds, 0), colour, half)
        source = (colour, dp, ds)
        dst = part(slot(*source, 0), colour, half) if slot.absolute else part(
            slot(colour, to[0], to[1], 0), colour, half)
        return pltpu.make_async_remote_copy(
            src_ref=src, dst_ref=dst, send_sem=send_sem.at[colour],
            recv_sem=recv_sem.at[colour, half, to[0] * SIDE + to[1]],
            device_id=(dev_y * SIDE + dev_z, 2 * x + core), device_id_type=MESH,
        )

    def arrived(colour, dp, ds, half):
        ref = part(slot(colour, dp, ds, 0), colour, half)
        pltpu.make_async_copy(ref, ref, recv_sem.at[colour, half, dp * SIDE + ds]).wait()

    return send, arrived


FIRST = ((1, 0), (3, 1), (1, 1), (3, 0), (2, 0), (2, 1))


def ring_start(send):
    for along in (0, 1):
        for half in (0, 1):
            for colour in (0, 1):
                for step in (1, -1):
                    send(colour, 0, 0, half, along, step).start()


def ring_first(send, arrived):
    for dp, half in FIRST:
        for colour in (0, 1):
            arrived(colour, dp, 0, half)
            if (dp, half) in ((1, 0), (3, 1)):
                send(colour, dp, 0, half, 0, 1 if dp == 1 else -1).start()
            for step in (1, -1):
                send(colour, dp, 0, half, 1, step).start()


def ring_second(send, arrived, dp):
    for ds, half in FIRST:
        for colour in (0, 1):
            arrived(colour, dp, ds, half)
            if (ds, half) in ((1, 0), (3, 1)):
                send(colour, dp, ds, half, 1, 1 if ds == 1 else -1).start()


def gray(i):
    return i + (i // 2) * (1 - 2 * (i % 2))


class Relative:
    absolute = False

    def __call__(self, colour, dp, ds, _):
        return dp * SIDE + ds


class Absolute:
    absolute = True

    def __init__(self, y, z):
        self.y, self.z = y, z

    def __call__(self, colour, dp, ds, _):
        dy, dz = (ds, dp) if colour == 0 else (dp, ds)
        return lax.rem(self.y - dy + SIDE, SIDE) * SIDE + lax.rem(self.z - dz + SIDE, SIDE)


def front_kernel(
    xe_ref, wt_ref, gain_ref, ub_ref, qkv_ref, units_ref,
    xbuf, wbuf, nbuf, pbuf, rbuf, bbuf, qsend, qrecv,
    xsend_sem, xrecv_sem, own_sem, wsend_sem, wrecv_sem, wself_sem,
    bias_sem, pair_sem, qsend_sem, qrecv_sem,
):
    y, z, x, core = place()
    me = y * SIDE + z
    mate = 1 - core
    barrier = pltpu.get_barrier_semaphore()

    def plane(i):
        return (i // 2, 2 * x + i % 2)

    meet(barrier, [(32, plane, lambda i: i != 2 * me + core)])
    pl.semaphore_wait(barrier, 31)

    goal = y // 2
    kat = pl.ds(pl.multiple_of(((y % 2) * SIDE + z) * 384, 384), 384)

    def wcopy(r):
        return pltpu.make_async_remote_copy(
            src_ref=wt_ref.at[r], dst_ref=wbuf.at[:, core, :, kat],
            send_sem=wsend_sem, recv_sem=wrecv_sem,
            device_id=(r, 2 * x + goal), device_id_type=MESH,
        )

    @pl.loop(1, 16)
    def _(i):
        wcopy(lax.rem(y + i // SIDE, SIDE) * SIDE + lax.rem(z + i % SIDE, SIDE)).start()

    def mate_w():
        return pltpu.make_async_remote_copy(
            src_ref=wt_ref.at[me], dst_ref=wbuf.at[:, core, :, kat],
            send_sem=wself_sem, recv_sem=wrecv_sem,
            device_id=(me, 2 * x + mate), device_id_type=MESH,
        )

    @pl.when(goal != core)
    def _():
        mate_w().start()

    @pl.when(goal == core)
    def _():
        pltpu.make_async_copy(wt_ref.at[me], wbuf.at[:, core, :, kat], wrecv_sem).start()

    def part(s, colour, half):
        return xbuf.at[colour, s, pl.ds(64 * half, 64)]

    def own(colour, half):
        return xe_ref.at[colour, pl.ds(64 * half, 64)]

    send, arrived = ring_units(y, z, x, core, own, Relative(), part, xsend_sem, xrecv_sem)
    ring_start(send)
    own_copies = [
        pltpu.make_async_copy(xe_ref.at[colour], xbuf.at[colour, 0], own_sem.at[colour])
        for colour in (0, 1)
    ]
    for copy in own_copies:
        copy.start()
    bias_own = pltpu.make_async_copy(ub_ref, bbuf.at[core], bias_sem.at[0])
    bias_mate = pltpu.make_async_remote_copy(
        src_ref=ub_ref, dst_ref=bbuf.at[core], send_sem=bias_sem.at[1], recv_sem=bias_sem.at[2],
        device_id=(me, 2 * x + mate), device_id_type=MESH,
    )
    bias_own.start()
    bias_mate.start()
    pbuf[...] = jnp.zeros_like(pbuf)
    for copy in own_copies:
        copy.wait()
    ring_first(send, arrived)

    def compute(colour, dp):
        @pl.loop(0, SIDE)
        def _(ds):
            s = dp * SIDE + ds
            stat = xbuf[colour, s, :, PART:EXT].astype(jnp.float32)
            center = stat[:, 0:1] + stat[:, 1:2] + stat[:, 2:3]
            spread = stat[:, 3:4] + stat[:, 4:5] + stat[:, 5:6]
            rows = pl.ds(pl.multiple_of(ds * NEW, NEW), NEW)
            for k in range(PART // 512):
                at = slice(k * 512, (k + 1) * 512)
                value = (xbuf[colour, s, :, at].astype(jnp.float32) - center) * spread
                for kind in (0, 1):
                    nbuf[kind, rows, at] = (
                        value * gain_ref[colour, 2 * kind:2 * kind + 1, at]
                        + gain_ref[colour, 2 * kind + 1:2 * kind + 2, at]
                    ).astype(jnp.bfloat16)

        for kind in (0, 1):
            left = wbuf[kind, :, :, pl.ds(pl.multiple_of(colour * PART, PART), PART)]
            product = lax.dot_general(
                left.reshape(192, PART), nbuf[kind], NT, preferred_element_type=jnp.float32
            )
            for ds in range(SIDE):
                dy = colour * dp + (1 - colour) * ds
                dz = colour * ds + (1 - colour) * dp
                row = lax.rem(y - dy + SIDE, SIDE) * SIDE + lax.rem(z - dz + SIDE, SIDE)
                pbuf[row, 192 * kind:192 * (kind + 1), :] += product[:, ds * NEW:(ds + 1) * NEW]

    @pl.loop(0, SIDE)
    def _(i):
        dp = gray(i)
        ring_second(send, arrived, dp)

        @pl.when(i == 0)
        def _():
            pltpu.make_async_copy(wbuf, wbuf, wrecv_sem).wait()

        @pl.loop(0, 2)
        def _(colour):
            compute(colour, dp)

    pair = pltpu.make_async_remote_copy(
        src_ref=pbuf.at[pl.ds(8 * mate, 8)], dst_ref=rbuf,
        send_sem=pair_sem.at[0], recv_sem=pair_sem.at[1],
        device_id=(me, 2 * x + mate), device_id_type=MESH,
    )
    pair.start()
    bias_own.wait()
    bias_mate.wait()
    pair.wait_recv()
    mine = pl.ds(pl.multiple_of(me * 72, 8), 72)

    @pl.loop(0, 8)
    def _(q):
        row = 8 * core + q
        total = pbuf[row] + rbuf[q]
        for h in (0, 1):
            qsend[2 * q + h] = total[96 * h:96 * h + 72]
            remote = pltpu.make_async_remote_copy(
                src_ref=qsend.at[2 * q + h], dst_ref=qrecv.at[mine],
                send_sem=qsend_sem, recv_sem=qrecv_sem,
                device_id=(row, 2 * x + h), device_id_type=MESH,
            )
            away = jnp.logical_or(row != me, core != h)

            @pl.when(away)
            def _():
                remote.start()

            @pl.when(jnp.logical_not(away))
            def _():
                pltpu.make_async_copy(qsend.at[2 * q + h], qrecv.at[mine], qrecv_sem).start()
        at = pl.ds(pl.multiple_of(q * NEW, NEW), NEW)
        for h in (0, 1):
            u = total[192 + 96 * h:288 + 96 * h] + bbuf[h]
            inner = 0.7978845608028654 * (u + 0.044715 * (u * u * u))
            units_ref[h, :, at] = (0.5 * u * (1.0 + jnp.tanh(inner))).astype(jnp.bfloat16)

    pltpu.make_async_copy(qrecv, qrecv, qrecv_sem).wait()
    qkv_ref[...] = qrecv[...]
    pair.wait_send()

    @pl.when(goal == core)
    def _():
        some = qsend.at[pl.ds(0, 15)]
        pltpu.make_async_copy(some, some, qsend_sem).wait()

    @pl.when(goal != core)
    def _():
        pltpu.make_async_copy(qsend, qsend, qsend_sem).wait()
        mate_w().wait_send()

    some = wt_ref.at[pl.ds(0, 15)]
    pltpu.make_async_copy(some, some, wsend_sem).wait()
    for colour in (0, 1):
        some = xbuf.at[colour, pl.ds(1, 15)]
        pltpu.make_async_copy(some, some, xsend_sem.at[colour]).wait()


def pieces(value):
    high = lax.reduce_precision(value, 8, 7)
    rest = value - high
    middle = lax.reduce_precision(rest, 8, 7)
    return [high, middle, rest - middle]


def front(hidden, gains, qkv_weight, up_weight, up_bias):
    req, core = lax.axis_index("req"), lax.axis_index("head") % 2
    widened = hidden.astype(jnp.float32)
    center = jnp.mean(widened, axis=-1, keepdims=True)
    spread = lax.rsqrt(jnp.mean(jnp.square(widened - center), axis=-1, keepdims=True) + 1e-05)
    stat = jnp.concatenate(pieces(center) + pieces(spread), axis=1).astype(jnp.bfloat16)
    stat = jnp.pad(stat, ((0, 0), (0, 122)))
    mine = lax.dynamic_slice_in_dim(hidden, core * HALF, HALF, 1)
    xe = jnp.stack([
        jnp.concatenate([mine[:, :PART], stat], axis=1),
        jnp.concatenate([mine[:, PART:], stat], axis=1),
    ])
    depth = qkv_weight.shape[0]
    wq = jnp.pad(qkv_weight.T.reshape(16, 72, depth), ((0, 0), (0, 24), (0, 0)))
    wt = jnp.stack([wq, up_weight.T.reshape(16, 96, depth)], axis=1)
    gain = lax.dynamic_slice_in_dim(jnp.stack(gains), core * HALF, HALF, 1)
    gain = gain.reshape(4, 2, PART).transpose(1, 0, 2)
    bias = lax.dynamic_slice_in_dim(up_bias, req * 96, 96, 0)
    bias = jnp.broadcast_to(bias[:, None], (96, 128))
    vmem = pl.BlockSpec(memory_space=pltpu.VMEM)
    hbm = pl.BlockSpec(memory_space=pl.ANY)
    dma = pltpu.SemaphoreType.DMA
    return pl.pallas_call(
        front_kernel,
        out_shape=(
            jax.ShapeDtypeStruct((1152, NEW), jnp.float32),
            jax.ShapeDtypeStruct((2, 96, 1024), jnp.bfloat16),
        ),
        in_specs=[hbm, hbm, vmem, hbm],
        out_specs=(vmem, vmem),
        scratch_shapes=[
            pltpu.VMEM((2, 16, NEW, EXT), jnp.bfloat16),
            pltpu.VMEM((2, 2, 96, HALF), jnp.bfloat16),
            pltpu.VMEM((2, 512, PART), jnp.bfloat16),
            pltpu.VMEM((16, 384, NEW), jnp.float32),
            pltpu.VMEM((8, 384, NEW), jnp.float32),
            pltpu.VMEM((2, 96, NEW), jnp.float32),
            pltpu.VMEM((16, 72, NEW), jnp.float32),
            pltpu.VMEM((1152, NEW), jnp.float32),
            dma((2,)), dma((2, 2, 16)), dma((2,)), dma, dma, dma,
            dma((3,)), dma((2,)), dma, dma,
        ],
        compiler_params=pltpu.CompilerParams(
            collective_id=0, has_side_effects=True, vmem_limit_bytes=VMEM_LIMIT
        ),
        name="front",
    )(xe, wt, gain, bias)


def back_kernel(
    units_ref, att_ref, wd_ref, wo_ref, base_ref, out_ref,
    ubuf, abuf, dbuf, obuf_w, dturn, total, rsum, share, fbuf, fout,
    usend_sem, urecv_sem, own_sem, asend_sem, aself_sem, arecv_sem, w_sem,
    rsend_sem, rrecv_sem, fsend_sem, frecv_sem, gsend_sem, grecv_sem,
):
    y, z, x, core = place()
    me = y * SIDE + z
    mate = 1 - core
    goal = y // 2
    barrier = pltpu.get_barrier_semaphore()

    def plane(i):
        return (i // 2, 2 * x + i % 2)

    def line(i):
        return (me, i)

    meet(barrier, [
        (32, plane, lambda i: i != 2 * me + core),
        (8, line, lambda i: i // 2 != x),
    ])
    pl.semaphore_wait(barrier, 37)

    spot = (y % 2) * SIDE + z
    alane = pl.ds(pl.multiple_of(core * 384, 384), 384)

    def acopy(r, sem):
        return pltpu.make_async_remote_copy(
            src_ref=att_ref, dst_ref=abuf.at[spot, :, alane],
            send_sem=sem, recv_sem=arecv_sem,
            device_id=(r, 2 * x + goal), device_id_type=MESH,
        )

    @pl.loop(1, 16)
    def _(i):
        acopy(lax.rem(y + i // SIDE, SIDE) * SIDE + lax.rem(z + i % SIDE, SIDE), asend_sem).start()

    def mate_a():
        return pltpu.make_async_remote_copy(
            src_ref=att_ref, dst_ref=abuf.at[spot, :, alane],
            send_sem=aself_sem, recv_sem=arecv_sem,
            device_id=(me, 2 * x + mate), device_id_type=MESH,
        )

    @pl.when(goal != core)
    def _():
        mate_a().start()

    @pl.when(goal == core)
    def _():
        pltpu.make_async_copy(att_ref, abuf.at[spot, :, alane], arecv_sem).start()

    def lanes(colour, half):
        return pl.ds((2 * colour + half) * 256, 256)

    def part(s, colour, half):
        return ubuf.at[:, s, :, lanes(colour, half)]

    def own(colour, half):
        return units_ref.at[:, :, lanes(colour, half)]

    send, arrived = ring_units(y, z, x, core, own, Absolute(y, z), part, usend_sem, urecv_sem)
    ring_start(send)
    own_copy = pltpu.make_async_copy(units_ref, ubuf.at[:, me], own_sem)
    own_copy.start()

    copies = []
    for n, (src, dst) in enumerate(((wd_ref, dbuf), (wo_ref, obuf_w))):
        copies.append(pltpu.make_async_copy(src, dst.at[core], w_sem.at[3 * n]))
        copies.append(pltpu.make_async_remote_copy(
            src_ref=src, dst_ref=dst.at[core], send_sem=w_sem.at[3 * n + 1],
            recv_sem=w_sem.at[3 * n + 2], device_id=(me, 2 * x + mate), device_id_type=MESH,
        ))
    for copy in copies:
        copy.start()
    ring_first(send, arrived)
    for copy in copies:
        copy.wait()

    @pl.loop(0, 24)
    def _(k):
        h, at = k // 12, pl.ds(pl.multiple_of((k % 12) * 128, 128), 128)
        dturn[h, :, at] = dbuf[h, at, :].T

    @pl.loop(0, SIDE)
    def _(i):
        ring_second(send, arrived, gray(i))

    own_copy.wait()
    pltpu.make_async_copy(abuf, abuf, arecv_sem).wait()

    @pl.loop(0, 8)
    def _(q):
        at = pl.ds(pl.multiple_of(q * NEW, NEW), NEW)
        turned = jnp.zeros((384, NEW), jnp.float32)
        for h in (0, 1):
            turned += jnp.dot(
                dturn[h], ubuf[h, :, :, at].reshape(PART, NEW), preferred_element_type=jnp.float32
            )
        attended = jnp.dot(
            abuf[q], obuf_w[...].reshape(768, 384), preferred_element_type=jnp.float32
        )
        total[q] = turned.T + attended

    def rcopy(step):
        to = lax.rem(x + step, SIDE)
        return pltpu.make_async_remote_copy(
            src_ref=total.at[:, pl.ds(pl.multiple_of(32 * to, 32), 32)], dst_ref=rsum.at[step - 1],
            send_sem=rsend_sem.at[step - 1], recv_sem=rrecv_sem.at[step - 1],
            device_id=(me, 2 * to + core), device_id_type=MESH,
        )

    for step in (2, 1, 3):
        rcopy(step).start()
    for step in (1, 3, 2):
        rcopy(step).wait_recv()
    share[...] = (
        total[:, pl.ds(pl.multiple_of(32 * x, 32), 32), :] + rsum[0] + rsum[1] + rsum[2]
    )

    @pl.loop(0, 8)
    def _(q):
        row = 8 * core + q

        @pl.when(row != me)
        def _():
            pltpu.make_async_remote_copy(
                src_ref=share.at[q], dst_ref=fbuf.at[spot],
                send_sem=fsend_sem, recv_sem=frecv_sem,
                device_id=(row, 2 * x + goal), device_id_type=MESH,
            ).start()

        @pl.when(row == me)
        def _():
            pltpu.make_async_copy(share.at[q], fbuf.at[spot], frecv_sem).start()

    pltpu.make_async_copy(fbuf, fbuf, frecv_sem).wait()
    rows = pl.ds(pl.multiple_of(32 * x, 32), 32)
    for j in range(8):
        at = pl.ds(pl.multiple_of(core * HALF + 384 * j, 384), 384)
        fout[rows, at] = (base_ref[:, 384 * j:384 * (j + 1)] + fbuf[j]).astype(jnp.bfloat16)

    def piece(owner, c):
        return fout.at[
            pl.ds(pl.multiple_of(32 * owner, 32), 32), pl.ds(pl.multiple_of(c * HALF, HALF), HALF)
        ]

    def gcopy(step):
        to = lax.rem(x + step, SIDE)
        return pltpu.make_async_remote_copy(
            src_ref=piece(x, core), dst_ref=piece(x, core), send_sem=gsend_sem.at[0, step],
            recv_sem=grecv_sem.at[0, step], device_id=(me, 2 * to + core), device_id_type=MESH,
        )

    def pass_on(step):
        owner = lax.rem(x - step + SIDE, SIDE)
        return pltpu.make_async_remote_copy(
            src_ref=piece(owner, core), dst_ref=piece(owner, core), send_sem=gsend_sem.at[1, step],
            recv_sem=grecv_sem.at[1, step], device_id=(me, 2 * x + mate), device_id_type=MESH,
        )

    def landed(kind, step):
        owner = lax.rem(x - step + SIDE, SIDE)
        ref = piece(owner, core if kind == 0 else mate)
        pltpu.make_async_copy(ref, ref, grecv_sem.at[kind, step]).wait()

    for step in (2, 1, 3):
        gcopy(step).start()
    pass_on(0).start()
    for step in (1, 3, 2):
        landed(0, step)
        pass_on(step).start()
    for step in (0, 1, 3, 2):
        landed(1, step)
    out_ref[...] = fout[...]

    for step in (1, 2, 3):
        gcopy(step).wait_send()
        rcopy(step).wait_send()
    for step in range(4):
        pass_on(step).wait_send()

    @pl.when(goal == core)
    def _():
        some = share.at[pl.ds(0, 7)]
        pltpu.make_async_copy(some, some, fsend_sem).wait()

    @pl.when(goal != core)
    def _():
        pltpu.make_async_copy(share, share, fsend_sem).wait()
        mate_a().wait_send()

    for half in (0, 1):
        some = abuf.at[pl.ds(0, 7), :, pl.ds(384 * half, 384)]
        if half == 0:
            some = abuf.at[:, :, pl.ds(0, 384)]
        else:
            some = abuf.at[pl.ds(0, 7), :, pl.ds(384, 384)]
        pltpu.make_async_copy(some, some, asend_sem).wait()
    for colour in (0, 1):
        some = ubuf.at[:, pl.ds(0, 15), :, pl.ds(512 * colour, 512)]
        pltpu.make_async_copy(some, some, usend_sem.at[colour]).wait()


def back(units, attended, hidden, out_weight, down_weight, bias_total):
    head = lax.axis_index("head")
    x, core = head // 2, head % 2
    base = lax.dynamic_slice(hidden, (32 * x, core * HALF), (32, HALF)).astype(jnp.float32)
    base = base + lax.dynamic_slice_in_dim(bias_total, core * HALF, HALF, 0)
    vmem = pl.BlockSpec(memory_space=pltpu.VMEM)
    hbm = pl.BlockSpec(memory_space=pl.ANY)
    dma = pltpu.SemaphoreType.DMA
    return pl.pallas_call(
        back_kernel,
        out_shape=jax.ShapeDtypeStruct((NEW, 2 * HALF), jnp.bfloat16),
        in_specs=[hbm, hbm, hbm, hbm, vmem],
        out_specs=vmem,
        scratch_shapes=[
            pltpu.VMEM((2, 16, 96, 1024), jnp.bfloat16),
            pltpu.VMEM((8, NEW, 768), jnp.bfloat16),
            pltpu.VMEM((2, PART, 384), jnp.bfloat16),
            pltpu.VMEM((2, 384, 384), jnp.bfloat16),
            pltpu.VMEM((2, 384, PART), jnp.bfloat16),
            pltpu.VMEM((8, NEW, 384), jnp.float32),
            pltpu.VMEM((3, 8, 32, 384), jnp.float32),
            pltpu.VMEM((8, 32, 384), jnp.float32),
            pltpu.VMEM((8, 32, 384), jnp.float32),
            pltpu.VMEM((NEW, 2 * HALF), jnp.bfloat16),
            dma((2,)), dma((2, 2, 16)), dma, dma, dma, dma, dma((6,)),
            dma((3,)), dma((3,)), dma, dma, dma((2, 4)), dma((2, 4)),
        ],
        compiler_params=pltpu.CompilerParams(
            collective_id=1, has_side_effects=True, vmem_limit_bytes=VMEM_LIMIT
        ),
        name="back",
    )(units, attended, down_weight, out_weight, base)


def body(
    hidden,
    attn_norm_gain,
    attn_norm_bias,
    mlp_norm_gain,
    mlp_norm_bias,
    qkv_weight,
    qkv_bias,
    out_weight,
    out_bias,
    up_weight,
    up_bias,
    down_weight,
    down_bias,
    cache_keys,
    cache_values,
    cached_len,
):
    gains = (attn_norm_gain, attn_norm_bias, mlp_norm_gain, mlp_norm_bias)
    qkv, units = front(hidden, gains, qkv_weight, up_weight, up_bias)
    attended, key_rows, value_rows = attention(
        qkv, qkv_bias, cached_len, cache_keys[0], cache_values[0]
    )
    result = back(units, attended, hidden, out_weight, down_weight, out_bias + down_bias)
    return (result, key_rows[None], value_rows[None])


def solution(mesh):
    return jax.shard_map(
        body,
        mesh=mesh,
        in_specs=(
            P("req", None),
            P(),
            P(),
            P(),
            P(),
            P("req", "head"),
            P("head"),
            P("head", "req"),
            P(),
            P("req", "head"),
            P("head"),
            P("head", "req"),
            P(),
            P("req", None, "head"),
            P("req", None, "head"),
            P("req"),
        ),
        out_specs=(P("req", None), P("req", None, "head"), P("req", None, "head")),
        check_vma=False,
    )
```

```python
import functools
import math

import jax
import jax.numpy as jnp
from jax import lax
from jax.experimental import pallas as pl
from jax.experimental.pallas import tpu as pltpu
from jax.sharding import PartitionSpec as P

DH = 96
ROT = 24
NEW = 128
CACHE = 4096
KB = 512
NT = (((1,), (1,)), ((), ()))


def rotation_tables(length):
    position = length.astype(jnp.float32) + jnp.arange(NEW, dtype=jnp.float32)
    halfway = ROT // 2
    exponent = jnp.arange(halfway, dtype=jnp.float32) * (2.0 / ROT)
    frequency = jnp.power(10000.0, -exponent)
    angle = position[None, :] * frequency[:, None]
    cosine, sine = jnp.cos(angle), jnp.sin(angle)
    return jnp.concatenate([cosine, cosine], 0), jnp.concatenate([-sine, sine], 0)


def attention_kernel(
    heads, len_ref, qkv_ref, bias_ref, cos_ref, sin_ref, k_hbm, v_hbm,
    att_ref, nk_ref, nv_ref, kbuf, vbuf, sbuf, qexp, ksem, vsem,
):
    scale = 1.0 / math.sqrt(DH)
    length = len_ref[0]
    width = heads * DH
    blocks = CACHE // KB
    used = (length + KB - 1) // KB

    def fetch(i, hbm, buf, sem):
        rows = pl.ds(pl.multiple_of(i * KB, KB), KB)
        return pltpu.make_async_copy(hbm.at[rows], buf.at[rows], sem.at[i])

    for hbm, buf, sem in ((k_hbm, kbuf, ksem), (v_hbm, vbuf, vsem)):
        @pl.loop(0, used)
        def _(i):
            fetch(i, hbm, buf, sem).start()

    cosine, sine = cos_ref[...], sin_ref[...]

    def turned(rows):
        low = rows[:ROT]
        swapped = jnp.concatenate([low[ROT // 2:], low[: ROT // 2]], axis=0)
        return jnp.concatenate([low * cosine + swapped * sine, rows[ROT:]], axis=0)

    def block(j, part):
        at = pl.ds((3 * j + part) * DH, DH)
        return qkv_ref[at, :] + bias_ref[at, :]

    queries = jnp.concatenate([turned(block(j, 0)) for j in range(heads)], 0).T.astype(jnp.bfloat16)
    keys = jnp.concatenate([turned(block(j, 1)) for j in range(heads)], 0).T.astype(jnp.bfloat16)
    values = jnp.concatenate([block(j, 2) for j in range(heads)], 0).T.astype(jnp.bfloat16)
    nk_ref[...] = keys
    nv_ref[...] = values
    lane_head = lax.broadcasted_iota(jnp.int32, (NEW, width), 1) // DH
    for j in range(heads):
        qexp[pl.ds(j * NEW, NEW), :] = jnp.where(lane_head == j, queries, jnp.zeros_like(queries))
    rows = heads * NEW
    fresh = lax.dot_general(qexp[...], keys, NT, preferred_element_type=jnp.float32) * scale
    row_at = lax.broadcasted_iota(jnp.int32, (rows, NEW), 0) % NEW
    col_at = lax.broadcasted_iota(jnp.int32, (rows, NEW), 1)
    fresh = jnp.where(col_at <= row_at, fresh, -1e30)

    def score(i, top):
        fetch(i, k_hbm, kbuf, ksem).wait()
        at = pl.ds(pl.multiple_of(i * KB, KB), KB)
        part = lax.dot_general(qexp[...], kbuf[at, :], NT, preferred_element_type=jnp.float32) * scale
        col = lax.broadcasted_iota(jnp.int32, (rows, KB), 1) + i * KB
        part = jnp.where(col < length, part, -1e30)
        sbuf[:, at] = part
        for t in range(KB // NEW):
            top = jnp.maximum(top, part[:, t * NEW:(t + 1) * NEW])
        return top

    top = lax.fori_loop(0, used, score, fresh)
    highest = jnp.max(top, axis=1, keepdims=True)
    fresh_weights = jnp.exp(fresh - highest)
    mixed = jnp.dot(fresh_weights.astype(jnp.bfloat16), values, preferred_element_type=jnp.float32)

    def weigh(i, carry):
        mixed, total = carry
        fetch(i, v_hbm, vbuf, vsem).wait()
        at = pl.ds(pl.multiple_of(i * KB, KB), KB)
        weights = jnp.exp(sbuf[:, at] - highest)
        for t in range(KB // NEW):
            total = total + weights[:, t * NEW:(t + 1) * NEW]
        mixed = mixed + jnp.dot(weights.astype(jnp.bfloat16), vbuf[at, :], preferred_element_type=jnp.float32)
        return mixed, total

    mixed, total = lax.fori_loop(0, used, weigh, (mixed, fresh_weights))
    total = jnp.sum(total, axis=1, keepdims=True)
    out = jnp.zeros((NEW, width), jnp.float32)
    for j in range(heads):
        at = slice(j * NEW, (j + 1) * NEW)
        out = jnp.where(lane_head == j, mixed[at] / total[at], out)
    att_ref[...] = out.astype(jnp.bfloat16)


def attention(qkv_t, bias, length, keys_old, values_old):
    heads = qkv_t.shape[0] // (3 * DH)
    width = heads * DH
    cosine, sine = rotation_tables(length[0])
    vmem = pl.BlockSpec(memory_space=pltpu.VMEM)
    hbm = pl.BlockSpec(memory_space=pl.ANY)
    out = jax.ShapeDtypeStruct((NEW, width), jnp.bfloat16)
    return pl.pallas_call(
        functools.partial(attention_kernel, heads),
        out_shape=(out, out, out),
        in_specs=[pl.BlockSpec(memory_space=pltpu.SMEM), vmem, vmem, vmem, vmem, hbm, hbm],
        out_specs=(vmem, vmem, vmem),
        scratch_shapes=[
            pltpu.VMEM((CACHE, width), jnp.bfloat16),
            pltpu.VMEM((CACHE, width), jnp.bfloat16),
            pltpu.VMEM((heads * NEW, CACHE), jnp.float32),
            pltpu.VMEM((heads * NEW, width), jnp.bfloat16),
            pltpu.SemaphoreType.DMA((CACHE // KB,)),
            pltpu.SemaphoreType.DMA((CACHE // KB,)),
        ],
        compiler_params=pltpu.CompilerParams(vmem_limit_bytes=60 * 2**20),
        name="attention",
    )(length, qkv_t, bias[:, None], cosine, sine, keys_old, values_old)


MESH = pl.DeviceIdType.MESH
SIDE = 4
HALF = 3072
PART = 1536
EXT = PART + 128
VMEM_LIMIT = 62 * 2**20


def place():
    req, head = lax.axis_index("req"), lax.axis_index("head")
    return req // SIDE, req % SIDE, head // 2, head % 2


def meet(barrier, others):
    for count, target, alone in others:
        @pl.loop(0, count)
        def _(i):
            @pl.when(alone(i))
            def _():
                pl.semaphore_signal(barrier, inc=1, device_id=target(i), device_id_type=MESH)


def ring_units(y, z, x, core, own, slot, part, send_sem, recv_sem):
    def send(colour, dp, ds, half, along, step):
        to = [dp, ds]
        to[along] = (to[along] + step) % SIDE if isinstance(to[along], int) else lax.rem(
            to[along] + step + SIDE, SIDE)
        on_z = (colour == 0) == (along == 0)
        dev_y = y if on_z else lax.rem(y + step + SIDE, SIDE)
        dev_z = lax.rem(z + step + SIDE, SIDE) if on_z else z
        is_own = isinstance(dp, int) and isinstance(ds, int) and dp == 0 and ds == 0
        src = own(colour, half) if is_own else part(slot(colour, dp, ds, 0), colour, half)
        source = (colour, dp, ds)
        dst = part(slot(*source, 0), colour, half) if slot.absolute else part(
            slot(colour, to[0], to[1], 0), colour, half)
        return pltpu.make_async_remote_copy(
            src_ref=src, dst_ref=dst, send_sem=send_sem.at[colour],
            recv_sem=recv_sem.at[colour, half, to[0] * SIDE + to[1]],
            device_id=(dev_y * SIDE + dev_z, 2 * x + core), device_id_type=MESH,
        )

    def arrived(colour, dp, ds, half):
        ref = part(slot(colour, dp, ds, 0), colour, half)
        pltpu.make_async_copy(ref, ref, recv_sem.at[colour, half, dp * SIDE + ds]).wait()

    return send, arrived


FIRST = ((1, 0), (3, 1), (1, 1), (3, 0), (2, 0), (2, 1))


def ring_start(send):
    for along in (0, 1):
        for half in (0, 1):
            for colour in (0, 1):
                for step in (1, -1):
                    send(colour, 0, 0, half, along, step).start()


def ring_spread(send, dp):
    for half in (0, 1):
        for colour in (0, 1):
            for step in (1, -1):
                send(colour, dp, 0, half, 1, step).start()


def ring_first(send, arrived):
    for dp, half in FIRST:
        if (dp, half) == (2, 0):
            ring_spread(send, 1)
        for colour in (0, 1):
            arrived(colour, dp, 0, half)
            if (dp, half) in ((1, 0), (3, 1)):
                send(colour, dp, 0, half, 0, 1 if dp == 1 else -1).start()


def ring_second(send, arrived, i):
    dp = gray(i)
    for ds, half in FIRST:
        if (ds, half) == (2, 0):
            @pl.when(i < 2)
            def _():
                ring_spread(send, gray(i + 2))
        for colour in (0, 1):
            arrived(colour, dp, ds, half)
            if (ds, half) in ((1, 0), (3, 1)):
                send(colour, dp, ds, half, 1, 1 if ds == 1 else -1).start()


def gray(i):
    return i + (i // 2) * (1 - 2 * (i % 2))


class Relative:
    absolute = False

    def __call__(self, colour, dp, ds, _):
        return dp * SIDE + ds


class Absolute:
    absolute = True

    def __init__(self, y, z):
        self.y, self.z = y, z

    def __call__(self, colour, dp, ds, _):
        dy, dz = (ds, dp) if colour == 0 else (dp, ds)
        return lax.rem(self.y - dy + SIDE, SIDE) * SIDE + lax.rem(self.z - dz + SIDE, SIDE)


def front_kernel(
    xe_ref, wt_ref, gain_ref, ub_ref, qkv_ref, units_ref,
    xbuf, wbuf, nbuf, pbuf, rbuf, bbuf, qsend, qrecv,
    xsend_sem, xrecv_sem, own_sem, wsend_sem, wrecv_sem, wself_sem,
    bias_sem, pair_sem, qsend_sem, qrecv_sem,
):
    y, z, x, core = place()
    me = y * SIDE + z
    mate = 1 - core
    barrier = pltpu.get_barrier_semaphore()

    def plane(i):
        return (i // 2, 2 * x + i % 2)

    meet(barrier, [(32, plane, lambda i: i != 2 * me + core)])
    pl.semaphore_wait(barrier, 31)

    goal = y // 2
    kat = pl.ds(pl.multiple_of(((y % 2) * SIDE + z) * 384, 384), 384)

    def wcopy(r):
        return pltpu.make_async_remote_copy(
            src_ref=wt_ref.at[r], dst_ref=wbuf.at[:, core, :, kat],
            send_sem=wsend_sem, recv_sem=wrecv_sem,
            device_id=(r, 2 * x + goal), device_id_type=MESH,
        )

    @pl.loop(1, 16)
    def _(i):
        wcopy(lax.rem(y + i // SIDE, SIDE) * SIDE + lax.rem(z + i % SIDE, SIDE)).start()

    def mate_w():
        return pltpu.make_async_remote_copy(
            src_ref=wt_ref.at[me], dst_ref=wbuf.at[:, core, :, kat],
            send_sem=wself_sem, recv_sem=wrecv_sem,
            device_id=(me, 2 * x + mate), device_id_type=MESH,
        )

    @pl.when(goal != core)
    def _():
        mate_w().start()

    @pl.when(goal == core)
    def _():
        pltpu.make_async_copy(wt_ref.at[me], wbuf.at[:, core, :, kat], wrecv_sem).start()

    def part(s, colour, half):
        return xbuf.at[colour, s, pl.ds(64 * half, 64)]

    def own(colour, half):
        return xe_ref.at[colour, pl.ds(64 * half, 64)]

    send, arrived = ring_units(y, z, x, core, own, Relative(), part, xsend_sem, xrecv_sem)
    ring_start(send)
    own_copies = [
        pltpu.make_async_copy(xe_ref.at[colour], xbuf.at[colour, 0], own_sem.at[colour])
        for colour in (0, 1)
    ]
    for copy in own_copies:
        copy.start()
    bias_own = pltpu.make_async_copy(ub_ref, bbuf.at[core], bias_sem.at[0])
    bias_mate = pltpu.make_async_remote_copy(
        src_ref=ub_ref, dst_ref=bbuf.at[core], send_sem=bias_sem.at[1], recv_sem=bias_sem.at[2],
        device_id=(me, 2 * x + mate), device_id_type=MESH,
    )
    bias_own.start()
    bias_mate.start()
    pbuf[...] = jnp.zeros_like(pbuf)
    for copy in own_copies:
        copy.wait()
    ring_first(send, arrived)

    def compute(colour, dp):
        @pl.loop(0, SIDE)
        def _(ds):
            s = dp * SIDE + ds
            stat = xbuf[colour, s, :, PART:EXT].astype(jnp.float32)
            center = stat[:, 0:1] + stat[:, 1:2] + stat[:, 2:3]
            spread = stat[:, 3:4] + stat[:, 4:5] + stat[:, 5:6]
            rows = pl.ds(pl.multiple_of(ds * NEW, NEW), NEW)
            for k in range(PART // 512):
                at = slice(k * 512, (k + 1) * 512)
                value = (xbuf[colour, s, :, at].astype(jnp.float32) - center) * spread
                for kind in (0, 1):
                    nbuf[kind, rows, at] = (
                        value * gain_ref[colour, 2 * kind:2 * kind + 1, at]
                        + gain_ref[colour, 2 * kind + 1:2 * kind + 2, at]
                    ).astype(jnp.bfloat16)

        for kind in (0, 1):
            left = wbuf[kind, :, :, pl.ds(pl.multiple_of(colour * PART, PART), PART)]
            product = lax.dot_general(
                left.reshape(192, PART), nbuf[kind], NT, preferred_element_type=jnp.float32
            )
            for ds in range(SIDE):
                dy = colour * dp + (1 - colour) * ds
                dz = colour * ds + (1 - colour) * dp
                row = lax.rem(y - dy + SIDE, SIDE) * SIDE + lax.rem(z - dz + SIDE, SIDE)
                pbuf[row, 192 * kind:192 * (kind + 1), :] += product[:, ds * NEW:(ds + 1) * NEW]

    @pl.loop(0, SIDE)
    def _(i):
        dp = gray(i)
        ring_second(send, arrived, i)

        @pl.when(i == 0)
        def _():
            pltpu.make_async_copy(wbuf, wbuf, wrecv_sem).wait()

        @pl.loop(0, 2)
        def _(colour):
            compute(colour, dp)

    pair = pltpu.make_async_remote_copy(
        src_ref=pbuf.at[pl.ds(8 * mate, 8)], dst_ref=rbuf,
        send_sem=pair_sem.at[0], recv_sem=pair_sem.at[1],
        device_id=(me, 2 * x + mate), device_id_type=MESH,
    )
    pair.start()
    bias_own.wait()
    bias_mate.wait()
    pair.wait_recv()
    mine = pl.ds(pl.multiple_of(me * 72, 8), 72)

    @pl.loop(0, 8)
    def _(q):
        row = 8 * core + q
        total = pbuf[row] + rbuf[q]
        for h in (0, 1):
            qsend[2 * q + h] = total[96 * h:96 * h + 72]
            remote = pltpu.make_async_remote_copy(
                src_ref=qsend.at[2 * q + h], dst_ref=qrecv.at[mine],
                send_sem=qsend_sem, recv_sem=qrecv_sem,
                device_id=(row, 2 * x + h), device_id_type=MESH,
            )
            away = jnp.logical_or(row != me, core != h)

            @pl.when(away)
            def _():
                remote.start()

            @pl.when(jnp.logical_not(away))
            def _():
                pltpu.make_async_copy(qsend.at[2 * q + h], qrecv.at[mine], qrecv_sem).start()
        at = pl.ds(pl.multiple_of(q * NEW, NEW), NEW)
        for h in (0, 1):
            u = total[192 + 96 * h:288 + 96 * h] + bbuf[h]
            inner = 0.7978845608028654 * (u + 0.044715 * (u * u * u))
            units_ref[h, :, at] = (0.5 * u * (1.0 + jnp.tanh(inner))).astype(jnp.bfloat16)

    pltpu.make_async_copy(qrecv, qrecv, qrecv_sem).wait()
    qkv_ref[...] = qrecv[...]
    pair.wait_send()

    @pl.when(goal == core)
    def _():
        some = qsend.at[pl.ds(0, 15)]
        pltpu.make_async_copy(some, some, qsend_sem).wait()

    @pl.when(goal != core)
    def _():
        pltpu.make_async_copy(qsend, qsend, qsend_sem).wait()
        mate_w().wait_send()

    some = wt_ref.at[pl.ds(0, 15)]
    pltpu.make_async_copy(some, some, wsend_sem).wait()
    for colour in (0, 1):
        some = xbuf.at[colour, pl.ds(1, 15)]
        pltpu.make_async_copy(some, some, xsend_sem.at[colour]).wait()


def pieces(value):
    high = lax.reduce_precision(value, 8, 7)
    rest = value - high
    middle = lax.reduce_precision(rest, 8, 7)
    return [high, middle, rest - middle]


def front(hidden, gains, qkv_weight, up_weight, up_bias):
    req, core = lax.axis_index("req"), lax.axis_index("head") % 2
    widened = hidden.astype(jnp.float32)
    center = jnp.mean(widened, axis=-1, keepdims=True)
    spread = lax.rsqrt(jnp.mean(jnp.square(widened - center), axis=-1, keepdims=True) + 1e-05)
    stat = jnp.concatenate(pieces(center) + pieces(spread), axis=1).astype(jnp.bfloat16)
    stat = jnp.pad(stat, ((0, 0), (0, 122)))
    mine = lax.dynamic_slice_in_dim(hidden, core * HALF, HALF, 1)
    xe = jnp.stack([
        jnp.concatenate([mine[:, :PART], stat], axis=1),
        jnp.concatenate([mine[:, PART:], stat], axis=1),
    ])
    depth = qkv_weight.shape[0]
    wq = jnp.pad(qkv_weight.T.reshape(16, 72, depth), ((0, 0), (0, 24), (0, 0)))
    wt = jnp.stack([wq, up_weight.T.reshape(16, 96, depth)], axis=1)
    gain = lax.dynamic_slice_in_dim(jnp.stack(gains), core * HALF, HALF, 1)
    gain = gain.reshape(4, 2, PART).transpose(1, 0, 2)
    bias = lax.dynamic_slice_in_dim(up_bias, req * 96, 96, 0)
    bias = jnp.broadcast_to(bias[:, None], (96, 128))
    vmem = pl.BlockSpec(memory_space=pltpu.VMEM)
    hbm = pl.BlockSpec(memory_space=pl.ANY)
    dma = pltpu.SemaphoreType.DMA
    return pl.pallas_call(
        front_kernel,
        out_shape=(
            jax.ShapeDtypeStruct((1152, NEW), jnp.float32),
            jax.ShapeDtypeStruct((2, 96, 1024), jnp.bfloat16),
        ),
        in_specs=[hbm, hbm, vmem, hbm],
        out_specs=(vmem, vmem),
        scratch_shapes=[
            pltpu.VMEM((2, 16, NEW, EXT), jnp.bfloat16),
            pltpu.VMEM((2, 2, 96, HALF), jnp.bfloat16),
            pltpu.VMEM((2, 512, PART), jnp.bfloat16),
            pltpu.VMEM((16, 384, NEW), jnp.float32),
            pltpu.VMEM((8, 384, NEW), jnp.float32),
            pltpu.VMEM((2, 96, NEW), jnp.float32),
            pltpu.VMEM((16, 72, NEW), jnp.float32),
            pltpu.VMEM((1152, NEW), jnp.float32),
            dma((2,)), dma((2, 2, 16)), dma((2,)), dma, dma, dma,
            dma((3,)), dma((2,)), dma, dma,
        ],
        compiler_params=pltpu.CompilerParams(
            collective_id=0, has_side_effects=True, vmem_limit_bytes=VMEM_LIMIT
        ),
        name="front",
    )(xe, wt, gain, bias)


def back_kernel(
    units_ref, att_ref, wd_ref, wo_ref, rest_ref, bias_ref, out_ref,
    ubuf, aring, amate, dbuf, obuf, dturn, total, tsend, rsum, share, rest, fout,
    usend_sem, urecv_sem, own_sem, asend_sem, arecv_sem, amate_sem, w_sem,
    hsend_sem, hrecv_sem, rsend_sem, rrecv_sem, fsend_sem, frecv_sem, gsend_sem, grecv_sem,
):
    y, z, x, core = place()
    me = y * SIDE + z
    mate = 1 - core
    goal = y // 2
    barrier = pltpu.get_barrier_semaphore()

    def plane(i):
        return (i // 2, 2 * x + i % 2)

    def line(i):
        return (me, i)

    meet(barrier, [
        (32, plane, lambda i: i != 2 * me + core),
        (8, line, lambda i: i // 2 != x),
    ])
    pl.semaphore_wait(barrier, 37)

    def apart(s, colour, half):
        return aring.at[s, pl.ds(32 * (2 * colour + half), 32)]

    def aown(colour, half):
        return att_ref.at[pl.ds(32 * (2 * colour + half), 32)]

    asend, aarrived = ring_units(y, z, x, core, aown, Absolute(y, z), apart, asend_sem, arecv_sem)
    ring_start(asend)

    def lanes(colour, half):
        return pl.ds((2 * colour + half) * 256, 256)

    def part(s, colour, half):
        return ubuf.at[:, s, :, lanes(colour, half)]

    def own(colour, half):
        return units_ref.at[:, :, lanes(colour, half)]

    send, arrived = ring_units(y, z, x, core, own, Absolute(y, z), part, usend_sem, urecv_sem)
    ring_start(send)
    copies = [
        pltpu.make_async_copy(units_ref, ubuf.at[:, me], own_sem.at[0]),
        pltpu.make_async_copy(att_ref, aring.at[me], own_sem.at[1]),
    ]
    for n, (src, dst) in enumerate(((wd_ref, dbuf), (wo_ref, obuf))):
        copies.append(pltpu.make_async_copy(src, dst.at[core], w_sem.at[3 * n]))
        copies.append(pltpu.make_async_remote_copy(
            src_ref=src, dst_ref=dst.at[core], send_sem=w_sem.at[3 * n + 1],
            recv_sem=w_sem.at[3 * n + 2], device_id=(me, 2 * x + mate), device_id_type=MESH,
        ))
    for copy in copies:
        copy.start()
    slot = me % 8

    @pl.when(goal == core)
    def _():
        @pl.loop(1, 16)
        def _(i):
            row = lax.rem(y + i // SIDE, SIDE) * SIDE + lax.rem(z + i % SIDE, SIDE)
            pltpu.make_async_remote_copy(
                src_ref=rest_ref.at[row], dst_ref=rest.at[slot],
                send_sem=hsend_sem, recv_sem=hrecv_sem,
                device_id=(row, 2 * x + core), device_id_type=MESH,
            ).start()
        pltpu.make_async_copy(rest_ref.at[me], rest.at[slot], hrecv_sem).start()

    ring_first(asend, aarrived)
    ring_first(send, arrived)

    @pl.loop(0, SIDE)
    def _(i):
        ring_second(asend, aarrived, i)

    for copy in copies:
        copy.wait()
    pair = pltpu.make_async_remote_copy(
        src_ref=aring.at[pl.ds(8 * mate, 8)], dst_ref=amate,
        send_sem=amate_sem.at[0], recv_sem=amate_sem.at[1],
        device_id=(me, 2 * x + mate), device_id_type=MESH,
    )
    pair.start()

    @pl.loop(0, SIDE)
    def _(i):
        @pl.loop(0, 6)
        def _(k):
            n = 6 * i + k
            h, at = n // 12, pl.ds(pl.multiple_of((n % 12) * 128, 128), 128)
            dturn[h, :, at] = dbuf[h, at, :].T

        ring_second(send, arrived, i)

    pair.wait_recv()

    def rcopy(q, step):
        to = lax.rem(x + step, SIDE)
        return pltpu.make_async_remote_copy(
            src_ref=tsend.at[q, pl.ds(pl.multiple_of(32 * to, 32), 32)],
            dst_ref=rsum.at[step - 1, q],
            send_sem=rsend_sem.at[step - 1], recv_sem=rrecv_sem.at[step - 1],
            device_id=(me, 2 * to + core), device_id_type=MESH,
        )

    @pl.loop(0, 4)
    def _(p):
        at = pl.ds(pl.multiple_of(2 * p * NEW, 2 * NEW), 2 * NEW)
        turned = jnp.zeros((384, 2 * NEW), jnp.float32)
        for h in (0, 1):
            turned += jnp.dot(
                dturn[h], ubuf[h, :, :, at].reshape(PART, 2 * NEW),
                preferred_element_type=jnp.float32,
            )
        for n in (0, 1):
            q = 2 * p + n
            value = turned[:, n * NEW:(n + 1) * NEW].T
            value += jnp.dot(
                aring[8 * core + q], obuf[core], preferred_element_type=jnp.float32
            ) + jnp.dot(amate[q], obuf[mate], preferred_element_type=jnp.float32)
            total[q] = value
            tsend[q] = value.astype(jnp.bfloat16)
        for n in (0, 1):
            for step in (2, 1, 3):
                rcopy(2 * p + n, step).start()

    pltpu.make_async_copy(rest, rest, hrecv_sem).wait()
    for step in (1, 3, 2):
        some = rsum.at[step - 1]
        pltpu.make_async_copy(some, some, rrecv_sem.at[step - 1]).wait()
    rows = pl.ds(pl.multiple_of(32 * x, 32), 32)
    mine = pl.ds(pl.multiple_of(384 * me, 384), 384)

    @pl.loop(0, 8)
    def _(q):
        value = total[q, rows, :] + rsum[0, q].astype(jnp.float32)
        value += rsum[1, q].astype(jnp.float32) + rsum[2, q].astype(jnp.float32)
        share[q] = (rest[q].astype(jnp.float32) + (value + bias_ref[...])).astype(jnp.bfloat16)
        row = 8 * core + q

        @pl.when(row != me)
        def _():
            pltpu.make_async_remote_copy(
                src_ref=share.at[q], dst_ref=fout.at[rows, mine],
                send_sem=fsend_sem, recv_sem=frecv_sem,
                device_id=(row, 2 * x + goal), device_id_type=MESH,
            ).start()

        @pl.when(row == me)
        def _():
            pltpu.make_async_copy(share.at[q], fout.at[rows, mine], frecv_sem).start()

    def piece(owner, c):
        return fout.at[
            pl.ds(pl.multiple_of(32 * owner, 32), 32), pl.ds(pl.multiple_of(c * HALF, HALF), HALF)
        ]

    def gcopy(step):
        to = lax.rem(x + step, SIDE)
        return pltpu.make_async_remote_copy(
            src_ref=piece(x, core), dst_ref=piece(x, core), send_sem=gsend_sem.at[0, step],
            recv_sem=grecv_sem.at[0, step], device_id=(me, 2 * to + core), device_id_type=MESH,
        )

    def pass_on(step):
        owner = lax.rem(x - step + SIDE, SIDE)
        return pltpu.make_async_remote_copy(
            src_ref=piece(owner, core), dst_ref=piece(owner, core), send_sem=gsend_sem.at[1, step],
            recv_sem=grecv_sem.at[1, step], device_id=(me, 2 * x + mate), device_id_type=MESH,
        )

    def landed(kind, step):
        owner = lax.rem(x - step + SIDE, SIDE)
        ref = piece(owner, core if kind == 0 else mate)
        pltpu.make_async_copy(ref, ref, grecv_sem.at[kind, step]).wait()

    pltpu.make_async_copy(piece(x, core), piece(x, core), frecv_sem).wait()
    for step in (2, 1, 3):
        gcopy(step).start()
    pass_on(0).start()
    for step in (1, 3, 2):
        landed(0, step)
        pass_on(step).start()
    for step in (0, 1, 3, 2):
        landed(1, step)
    out_ref[...] = fout[...]

    for step in (1, 2, 3):
        gcopy(step).wait_send()
        some = rsum.at[step - 1]
        pltpu.make_async_copy(some, some, rsend_sem.at[step - 1]).wait()
    for step in range(4):
        pass_on(step).wait_send()
    pair.wait_send()

    @pl.when(goal == core)
    def _():
        some = share.at[pl.ds(0, 7)]
        pltpu.make_async_copy(some, some, fsend_sem).wait()
        some = rest_ref.at[pl.ds(0, 15)]
        pltpu.make_async_copy(some, some, hsend_sem).wait()

    @pl.when(goal != core)
    def _():
        pltpu.make_async_copy(share, share, fsend_sem).wait()

    for colour in (0, 1):
        some = ubuf.at[:, pl.ds(0, 15), :, pl.ds(512 * colour, 512)]
        pltpu.make_async_copy(some, some, usend_sem.at[colour]).wait()
        some = aring.at[pl.ds(0, 15), pl.ds(64 * colour, 64)]
        pltpu.make_async_copy(some, some, asend_sem.at[colour]).wait()


def back(units, attended, hidden, out_weight, down_weight, bias_total):
    req, x = lax.axis_index("req"), lax.axis_index("head") // 2
    rest = lax.dynamic_slice_in_dim(hidden, 32 * x, 32, 0)
    rest = rest.reshape(32, 16, 384).transpose(1, 0, 2)
    bias = lax.dynamic_slice_in_dim(bias_total, req * 384, 384, 0)[None, :]
    vmem = pl.BlockSpec(memory_space=pltpu.VMEM)
    hbm = pl.BlockSpec(memory_space=pl.ANY)
    dma = pltpu.SemaphoreType.DMA
    return pl.pallas_call(
        back_kernel,
        out_shape=jax.ShapeDtypeStruct((NEW, 2 * HALF), jnp.bfloat16),
        in_specs=[hbm, hbm, hbm, hbm, hbm, vmem],
        out_specs=vmem,
        scratch_shapes=[
            pltpu.VMEM((2, 16, 96, 1024), jnp.bfloat16),
            pltpu.VMEM((16, NEW, 384), jnp.bfloat16),
            pltpu.VMEM((8, NEW, 384), jnp.bfloat16),
            pltpu.VMEM((2, PART, 384), jnp.bfloat16),
            pltpu.VMEM((2, 384, 384), jnp.bfloat16),
            pltpu.VMEM((2, 384, PART), jnp.bfloat16),
            pltpu.VMEM((8, NEW, 384), jnp.float32),
            pltpu.VMEM((8, NEW, 384), jnp.bfloat16),
            pltpu.VMEM((3, 8, 32, 384), jnp.bfloat16),
            pltpu.VMEM((8, 32, 384), jnp.bfloat16),
            pltpu.VMEM((8, 32, 384), jnp.bfloat16),
            pltpu.VMEM((NEW, 2 * HALF), jnp.bfloat16),
            dma((2,)), dma((2, 2, 16)), dma((2,)), dma((2,)), dma((2, 2, 16)), dma((2,)), dma((6,)),
            dma, dma, dma((3,)), dma((3,)), dma, dma, dma((2, 4)), dma((2, 4)),
        ],
        compiler_params=pltpu.CompilerParams(
            collective_id=1, has_side_effects=True, vmem_limit_bytes=VMEM_LIMIT
        ),
        name="back",
    )(units, attended, down_weight, out_weight, rest, bias)


def body(
    hidden,
    attn_norm_gain,
    attn_norm_bias,
    mlp_norm_gain,
    mlp_norm_bias,
    qkv_weight,
    qkv_bias,
    out_weight,
    out_bias,
    up_weight,
    up_bias,
    down_weight,
    down_bias,
    cache_keys,
    cache_values,
    cached_len,
):
    gains = (attn_norm_gain, attn_norm_bias, mlp_norm_gain, mlp_norm_bias)
    qkv, units = front(hidden, gains, qkv_weight, up_weight, up_bias)
    attended, key_rows, value_rows = attention(
        qkv, qkv_bias, cached_len, cache_keys[0], cache_values[0]
    )
    result = back(units, attended, hidden, out_weight, down_weight, out_bias + down_bias)
    return (result, key_rows[None], value_rows[None])


def solution(mesh):
    return jax.shard_map(
        body,
        mesh=mesh,
        in_specs=(
            P("req", None),
            P(),
            P(),
            P(),
            P(),
            P("req", "head"),
            P("head"),
            P("head", "req"),
            P(),
            P("req", "head"),
            P("head"),
            P("head", "req"),
            P(),
            P("req", None, "head"),
            P("req", None, "head"),
            P("req"),
        ),
        out_specs=(P("req", None), P("req", None, "head"), P("req", None, "head")),
        check_vma=False,
    )
```

```python
import functools
import math

import jax
import jax.numpy as jnp
from jax import lax
from jax.experimental import pallas as pl
from jax.experimental.pallas import tpu as pltpu
from jax.sharding import PartitionSpec as P

DH = 96
ROT = 24
NEW = 128
CACHE = 4096
KB = 512
NT = (((1,), (1,)), ((), ()))


def rotation_tables(length):
    position = length.astype(jnp.float32) + jnp.arange(NEW, dtype=jnp.float32)
    halfway = ROT // 2
    exponent = jnp.arange(halfway, dtype=jnp.float32) * (2.0 / ROT)
    frequency = jnp.power(10000.0, -exponent)
    angle = position[None, :] * frequency[:, None]
    cosine, sine = jnp.cos(angle), jnp.sin(angle)
    return jnp.concatenate([cosine, cosine], 0), jnp.concatenate([-sine, sine], 0)


def attention_kernel(
    heads, len_ref, qkv_ref, bias_ref, cos_ref, sin_ref, k_hbm, v_hbm,
    att_ref, nk_ref, nv_ref, kbuf, vbuf, sbuf, qexp, ksem, vsem,
):
    scale = 1.0 / math.sqrt(DH)
    length = len_ref[0]
    width = heads * DH
    blocks = CACHE // KB
    used = (length + KB - 1) // KB

    def fetch(i, hbm, buf, sem):
        rows = pl.ds(pl.multiple_of(i * KB, KB), KB)
        return pltpu.make_async_copy(hbm.at[rows], buf.at[rows], sem.at[i])

    for hbm, buf, sem in ((k_hbm, kbuf, ksem), (v_hbm, vbuf, vsem)):
        @pl.loop(0, used)
        def _(i):
            fetch(i, hbm, buf, sem).start()

    cosine, sine = cos_ref[...], sin_ref[...]

    def turned(rows):
        low = rows[:ROT]
        swapped = jnp.concatenate([low[ROT // 2:], low[: ROT // 2]], axis=0)
        return jnp.concatenate([low * cosine + swapped * sine, rows[ROT:]], axis=0)

    def block(j, part):
        at = pl.ds((3 * j + part) * DH, DH)
        return qkv_ref[at, :] + bias_ref[at, :]

    queries = jnp.concatenate([turned(block(j, 0)) for j in range(heads)], 0).T.astype(jnp.bfloat16)
    keys = jnp.concatenate([turned(block(j, 1)) for j in range(heads)], 0).T.astype(jnp.bfloat16)
    values = jnp.concatenate([block(j, 2) for j in range(heads)], 0).T.astype(jnp.bfloat16)
    nk_ref[...] = keys
    nv_ref[...] = values
    lane_head = lax.broadcasted_iota(jnp.int32, (NEW, width), 1) // DH
    for j in range(heads):
        qexp[pl.ds(j * NEW, NEW), :] = jnp.where(lane_head == j, queries, jnp.zeros_like(queries))
    rows = heads * NEW
    fresh = lax.dot_general(qexp[...], keys, NT, preferred_element_type=jnp.float32) * scale
    row_at = lax.broadcasted_iota(jnp.int32, (rows, NEW), 0) % NEW
    col_at = lax.broadcasted_iota(jnp.int32, (rows, NEW), 1)
    fresh = jnp.where(col_at <= row_at, fresh, -1e30)

    def score(i, top):
        fetch(i, k_hbm, kbuf, ksem).wait()
        at = pl.ds(pl.multiple_of(i * KB, KB), KB)
        part = lax.dot_general(qexp[...], kbuf[at, :], NT, preferred_element_type=jnp.float32) * scale
        col = lax.broadcasted_iota(jnp.int32, (rows, KB), 1) + i * KB
        part = jnp.where(col < length, part, -1e30)
        sbuf[:, at] = part
        for t in range(KB // NEW):
            top = jnp.maximum(top, part[:, t * NEW:(t + 1) * NEW])
        return top

    top = lax.fori_loop(0, used, score, fresh)
    highest = jnp.max(top, axis=1, keepdims=True)
    fresh_weights = jnp.exp(fresh - highest)
    mixed = jnp.dot(fresh_weights.astype(jnp.bfloat16), values, preferred_element_type=jnp.float32)

    def weigh(i, carry):
        mixed, total = carry
        fetch(i, v_hbm, vbuf, vsem).wait()
        at = pl.ds(pl.multiple_of(i * KB, KB), KB)
        weights = jnp.exp(sbuf[:, at] - highest)
        for t in range(KB // NEW):
            total = total + weights[:, t * NEW:(t + 1) * NEW]
        mixed = mixed + jnp.dot(weights.astype(jnp.bfloat16), vbuf[at, :], preferred_element_type=jnp.float32)
        return mixed, total

    mixed, total = lax.fori_loop(0, used, weigh, (mixed, fresh_weights))
    total = jnp.sum(total, axis=1, keepdims=True)
    out = jnp.zeros((NEW, width), jnp.float32)
    for j in range(heads):
        at = slice(j * NEW, (j + 1) * NEW)
        out = jnp.where(lane_head == j, mixed[at] / total[at], out)
    att_ref[...] = out.astype(jnp.bfloat16)


def attention(qkv_t, bias, length, keys_old, values_old):
    heads = qkv_t.shape[0] // (3 * DH)
    width = heads * DH
    cosine, sine = rotation_tables(length[0])
    vmem = pl.BlockSpec(memory_space=pltpu.VMEM)
    hbm = pl.BlockSpec(memory_space=pl.ANY)
    out = jax.ShapeDtypeStruct((NEW, width), jnp.bfloat16)
    return pl.pallas_call(
        functools.partial(attention_kernel, heads),
        out_shape=(out, out, out),
        in_specs=[pl.BlockSpec(memory_space=pltpu.SMEM), vmem, vmem, vmem, vmem, hbm, hbm],
        out_specs=(vmem, vmem, vmem),
        scratch_shapes=[
            pltpu.VMEM((CACHE, width), jnp.bfloat16),
            pltpu.VMEM((CACHE, width), jnp.bfloat16),
            pltpu.VMEM((heads * NEW, CACHE), jnp.float32),
            pltpu.VMEM((heads * NEW, width), jnp.bfloat16),
            pltpu.SemaphoreType.DMA((CACHE // KB,)),
            pltpu.SemaphoreType.DMA((CACHE // KB,)),
        ],
        compiler_params=pltpu.CompilerParams(vmem_limit_bytes=60 * 2**20),
        name="attention",
    )(length, qkv_t, bias[:, None], cosine, sine, keys_old, values_old)


MESH = pl.DeviceIdType.MESH
SIDE = 4
HALF = 3072
PART = 1536
DIRECT = 512
VMEM_LIMIT = 62 * 2**20


def place():
    req, head = lax.axis_index("req"), lax.axis_index("head")
    return req // SIDE, req % SIDE, head // 2, head % 2


def meet(barrier, others):
    for count, target, alone in others:
        @pl.loop(0, count)
        def _(i):
            @pl.when(alone(i))
            def _():
                pl.semaphore_signal(barrier, inc=1, device_id=target(i), device_id_type=MESH)


def ring_units(y, z, x, core, own, slot, part, send_sem, recv_sem):
    def send(colour, dp, ds, half, along, step):
        to = [dp, ds]
        to[along] = (to[along] + step) % SIDE if isinstance(to[along], int) else lax.rem(
            to[along] + step + SIDE, SIDE)
        on_z = (colour == 0) == (along == 0)
        dev_y = y if on_z else lax.rem(y + step + SIDE, SIDE)
        dev_z = lax.rem(z + step + SIDE, SIDE) if on_z else z
        is_own = isinstance(dp, int) and isinstance(ds, int) and dp == 0 and ds == 0
        src = own(colour, half) if is_own else part(slot(colour, dp, ds, 0), colour, half)
        source = (colour, dp, ds)
        dst = part(slot(*source, 0), colour, half) if slot.absolute else part(
            slot(colour, to[0], to[1], 0), colour, half)
        return pltpu.make_async_remote_copy(
            src_ref=src, dst_ref=dst, send_sem=send_sem.at[colour],
            recv_sem=recv_sem.at[colour, half, to[0] * SIDE + to[1]],
            device_id=(dev_y * SIDE + dev_z, 2 * x + core), device_id_type=MESH,
        )

    def arrived(colour, dp, ds, half):
        ref = part(slot(colour, dp, ds, 0), colour, half)
        pltpu.make_async_copy(ref, ref, recv_sem.at[colour, half, dp * SIDE + ds]).wait()

    return send, arrived


FIRST = ((1, 0), (3, 1), (1, 1), (3, 0), (2, 0), (2, 1))


def ring_start(send):
    for along in (0, 1):
        for half in (0, 1):
            for colour in (0, 1):
                for step in (1, -1):
                    send(colour, 0, 0, half, along, step).start()


def ring_spread(send, dp):
    for half in (0, 1):
        for colour in (0, 1):
            for step in (1, -1):
                send(colour, dp, 0, half, 1, step).start()


def ring_first(send, arrived):
    for dp, half in FIRST:
        if (dp, half) == (2, 0):
            ring_spread(send, 1)
        for colour in (0, 1):
            arrived(colour, dp, 0, half)
            if (dp, half) in ((1, 0), (3, 1)):
                send(colour, dp, 0, half, 0, 1 if dp == 1 else -1).start()


def ring_second(send, arrived, i):
    dp = gray(i)
    for ds, half in FIRST:
        if (ds, half) == (2, 0):
            @pl.when(i < 2)
            def _():
                ring_spread(send, gray(i + 2))
        for colour in (0, 1):
            arrived(colour, dp, ds, half)
            if (ds, half) in ((1, 0), (3, 1)):
                send(colour, dp, ds, half, 1, 1 if ds == 1 else -1).start()


def gray(i):
    return i + (i // 2) * (1 - 2 * (i % 2))


class Relative:
    absolute = False

    def __call__(self, colour, dp, ds, _):
        return dp * SIDE + ds


class Absolute:
    absolute = True

    def __init__(self, y, z):
        self.y, self.z = y, z

    def __call__(self, colour, dp, ds, _):
        dy, dz = (ds, dp) if colour == 0 else (dp, ds)
        return lax.rem(self.y - dy + SIDE, SIDE) * SIDE + lax.rem(self.z - dz + SIDE, SIDE)


def front_kernel(
    hid_ref, stat_ref, wt_ref, gain_ref, ub_ref, qkv_ref, units_ref,
    xbuf, sbuf, stats, wbuf, nbuf, pbuf, rbuf, bbuf, qsend, qrecv,
    xsend_sem, xrecv_sem, own_sem, side_send, side_recv, stat_send, stat_recv,
    wsend_sem, wrecv_sem, wself_sem, bias_sem, pair_sem, qsend_sem, qrecv_sem,
):
    y, z, x, core = place()
    me = y * SIDE + z
    mate = 1 - core
    own_copies = []
    for colour in (0, 1):
        base = core * HALF + colour * PART

        def take(lane, width, dst, n):
            at = pl.ds(pl.multiple_of(base + lane, 256), width)
            own_copies.append(
                pltpu.make_async_copy(hid_ref.at[:, at], dst, own_sem.at[colour, n]))

        take(0, DIRECT, xbuf.at[colour, 0, :, pl.ds(0, DIRECT)], 0)
        take(DIRECT + 256 * x, 256, xbuf.at[colour, 0, :, pl.ds(DIRECT, 256)], 1)
        for dx in (1, 2, 3):
            plane_at = lax.rem(x - dx + SIDE, SIDE)
            take(DIRECT + 256 * plane_at, 256, sbuf.at[colour, dx - 1, 0], 1 + dx)
    for copy in own_copies:
        copy.start()
    barrier = pltpu.get_barrier_semaphore()

    def plane(i):
        return (i // 2, 2 * x + i % 2)

    def line(i):
        return (me, i)

    meet(barrier, [
        (32, plane, lambda i: i != 2 * me + core),
        (8, line, lambda i: i // 2 != x),
    ])
    for copy in own_copies:
        copy.wait()
    pl.semaphore_wait(barrier, 37)

    goal = y // 2
    kat = pl.ds(pl.multiple_of(((y % 2) * SIDE + z) * 384, 384), 384)

    def part(s, colour, half):
        return xbuf.at[colour, s, pl.ds(64 * half, 64)]

    def own(colour, half):
        return part(0, colour, half)

    send, arrived = ring_units(y, z, x, core, own, Relative(), part, xsend_sem, xrecv_sem)
    ring_start(send)

    def other(i):
        return lax.rem(y + i // SIDE, SIDE) * SIDE + lax.rem(z + i % SIDE, SIDE)

    @pl.loop(1, 16)
    def _(i):
        pltpu.make_async_remote_copy(
            src_ref=stat_ref, dst_ref=stats.at[me], send_sem=stat_send, recv_sem=stat_recv,
            device_id=(other(i), 2 * x + core), device_id_type=MESH,
        ).start()
    pltpu.make_async_copy(stat_ref, stats.at[me], stat_recv).start()
    bias_own = pltpu.make_async_copy(ub_ref, bbuf.at[core], bias_sem.at[0])
    bias_mate = pltpu.make_async_remote_copy(
        src_ref=ub_ref, dst_ref=bbuf.at[core], send_sem=bias_sem.at[1], recv_sem=bias_sem.at[2],
        device_id=(me, 2 * x + mate), device_id_type=MESH,
    )
    bias_own.start()
    bias_mate.start()

    def mate_w():
        return pltpu.make_async_remote_copy(
            src_ref=wt_ref.at[me], dst_ref=wbuf.at[:, core, :, kat],
            send_sem=wself_sem, recv_sem=wrecv_sem,
            device_id=(me, 2 * x + mate), device_id_type=MESH,
        )

    @pl.when(goal != core)
    def _():
        mate_w().start()

    @pl.when(goal == core)
    def _():
        pltpu.make_async_copy(wt_ref.at[me], wbuf.at[:, core, :, kat], wrecv_sem).start()

    def weights_out(first, count):
        @pl.loop(first, first + count)
        def _(i):
            pltpu.make_async_remote_copy(
                src_ref=wt_ref.at[other(i)], dst_ref=wbuf.at[:, core, :, kat],
                send_sem=wsend_sem, recv_sem=wrecv_sem,
                device_id=(other(i), 2 * x + goal), device_id_type=MESH,
            ).start()

    def slots(kind, dp):
        return pl.ds(dp * SIDE, 1) if kind == 0 else pl.ds(dp * SIDE + 1, 3)

    def side_full(colour, kind, dp, step):
        way = (1 - step) // 2
        return pltpu.make_async_remote_copy(
            src_ref=xbuf.at[colour, slots(kind, dp), :, pl.ds(DIRECT, 256)],
            dst_ref=sbuf.at[colour, 2 * way, slots(kind, dp)],
            send_sem=side_send.at[colour], recv_sem=side_recv.at[colour, kind, dp, way],
            device_id=(me, 2 * lax.rem(x + step + SIDE, SIDE) + core), device_id_type=MESH,
        )

    def side_relay(colour, kind, dp, step):
        way = (1 - step) // 2
        rows = pl.ds(64 * way, 64)
        return pltpu.make_async_remote_copy(
            src_ref=sbuf.at[colour, 2 * way, slots(kind, dp), rows],
            dst_ref=sbuf.at[colour, 1, slots(kind, dp), rows],
            send_sem=side_send.at[colour], recv_sem=side_recv.at[colour, kind, dp, 2 + way],
            device_id=(me, 2 * lax.rem(x + step + SIDE, SIDE) + core), device_id_type=MESH,
        )

    def side_wait(colour, kind, dp, n):
        if n < 2:
            ref = sbuf.at[colour, 2 * n, slots(kind, dp)]
        else:
            ref = sbuf.at[colour, 1, slots(kind, dp), pl.ds(64 * (n - 2), 64)]
        pltpu.make_async_copy(ref, ref, side_recv.at[colour, kind, dp, n]).wait()

    def side_out(kind, dp):
        for colour in (0, 1):
            for step in (1, -1):
                side_full(colour, kind, dp, step).start()

    def side_on(kind, dp):
        for colour in (0, 1):
            for way in (0, 1):
                side_wait(colour, kind, dp, way)
                side_relay(colour, kind, dp, 1 - 2 * way).start()

    pbuf[...] = jnp.zeros_like(pbuf)
    ring_first(send, arrived)
    for dp in (1, 3, 2):
        side_out(0, dp)

    def origin(colour, dp, ds):
        dy = colour * dp + (1 - colour) * ds
        dz = colour * ds + (1 - colour) * dp
        return lax.rem(y - dy + SIDE, SIDE) * SIDE + lax.rem(z - dz + SIDE, SIDE)

    def compute(colour, dp):
        @pl.loop(0, SIDE)
        def _(ds):
            s = dp * SIDE + ds
            turned = stats[origin(colour, dp, ds)].T
            center, spread = turned[:, 0:1], turned[:, 1:2]
            rows = pl.ds(pl.multiple_of(ds * NEW, NEW), NEW)
            base = core * HALF + colour * PART

            def norm(raw, lane, width):
                value = (raw.astype(jnp.float32) - center) * spread
                at = pl.ds(pl.multiple_of(base + lane, 256), width)
                to = pl.ds(pl.multiple_of(lane, 256), width)
                for kind in (0, 1):
                    nbuf[kind, rows, to] = (
                        value * gain_ref[2 * kind:2 * kind + 1, at]
                        + gain_ref[2 * kind + 1:2 * kind + 2, at]
                    ).astype(jnp.bfloat16)

            norm(xbuf[colour, s, :, 0:DIRECT], 0, DIRECT)
            norm(xbuf[colour, s, :, DIRECT:DIRECT + 256], DIRECT + 256 * x, 256)
            for dx in (1, 2, 3):
                norm(sbuf[colour, dx - 1, s], DIRECT + 256 * lax.rem(x - dx + SIDE, SIDE), 256)

        for kind in (0, 1):
            left = wbuf[kind, :, :, pl.ds(pl.multiple_of(colour * PART, PART), PART)]
            product = lax.dot_general(
                left.reshape(192, PART), nbuf[kind], NT, preferred_element_type=jnp.float32
            )
            for ds in range(SIDE):
                row = origin(colour, dp, ds)
                pbuf[row, 192 * kind:192 * (kind + 1), :] += product[:, ds * NEW:(ds + 1) * NEW]

    @pl.loop(0, SIDE)
    def _(i):
        ring_second(send, arrived, i)
        side_out(1, gray(i))

    weights_out(1, 15)
    for dp in (1, 3, 2):
        side_on(0, dp)

    @pl.loop(0, SIDE)
    def _(i):
        side_on(1, gray(i))

    pltpu.make_async_copy(stats, stats, stat_recv).wait()
    pltpu.make_async_copy(wbuf, wbuf, wrecv_sem).wait()

    @pl.loop(0, SIDE)
    def _(i):
        dp = gray(i)
        for colour in (0, 1):
            for n in (2, 3):
                side_wait(colour, 1, dp, n)

            @pl.when(i > 0)
            def _():
                for n in (2, 3):
                    side_wait(colour, 0, dp, n)

        @pl.loop(0, 2)
        def _(colour):
            compute(colour, dp)

    pair = pltpu.make_async_remote_copy(
        src_ref=pbuf.at[pl.ds(8 * mate, 8)], dst_ref=rbuf,
        send_sem=pair_sem.at[0], recv_sem=pair_sem.at[1],
        device_id=(me, 2 * x + mate), device_id_type=MESH,
    )
    pair.start()
    bias_own.wait()
    bias_mate.wait()
    pair.wait_recv()
    mine = pl.ds(pl.multiple_of(me * 72, 8), 72)

    @pl.loop(0, 8)
    def _(q):
        row = 8 * core + q
        total = pbuf[row] + rbuf[q]
        for h in (0, 1):
            qsend[2 * q + h] = total[96 * h:96 * h + 72]
            remote = pltpu.make_async_remote_copy(
                src_ref=qsend.at[2 * q + h], dst_ref=qrecv.at[mine],
                send_sem=qsend_sem, recv_sem=qrecv_sem,
                device_id=(row, 2 * x + h), device_id_type=MESH,
            )
            away = jnp.logical_or(row != me, core != h)

            @pl.when(away)
            def _():
                remote.start()

            @pl.when(jnp.logical_not(away))
            def _():
                pltpu.make_async_copy(qsend.at[2 * q + h], qrecv.at[mine], qrecv_sem).start()
        at = pl.ds(pl.multiple_of(q * NEW, NEW), NEW)
        for h in (0, 1):
            u = total[192 + 96 * h:288 + 96 * h] + bbuf[h]
            inner = 0.7978845608028654 * (u + 0.044715 * (u * u * u))
            units_ref[h, :, at] = (0.5 * u * (1.0 + jnp.tanh(inner))).astype(jnp.bfloat16)

    pltpu.make_async_copy(qrecv, qrecv, qrecv_sem).wait()
    qkv_ref[...] = qrecv[...]
    pair.wait_send()

    @pl.when(goal == core)
    def _():
        some = qsend.at[pl.ds(0, 15)]
        pltpu.make_async_copy(some, some, qsend_sem).wait()

    @pl.when(goal != core)
    def _():
        pltpu.make_async_copy(qsend, qsend, qsend_sem).wait()
        mate_w().wait_send()

    some = wt_ref.at[pl.ds(0, 15)]
    pltpu.make_async_copy(some, some, wsend_sem).wait()
    for colour in (0, 1):
        some = xbuf.at[colour, pl.ds(1, 15)]
        pltpu.make_async_copy(some, some, xsend_sem.at[colour]).wait()
        some = sbuf.at[colour, :, pl.ds(1, 15)]
        pltpu.make_async_copy(some, some, side_send.at[colour]).wait()
    some = stats.at[pl.ds(0, 15)]
    pltpu.make_async_copy(some, some, stat_send).wait()


def front(hidden, gains, qkv_weight, up_weight, up_bias):
    req = lax.axis_index("req")
    widened = hidden.astype(jnp.float32)
    center = jnp.mean(widened, axis=-1)
    spread = lax.rsqrt(jnp.mean(jnp.square(widened - center[:, None]), axis=-1) + 1e-05)
    stat = jnp.pad(jnp.stack([center, spread]), ((0, 6), (0, 0)))
    depth = qkv_weight.shape[0]
    wq = jnp.pad(qkv_weight.T.reshape(16, 72, depth), ((0, 0), (0, 24), (0, 0)))
    wt = jnp.stack([wq, up_weight.T.reshape(16, 96, depth)], axis=1)
    gain = jnp.stack(gains)
    bias = lax.dynamic_slice_in_dim(up_bias, req * 96, 96, 0)
    bias = jnp.broadcast_to(bias[:, None], (96, 128))
    vmem = pl.BlockSpec(memory_space=pltpu.VMEM)
    hbm = pl.BlockSpec(memory_space=pl.ANY)
    dma = pltpu.SemaphoreType.DMA
    return pl.pallas_call(
        front_kernel,
        out_shape=(
            jax.ShapeDtypeStruct((1152, NEW), jnp.float32),
            jax.ShapeDtypeStruct((2, 96, 1024), jnp.bfloat16),
        ),
        in_specs=[hbm, hbm, hbm, vmem, hbm],
        out_specs=(vmem, vmem),
        scratch_shapes=[
            pltpu.VMEM((2, 16, NEW, DIRECT + 256), jnp.bfloat16),
            pltpu.VMEM((2, 3, 16, NEW, 256), jnp.bfloat16),
            pltpu.VMEM((16, 8, NEW), jnp.float32),
            pltpu.VMEM((2, 2, 96, HALF), jnp.bfloat16),
            pltpu.VMEM((2, 512, PART), jnp.bfloat16),
            pltpu.VMEM((16, 384, NEW), jnp.float32),
            pltpu.VMEM((8, 384, NEW), jnp.float32),
            pltpu.VMEM((2, 96, NEW), jnp.float32),
            pltpu.VMEM((16, 72, NEW), jnp.float32),
            pltpu.VMEM((1152, NEW), jnp.float32),
            dma((2,)), dma((2, 2, 16)), dma((2, 5)), dma((2,)), dma((2, 2, 4, 4)), dma, dma,
            dma, dma, dma, dma((3,)), dma((2,)), dma, dma,
        ],
        compiler_params=pltpu.CompilerParams(
            collective_id=0, has_side_effects=True, vmem_limit_bytes=VMEM_LIMIT
        ),
        name="front",
    )(hidden, stat, wt, gain, bias)


def back_kernel(
    units_ref, att_ref, wd_ref, wo_ref, rest_ref, bias_ref, out_ref,
    ubuf, aring, amate, dbuf, obuf, dturn, total, tsend, rsum, share, rest, fout,
    usend_sem, urecv_sem, own_sem, asend_sem, arecv_sem, amate_sem, w_sem,
    hsend_sem, hrecv_sem, rsend_sem, rrecv_sem, fsend_sem, frecv_sem, gsend_sem, grecv_sem,
):
    y, z, x, core = place()
    me = y * SIDE + z
    mate = 1 - core
    goal = y // 2
    barrier = pltpu.get_barrier_semaphore()

    def plane(i):
        return (i // 2, 2 * x + i % 2)

    def line(i):
        return (me, i)

    meet(barrier, [
        (32, plane, lambda i: i != 2 * me + core),
        (8, line, lambda i: i // 2 != x),
    ])
    pl.semaphore_wait(barrier, 37)

    def apart(s, colour, half):
        return aring.at[s, pl.ds(32 * (2 * colour + half), 32)]

    def aown(colour, half):
        return att_ref.at[pl.ds(32 * (2 * colour + half), 32)]

    asend, aarrived = ring_units(y, z, x, core, aown, Absolute(y, z), apart, asend_sem, arecv_sem)
    ring_start(asend)

    def lanes(colour, half):
        return pl.ds((2 * colour + half) * 256, 256)

    def part(s, colour, half):
        return ubuf.at[:, s, :, lanes(colour, half)]

    def own(colour, half):
        return units_ref.at[:, :, lanes(colour, half)]

    send, arrived = ring_units(y, z, x, core, own, Absolute(y, z), part, usend_sem, urecv_sem)
    ring_start(send)
    copies = [
        pltpu.make_async_copy(units_ref, ubuf.at[:, me], own_sem.at[0]),
        pltpu.make_async_copy(att_ref, aring.at[me], own_sem.at[1]),
    ]
    for n, (src, dst) in enumerate(((wd_ref, dbuf), (wo_ref, obuf))):
        copies.append(pltpu.make_async_copy(src, dst.at[core], w_sem.at[3 * n]))
        copies.append(pltpu.make_async_remote_copy(
            src_ref=src, dst_ref=dst.at[core], send_sem=w_sem.at[3 * n + 1],
            recv_sem=w_sem.at[3 * n + 2], device_id=(me, 2 * x + mate), device_id_type=MESH,
        ))
    for copy in copies:
        copy.start()
    slot = me % 8

    @pl.when(goal == core)
    def _():
        @pl.loop(1, 16)
        def _(i):
            row = lax.rem(y + i // SIDE, SIDE) * SIDE + lax.rem(z + i % SIDE, SIDE)
            pltpu.make_async_remote_copy(
                src_ref=rest_ref.at[row], dst_ref=rest.at[slot],
                send_sem=hsend_sem, recv_sem=hrecv_sem,
                device_id=(row, 2 * x + core), device_id_type=MESH,
            ).start()
        pltpu.make_async_copy(rest_ref.at[me], rest.at[slot], hrecv_sem).start()

    ring_first(asend, aarrived)
    ring_first(send, arrived)

    @pl.loop(0, SIDE)
    def _(i):
        ring_second(asend, aarrived, i)

    for copy in copies:
        copy.wait()
    pair = pltpu.make_async_remote_copy(
        src_ref=aring.at[pl.ds(8 * mate, 8)], dst_ref=amate,
        send_sem=amate_sem.at[0], recv_sem=amate_sem.at[1],
        device_id=(me, 2 * x + mate), device_id_type=MESH,
    )
    pair.start()

    @pl.loop(0, SIDE)
    def _(i):
        @pl.loop(0, 6)
        def _(k):
            n = 6 * i + k
            h, at = n // 12, pl.ds(pl.multiple_of((n % 12) * 128, 128), 128)
            dturn[h, :, at] = dbuf[h, at, :].T

        ring_second(send, arrived, i)

    pair.wait_recv()

    def rcopy(q, step):
        to = lax.rem(x + step, SIDE)
        return pltpu.make_async_remote_copy(
            src_ref=tsend.at[q, pl.ds(pl.multiple_of(32 * to, 32), 32)],
            dst_ref=rsum.at[step - 1, q],
            send_sem=rsend_sem.at[step - 1], recv_sem=rrecv_sem.at[step - 1],
            device_id=(me, 2 * to + core), device_id_type=MESH,
        )

    @pl.loop(0, 4)
    def _(p):
        at = pl.ds(pl.multiple_of(2 * p * NEW, 2 * NEW), 2 * NEW)
        turned = jnp.zeros((384, 2 * NEW), jnp.float32)
        for h in (0, 1):
            turned += jnp.dot(
                dturn[h], ubuf[h, :, :, at].reshape(PART, 2 * NEW),
                preferred_element_type=jnp.float32,
            )
        for n in (0, 1):
            q = 2 * p + n
            value = turned[:, n * NEW:(n + 1) * NEW].T
            value += jnp.dot(
                aring[8 * core + q], obuf[core], preferred_element_type=jnp.float32
            ) + jnp.dot(amate[q], obuf[mate], preferred_element_type=jnp.float32)
            total[q] = value
            tsend[q] = value.astype(jnp.bfloat16)
        for n in (0, 1):
            for step in (2, 1, 3):
                rcopy(2 * p + n, step).start()

    pltpu.make_async_copy(rest, rest, hrecv_sem).wait()
    for step in (1, 3, 2):
        some = rsum.at[step - 1]
        pltpu.make_async_copy(some, some, rrecv_sem.at[step - 1]).wait()
    rows = pl.ds(pl.multiple_of(32 * x, 32), 32)
    mine = pl.ds(pl.multiple_of(384 * me, 384), 384)

    @pl.loop(0, 8)
    def _(q):
        value = total[q, rows, :] + rsum[0, q].astype(jnp.float32)
        value += rsum[1, q].astype(jnp.float32) + rsum[2, q].astype(jnp.float32)
        share[q] = (rest[q].astype(jnp.float32) + (value + bias_ref[...])).astype(jnp.bfloat16)
        row = 8 * core + q

        @pl.when(row != me)
        def _():
            pltpu.make_async_remote_copy(
                src_ref=share.at[q], dst_ref=fout.at[rows, mine],
                send_sem=fsend_sem, recv_sem=frecv_sem,
                device_id=(row, 2 * x + goal), device_id_type=MESH,
            ).start()

        @pl.when(row == me)
        def _():
            pltpu.make_async_copy(share.at[q], fout.at[rows, mine], frecv_sem).start()

    def piece(owner, c):
        return fout.at[
            pl.ds(pl.multiple_of(32 * owner, 32), 32), pl.ds(pl.multiple_of(c * HALF, HALF), HALF)
        ]

    def gcopy(step):
        to = lax.rem(x + step, SIDE)
        return pltpu.make_async_remote_copy(
            src_ref=piece(x, core), dst_ref=piece(x, core), send_sem=gsend_sem.at[0, step],
            recv_sem=grecv_sem.at[0, step], device_id=(me, 2 * to + core), device_id_type=MESH,
        )

    def pass_on(step):
        owner = lax.rem(x - step + SIDE, SIDE)
        return pltpu.make_async_remote_copy(
            src_ref=piece(owner, core), dst_ref=piece(owner, core), send_sem=gsend_sem.at[1, step],
            recv_sem=grecv_sem.at[1, step], device_id=(me, 2 * x + mate), device_id_type=MESH,
        )

    def landed(kind, step):
        owner = lax.rem(x - step + SIDE, SIDE)
        ref = piece(owner, core if kind == 0 else mate)
        pltpu.make_async_copy(ref, ref, grecv_sem.at[kind, step]).wait()

    pltpu.make_async_copy(piece(x, core), piece(x, core), frecv_sem).wait()
    for step in (2, 1, 3):
        gcopy(step).start()
    pass_on(0).start()
    for step in (1, 3, 2):
        landed(0, step)
        pass_on(step).start()
    for step in (0, 1, 3, 2):
        landed(1, step)
    out_ref[...] = fout[...]

    for step in (1, 2, 3):
        gcopy(step).wait_send()
        some = rsum.at[step - 1]
        pltpu.make_async_copy(some, some, rsend_sem.at[step - 1]).wait()
    for step in range(4):
        pass_on(step).wait_send()
    pair.wait_send()

    @pl.when(goal == core)
    def _():
        some = share.at[pl.ds(0, 7)]
        pltpu.make_async_copy(some, some, fsend_sem).wait()
        some = rest_ref.at[pl.ds(0, 15)]
        pltpu.make_async_copy(some, some, hsend_sem).wait()

    @pl.when(goal != core)
    def _():
        pltpu.make_async_copy(share, share, fsend_sem).wait()

    for colour in (0, 1):
        some = ubuf.at[:, pl.ds(0, 15), :, pl.ds(512 * colour, 512)]
        pltpu.make_async_copy(some, some, usend_sem.at[colour]).wait()
        some = aring.at[pl.ds(0, 15), pl.ds(64 * colour, 64)]
        pltpu.make_async_copy(some, some, asend_sem.at[colour]).wait()


def back(units, attended, hidden, out_weight, down_weight, bias_total):
    req, x = lax.axis_index("req"), lax.axis_index("head") // 2
    rest = lax.dynamic_slice_in_dim(hidden, 32 * x, 32, 0)
    rest = rest.reshape(32, 16, 384).transpose(1, 0, 2)
    bias = lax.dynamic_slice_in_dim(bias_total, req * 384, 384, 0)[None, :]
    vmem = pl.BlockSpec(memory_space=pltpu.VMEM)
    hbm = pl.BlockSpec(memory_space=pl.ANY)
    dma = pltpu.SemaphoreType.DMA
    return pl.pallas_call(
        back_kernel,
        out_shape=jax.ShapeDtypeStruct((NEW, 2 * HALF), jnp.bfloat16),
        in_specs=[hbm, hbm, hbm, hbm, hbm, vmem],
        out_specs=vmem,
        scratch_shapes=[
            pltpu.VMEM((2, 16, 96, 1024), jnp.bfloat16),
            pltpu.VMEM((16, NEW, 384), jnp.bfloat16),
            pltpu.VMEM((8, NEW, 384), jnp.bfloat16),
            pltpu.VMEM((2, PART, 384), jnp.bfloat16),
            pltpu.VMEM((2, 384, 384), jnp.bfloat16),
            pltpu.VMEM((2, 384, PART), jnp.bfloat16),
            pltpu.VMEM((8, NEW, 384), jnp.float32),
            pltpu.VMEM((8, NEW, 384), jnp.bfloat16),
            pltpu.VMEM((3, 8, 32, 384), jnp.bfloat16),
            pltpu.VMEM((8, 32, 384), jnp.bfloat16),
            pltpu.VMEM((8, 32, 384), jnp.bfloat16),
            pltpu.VMEM((NEW, 2 * HALF), jnp.bfloat16),
            dma((2,)), dma((2, 2, 16)), dma((2,)), dma((2,)), dma((2, 2, 16)), dma((2,)), dma((6,)),
            dma, dma, dma((3,)), dma((3,)), dma, dma, dma((2, 4)), dma((2, 4)),
        ],
        compiler_params=pltpu.CompilerParams(
            collective_id=1, has_side_effects=True, vmem_limit_bytes=VMEM_LIMIT
        ),
        name="back",
    )(units, attended, down_weight, out_weight, rest, bias)


def body(
    hidden,
    attn_norm_gain,
    attn_norm_bias,
    mlp_norm_gain,
    mlp_norm_bias,
    qkv_weight,
    qkv_bias,
    out_weight,
    out_bias,
    up_weight,
    up_bias,
    down_weight,
    down_bias,
    cache_keys,
    cache_values,
    cached_len,
):
    gains = (attn_norm_gain, attn_norm_bias, mlp_norm_gain, mlp_norm_bias)
    qkv, units = front(hidden, gains, qkv_weight, up_weight, up_bias)
    attended, key_rows, value_rows = attention(
        qkv, qkv_bias, cached_len, cache_keys[0], cache_values[0]
    )
    result = back(units, attended, hidden, out_weight, down_weight, out_bias + down_bias)
    return (result, key_rows[None], value_rows[None])


def solution(mesh):
    return jax.shard_map(
        body,
        mesh=mesh,
        in_specs=(
            P("req", None),
            P(),
            P(),
            P(),
            P(),
            P("req", "head"),
            P("head"),
            P("head", "req"),
            P(),
            P("req", "head"),
            P("head"),
            P("head", "req"),
            P(),
            P("req", None, "head"),
            P("req", None, "head"),
            P("req"),
        ),
        out_specs=(P("req", None), P("req", None, "head"), P("req", None, "head")),
        check_vma=False,
    )
```

```python
import functools
import math

import jax
import jax.numpy as jnp
from jax import lax
from jax.experimental import pallas as pl
from jax.experimental.pallas import tpu as pltpu
from jax.sharding import PartitionSpec as P

DH = 96
ROT = 24
NEW = 128
CACHE = 4096
KB = 512
NT = (((1,), (1,)), ((), ()))


def rotation_tables(length):
    position = length.astype(jnp.float32) + jnp.arange(NEW, dtype=jnp.float32)
    halfway = ROT // 2
    exponent = jnp.arange(halfway, dtype=jnp.float32) * (2.0 / ROT)
    frequency = jnp.power(10000.0, -exponent)
    angle = position[None, :] * frequency[:, None]
    cosine, sine = jnp.cos(angle), jnp.sin(angle)
    return jnp.concatenate([cosine, cosine], 0), jnp.concatenate([-sine, sine], 0)


def fetch(n, hbm, buf, sem):
    rows = pl.ds(pl.multiple_of(n * KB, KB), KB)
    return pltpu.make_async_copy(hbm.at[rows], buf.at[rows], sem.at[n])


def attention_scores(heads, length, qkv_ref, bias_ref, cos_ref, sin_ref, nk_ref, nv_ref, keep, key_block):
    scale = 1.0 / math.sqrt(DH)
    width = heads * DH
    vkeep, qexp, sbuf = keep
    cosine, sine = cos_ref[...], sin_ref[...]

    def turned(rows):
        low = rows[:ROT]
        swapped = jnp.concatenate([low[ROT // 2:], low[: ROT // 2]], axis=0)
        return jnp.concatenate([low * cosine + swapped * sine, rows[ROT:]], axis=0)

    def block(j, part):
        at = pl.ds((3 * j + part) * DH, DH)
        return qkv_ref[at, :] + bias_ref[at, :]

    queries = jnp.concatenate([turned(block(j, 0)) for j in range(heads)], 0).T.astype(jnp.bfloat16)
    keys = jnp.concatenate([turned(block(j, 1)) for j in range(heads)], 0).T.astype(jnp.bfloat16)
    values = jnp.concatenate([block(j, 2) for j in range(heads)], 0).T.astype(jnp.bfloat16)
    nk_ref[...] = keys
    nv_ref[...] = values
    vkeep[...] = values
    lane_head = lax.broadcasted_iota(jnp.int32, (NEW, width), 1) // DH
    for j in range(heads):
        qexp[pl.ds(j * NEW, NEW), :] = jnp.where(lane_head == j, queries, jnp.zeros_like(queries))
    rows = heads * NEW
    fresh = lax.dot_general(qexp[...], keys, NT, preferred_element_type=jnp.float32) * scale
    row_at = lax.broadcasted_iota(jnp.int32, (rows, NEW), 0) % NEW
    col_at = lax.broadcasted_iota(jnp.int32, (rows, NEW), 1)
    fresh = jnp.where(col_at <= row_at, fresh, -1e30)
    sbuf[:, CACHE:] = fresh

    def score(n, top):
        at = pl.ds(pl.multiple_of(n * KB, KB), KB)
        part = lax.dot_general(
            qexp[...], key_block(n, at), NT, preferred_element_type=jnp.float32) * scale
        col = lax.broadcasted_iota(jnp.int32, (rows, KB), 1) + n * KB
        part = jnp.where(col < length, part, -1e30)
        sbuf[:, at] = part
        for t in range(KB // NEW):
            top = jnp.maximum(top, part[:, t * NEW:(t + 1) * NEW])
        return top

    return lax.fori_loop(0, CACHE // KB, score, fresh)


def attention_mix(heads, top, keep, att_ref, value_block):
    width = heads * DH
    vkeep, _, sbuf = keep
    highest = jnp.max(top, axis=1, keepdims=True)
    fresh_weights = jnp.exp(sbuf[:, CACHE:] - highest)
    mixed = jnp.dot(
        fresh_weights.astype(jnp.bfloat16), vkeep[...], preferred_element_type=jnp.float32)

    def weigh(n, carry):
        mixed, total = carry
        at = pl.ds(pl.multiple_of(n * KB, KB), KB)
        weights = jnp.exp(sbuf[:, at] - highest)
        for t in range(KB // NEW):
            total = total + weights[:, t * NEW:(t + 1) * NEW]
        mixed = mixed + jnp.dot(
            weights.astype(jnp.bfloat16), value_block(n, at), preferred_element_type=jnp.float32)
        return mixed, total

    mixed, total = lax.fori_loop(0, CACHE // KB, weigh, (mixed, fresh_weights))
    total = jnp.sum(total, axis=1, keepdims=True)
    lane_head = lax.broadcasted_iota(jnp.int32, (NEW, width), 1) // DH
    out = jnp.zeros((NEW, width), jnp.float32)
    for j in range(heads):
        at = slice(j * NEW, (j + 1) * NEW)
        out = jnp.where(lane_head == j, mixed[at] / total[at], out)
    att_ref[...] = out.astype(jnp.bfloat16)


MESH = pl.DeviceIdType.MESH
SIDE = 4
HALF = 3072
PART = 1536
DIRECT = 512
HEADS_HERE = 4
VMEM_LIMIT = 62 * 2**20


def place():
    req, head = lax.axis_index("req"), lax.axis_index("head")
    return req // SIDE, req % SIDE, head // 2, head % 2


def meet(barrier, others):
    for count, target, alone in others:
        @pl.loop(0, count)
        def _(i):
            @pl.when(alone(i))
            def _():
                pl.semaphore_signal(barrier, inc=1, device_id=target(i), device_id_type=MESH)


def ring_units(y, z, x, core, own, slot, part, send_sem, recv_sem):
    def send(colour, dp, ds, half, along, step):
        to = [dp, ds]
        to[along] = (to[along] + step) % SIDE if isinstance(to[along], int) else lax.rem(
            to[along] + step + SIDE, SIDE)
        on_z = (colour == 0) == (along == 0)
        dev_y = y if on_z else lax.rem(y + step + SIDE, SIDE)
        dev_z = lax.rem(z + step + SIDE, SIDE) if on_z else z
        is_own = isinstance(dp, int) and isinstance(ds, int) and dp == 0 and ds == 0
        src = own(colour, half) if is_own else part(slot(colour, dp, ds, 0), colour, half)
        source = (colour, dp, ds)
        dst = part(slot(*source, 0), colour, half) if slot.absolute else part(
            slot(colour, to[0], to[1], 0), colour, half)
        return pltpu.make_async_remote_copy(
            src_ref=src, dst_ref=dst, send_sem=send_sem.at[colour],
            recv_sem=recv_sem.at[colour, half, to[0] * SIDE + to[1]],
            device_id=(dev_y * SIDE + dev_z, 2 * x + core), device_id_type=MESH,
        )

    def arrived(colour, dp, ds, half):
        ref = part(slot(colour, dp, ds, 0), colour, half)
        pltpu.make_async_copy(ref, ref, recv_sem.at[colour, half, dp * SIDE + ds]).wait()

    return send, arrived


FIRST = ((1, 0), (3, 1), (1, 1), (3, 0), (2, 0), (2, 1))


def ring_start(send):
    for along in (0, 1):
        for half in (0, 1):
            for colour in (0, 1):
                for step in (1, -1):
                    send(colour, 0, 0, half, along, step).start()


def ring_spread(send, dp):
    for half in (0, 1):
        for colour in (0, 1):
            for step in (1, -1):
                send(colour, dp, 0, half, 1, step).start()


def ring_first(send, arrived):
    for dp, half in FIRST:
        if (dp, half) == (2, 0):
            ring_spread(send, 1)
        for colour in (0, 1):
            arrived(colour, dp, 0, half)
            if (dp, half) in ((1, 0), (3, 1)):
                send(colour, dp, 0, half, 0, 1 if dp == 1 else -1).start()


def ring_second(send, arrived, i):
    dp = gray(i)
    for ds, half in FIRST:
        if (ds, half) == (2, 0):
            if i < 2:
                ring_spread(send, gray(i + 2))
        for colour in (0, 1):
            arrived(colour, dp, ds, half)
            if (ds, half) in ((1, 0), (3, 1)):
                send(colour, dp, ds, half, 1, 1 if ds == 1 else -1).start()


def gray(i):
    return i + (i // 2) * (1 - 2 * (i % 2))


class Relative:
    absolute = False

    def __call__(self, colour, dp, ds, _):
        return dp * SIDE + ds


class Absolute:
    absolute = True

    def __init__(self, y, z):
        self.y, self.z = y, z

    def __call__(self, colour, dp, ds, _):
        dy, dz = (ds, dp) if colour == 0 else (dp, ds)
        return lax.rem(self.y - dy + SIDE, SIDE) * SIDE + lax.rem(self.z - dz + SIDE, SIDE)


def front_kernel(
    hid_ref, stat_ref, wt_ref, gain_ref, ub_ref, qkv_ref, units_ref,
    xbuf, sbuf, stats, wbuf, nbuf, pbuf, rbuf, bbuf, qsend, qrecv,
    xsend_sem, xrecv_sem, own_sem, side_send, side_recv, stat_send, stat_recv,
    wsend_sem, wrecv_sem, wself_sem, bias_sem, pair_sem, qsend_sem, qrecv_sem,
):
    y, z, x, core = place()
    me = y * SIDE + z
    mate = 1 - core
    own_copies = []
    for colour in (0, 1):
        base = core * HALF + colour * PART

        def take(lane, width, dst, n):
            at = pl.ds(pl.multiple_of(base + lane, 256), width)
            own_copies.append(
                pltpu.make_async_copy(hid_ref.at[:, at], dst, own_sem.at[colour, n]))

        take(0, DIRECT, xbuf.at[colour, 0, :, pl.ds(0, DIRECT)], 0)
        take(DIRECT + 256 * x, 256, xbuf.at[colour, 0, :, pl.ds(DIRECT, 256)], 1)
        for dx in (1, 2, 3):
            plane_at = lax.rem(x - dx + SIDE, SIDE)
            take(DIRECT + 256 * plane_at, 256, sbuf.at[colour, dx - 1, 0], 1 + dx)
    for copy in own_copies:
        copy.start()
    barrier = pltpu.get_barrier_semaphore()

    def plane(i):
        return (i // 2, 2 * x + i % 2)

    def line(i):
        return (me, i)

    meet(barrier, [
        (32, plane, lambda i: i != 2 * me + core),
        (8, line, lambda i: i // 2 != x),
    ])
    for copy in own_copies:
        copy.wait()
    pl.semaphore_wait(barrier, 37)

    goal = y // 2
    kat = pl.ds(pl.multiple_of(((y % 2) * SIDE + z) * 384, 384), 384)

    def part(s, colour, half):
        return xbuf.at[colour, s, pl.ds(64 * half, 64)]

    def own(colour, half):
        return part(0, colour, half)

    send, arrived = ring_units(y, z, x, core, own, Relative(), part, xsend_sem, xrecv_sem)
    ring_start(send)

    def other(i):
        return lax.rem(y + i // SIDE, SIDE) * SIDE + lax.rem(z + i % SIDE, SIDE)

    @pl.loop(1, 16)
    def _(i):
        pltpu.make_async_remote_copy(
            src_ref=stat_ref, dst_ref=stats.at[me], send_sem=stat_send, recv_sem=stat_recv,
            device_id=(other(i), 2 * x + core), device_id_type=MESH,
        ).start()
    pltpu.make_async_copy(stat_ref, stats.at[me], stat_recv).start()
    bias_own = pltpu.make_async_copy(ub_ref, bbuf.at[core], bias_sem.at[0])
    bias_mate = pltpu.make_async_remote_copy(
        src_ref=ub_ref, dst_ref=bbuf.at[core], send_sem=bias_sem.at[1], recv_sem=bias_sem.at[2],
        device_id=(me, 2 * x + mate), device_id_type=MESH,
    )
    bias_own.start()
    bias_mate.start()

    def mate_w():
        return pltpu.make_async_remote_copy(
            src_ref=wt_ref.at[me], dst_ref=wbuf.at[:, core, :, kat],
            send_sem=wself_sem, recv_sem=wrecv_sem,
            device_id=(me, 2 * x + mate), device_id_type=MESH,
        )

    @pl.when(goal != core)
    def _():
        mate_w().start()

    @pl.when(goal == core)
    def _():
        pltpu.make_async_copy(wt_ref.at[me], wbuf.at[:, core, :, kat], wrecv_sem).start()

    def weights_out(first, count):
        @pl.loop(first, first + count)
        def _(i):
            pltpu.make_async_remote_copy(
                src_ref=wt_ref.at[other(i)], dst_ref=wbuf.at[:, core, :, kat],
                send_sem=wsend_sem, recv_sem=wrecv_sem,
                device_id=(other(i), 2 * x + goal), device_id_type=MESH,
            ).start()

    def slots(kind, dp):
        return pl.ds(dp * SIDE, 1) if kind == 0 else pl.ds(dp * SIDE + 1, 3)

    def side_full(colour, kind, dp, step):
        way = (1 - step) // 2
        return pltpu.make_async_remote_copy(
            src_ref=xbuf.at[colour, slots(kind, dp), :, pl.ds(DIRECT, 256)],
            dst_ref=sbuf.at[colour, 2 * way, slots(kind, dp)],
            send_sem=side_send.at[colour], recv_sem=side_recv.at[colour, kind, dp, way],
            device_id=(me, 2 * lax.rem(x + step + SIDE, SIDE) + core), device_id_type=MESH,
        )

    def side_relay(colour, kind, dp, step):
        way = (1 - step) // 2
        rows = pl.ds(64 * way, 64)
        return pltpu.make_async_remote_copy(
            src_ref=sbuf.at[colour, 2 * way, slots(kind, dp), rows],
            dst_ref=sbuf.at[colour, 1, slots(kind, dp), rows],
            send_sem=side_send.at[colour], recv_sem=side_recv.at[colour, kind, dp, 2 + way],
            device_id=(me, 2 * lax.rem(x + step + SIDE, SIDE) + core), device_id_type=MESH,
        )

    def side_wait(colour, kind, dp, n):
        if n < 2:
            ref = sbuf.at[colour, 2 * n, slots(kind, dp)]
        else:
            ref = sbuf.at[colour, 1, slots(kind, dp), pl.ds(64 * (n - 2), 64)]
        pltpu.make_async_copy(ref, ref, side_recv.at[colour, kind, dp, n]).wait()

    def side_out(kind, dp):
        for colour in (0, 1):
            for step in (1, -1):
                side_full(colour, kind, dp, step).start()

    def side_on(kind, dp):
        for colour in (0, 1):
            for way in (0, 1):
                side_wait(colour, kind, dp, way)
                side_relay(colour, kind, dp, 1 - 2 * way).start()

    pbuf[...] = jnp.zeros_like(pbuf)
    ring_first(send, arrived)
    for dp in (1, 3, 2):
        side_out(0, dp)

    def origin(colour, dp, ds):
        dy = colour * dp + (1 - colour) * ds
        dz = colour * ds + (1 - colour) * dp
        return lax.rem(y - dy + SIDE, SIDE) * SIDE + lax.rem(z - dz + SIDE, SIDE)

    def compute(colour, dp):
        @pl.loop(0, SIDE)
        def _(ds):
            s = dp * SIDE + ds
            turned = stats[origin(colour, dp, ds)].T
            center, spread = turned[:, 0:1], turned[:, 1:2]
            rows = pl.ds(pl.multiple_of(ds * NEW, NEW), NEW)
            base = core * HALF + colour * PART

            def norm(raw, lane, width):
                value = (raw.astype(jnp.float32) - center) * spread
                at = pl.ds(pl.multiple_of(base + lane, 256), width)
                to = pl.ds(pl.multiple_of(lane, 256), width)
                for kind in (0, 1):
                    nbuf[kind, rows, to] = (
                        value * gain_ref[2 * kind:2 * kind + 1, at]
                        + gain_ref[2 * kind + 1:2 * kind + 2, at]
                    ).astype(jnp.bfloat16)

            norm(xbuf[colour, s, :, 0:DIRECT], 0, DIRECT)
            norm(xbuf[colour, s, :, DIRECT:DIRECT + 256], DIRECT + 256 * x, 256)
            for dx in (1, 2, 3):
                norm(sbuf[colour, dx - 1, s], DIRECT + 256 * lax.rem(x - dx + SIDE, SIDE), 256)

        for kind in (0, 1):
            left = wbuf[kind, :, :, pl.ds(pl.multiple_of(colour * PART, PART), PART)]
            product = lax.dot_general(
                left.reshape(192, PART), nbuf[kind], NT, preferred_element_type=jnp.float32
            )
            for ds in range(SIDE):
                row = origin(colour, dp, ds)
                pbuf[row, 192 * kind:192 * (kind + 1), :] += product[:, ds * NEW:(ds + 1) * NEW]

    for i in range(SIDE):
        ring_second(send, arrived, i)
        side_out(1, gray(i))

    weights_out(1, 15)
    for dp in (1, 3, 2):
        side_on(0, dp)

    @pl.loop(0, SIDE)
    def _(i):
        side_on(1, gray(i))

    pltpu.make_async_copy(stats, stats, stat_recv).wait()
    pltpu.make_async_copy(wbuf, wbuf, wrecv_sem).wait()

    @pl.loop(0, SIDE)
    def _(i):
        dp = gray(i)
        for colour in (0, 1):
            for n in (2, 3):
                side_wait(colour, 1, dp, n)

            @pl.when(i > 0)
            def _():
                for n in (2, 3):
                    side_wait(colour, 0, dp, n)

        @pl.loop(0, 2)
        def _(colour):
            compute(colour, dp)

    pair = pltpu.make_async_remote_copy(
        src_ref=pbuf.at[pl.ds(8 * mate, 8)], dst_ref=rbuf,
        send_sem=pair_sem.at[0], recv_sem=pair_sem.at[1],
        device_id=(me, 2 * x + mate), device_id_type=MESH,
    )
    pair.start()
    bias_own.wait()
    bias_mate.wait()
    pair.wait_recv()
    mine = pl.ds(pl.multiple_of(me * 72, 8), 72)

    @pl.loop(0, 8)
    def _(q):
        row = 8 * core + q
        total = pbuf[row] + rbuf[q]
        for h in (0, 1):
            qsend[2 * q + h] = total[96 * h:96 * h + 72]
            remote = pltpu.make_async_remote_copy(
                src_ref=qsend.at[2 * q + h], dst_ref=qrecv.at[mine],
                send_sem=qsend_sem, recv_sem=qrecv_sem,
                device_id=(row, 2 * x + h), device_id_type=MESH,
            )
            away = jnp.logical_or(row != me, core != h)

            @pl.when(away)
            def _():
                remote.start()

            @pl.when(jnp.logical_not(away))
            def _():
                pltpu.make_async_copy(qsend.at[2 * q + h], qrecv.at[mine], qrecv_sem).start()
        at = pl.ds(pl.multiple_of(q * NEW, NEW), NEW)
        for h in (0, 1):
            u = total[192 + 96 * h:288 + 96 * h] + bbuf[h]
            inner = 0.7978845608028654 * (u + 0.044715 * (u * u * u))
            units_ref[h, :, at] = (0.5 * u * (1.0 + jnp.tanh(inner))).astype(jnp.bfloat16)

    pltpu.make_async_copy(qrecv, qrecv, qrecv_sem).wait()
    qkv_ref[...] = qrecv[...]
    pair.wait_send()

    @pl.when(goal == core)
    def _():
        some = qsend.at[pl.ds(0, 15)]
        pltpu.make_async_copy(some, some, qsend_sem).wait()

    @pl.when(goal != core)
    def _():
        pltpu.make_async_copy(qsend, qsend, qsend_sem).wait()
        mate_w().wait_send()

    some = wt_ref.at[pl.ds(0, 15)]
    pltpu.make_async_copy(some, some, wsend_sem).wait()
    for colour in (0, 1):
        some = xbuf.at[colour, pl.ds(1, 15)]
        pltpu.make_async_copy(some, some, xsend_sem.at[colour]).wait()
        some = sbuf.at[colour, :, pl.ds(1, 15)]
        pltpu.make_async_copy(some, some, side_send.at[colour]).wait()
    some = stats.at[pl.ds(0, 15)]
    pltpu.make_async_copy(some, some, stat_send).wait()


def front(hidden, gains, qkv_weight, up_weight, up_bias):
    req = lax.axis_index("req")
    widened = hidden.astype(jnp.float32)
    center = jnp.mean(widened, axis=-1)
    spread = lax.rsqrt(jnp.mean(jnp.square(widened - center[:, None]), axis=-1) + 1e-05)
    stat = jnp.pad(jnp.stack([center, spread]), ((0, 6), (0, 0)))
    depth = qkv_weight.shape[0]
    wq = jnp.pad(qkv_weight.T.reshape(16, 72, depth), ((0, 0), (0, 24), (0, 0)))
    wt = jnp.stack([wq, up_weight.T.reshape(16, 96, depth)], axis=1)
    gain = jnp.stack(gains)
    bias = lax.dynamic_slice_in_dim(up_bias, req * 96, 96, 0)
    bias = jnp.broadcast_to(bias[:, None], (96, 128))
    vmem = pl.BlockSpec(memory_space=pltpu.VMEM)
    hbm = pl.BlockSpec(memory_space=pl.ANY)
    dma = pltpu.SemaphoreType.DMA
    return pl.pallas_call(
        front_kernel,
        out_shape=(
            jax.ShapeDtypeStruct((1152, NEW), jnp.float32),
            jax.ShapeDtypeStruct((2, 96, 1024), jnp.bfloat16),
        ),
        in_specs=[hbm, hbm, hbm, vmem, hbm],
        out_specs=(vmem, vmem),
        scratch_shapes=[
            pltpu.VMEM((2, 16, NEW, DIRECT + 256), jnp.bfloat16),
            pltpu.VMEM((2, 3, 16, NEW, 256), jnp.bfloat16),
            pltpu.VMEM((16, 8, NEW), jnp.float32),
            pltpu.VMEM((2, 2, 96, HALF), jnp.bfloat16),
            pltpu.VMEM((2, 512, PART), jnp.bfloat16),
            pltpu.VMEM((16, 384, NEW), jnp.float32),
            pltpu.VMEM((8, 384, NEW), jnp.float32),
            pltpu.VMEM((2, 96, NEW), jnp.float32),
            pltpu.VMEM((16, 72, NEW), jnp.float32),
            pltpu.VMEM((1152, NEW), jnp.float32),
            dma((2,)), dma((2, 2, 16)), dma((2, 5)), dma((2,)), dma((2, 2, 4, 4)), dma, dma,
            dma, dma, dma, dma((3,)), dma((2,)), dma, dma,
        ],
        compiler_params=pltpu.CompilerParams(
            collective_id=0, has_side_effects=True, vmem_limit_bytes=VMEM_LIMIT
        ),
        name="front",
    )(hidden, stat, wt, gain, bias)


def back_kernel(
    len_ref, units_ref, qkv_ref, qbias_ref, cos_ref, sin_ref, k_hbm, v_hbm,
    wd_ref, wo_ref, rest_ref, bias_ref, out_ref, nk_ref, nv_ref,
    ubuf, aring, amate, dbuf, obuf, dturn, total, tsend, rsum, share, rest, fout,
    kbuf, vbuf, sbuf, qexp, vkeep, att_ref, ksem, vsem,
    usend_sem, urecv_sem, own_sem, asend_sem, arecv_sem, amate_sem, w_sem,
    hsend_sem, hrecv_sem, rsend_sem, rrecv_sem, fsend_sem, frecv_sem, gsend_sem, grecv_sem,
):
    for hbm, buf, sem in ((k_hbm, kbuf, ksem), (v_hbm, vbuf, vsem)):
        for n in range(CACHE // KB):
            fetch(n, hbm, buf, sem).start()
    y, z, x, core = place()
    me = y * SIDE + z
    mate = 1 - core
    goal = y // 2
    barrier = pltpu.get_barrier_semaphore()

    def plane(i):
        return (i // 2, 2 * x + i % 2)

    def line(i):
        return (me, i)

    meet(barrier, [
        (32, plane, lambda i: i != 2 * me + core),
        (8, line, lambda i: i // 2 != x),
    ])
    pl.semaphore_wait(barrier, 37)

    def apart(s, colour, half):
        return aring.at[s, pl.ds(32 * (2 * colour + half), 32)]

    def aown(colour, half):
        return att_ref.at[pl.ds(32 * (2 * colour + half), 32)]

    asend, aarrived = ring_units(y, z, x, core, aown, Absolute(y, z), apart, asend_sem, arecv_sem)

    def lanes(colour, half):
        return pl.ds((2 * colour + half) * 256, 256)

    def part(s, colour, half):
        return ubuf.at[:, s, :, lanes(colour, half)]

    def own(colour, half):
        return units_ref.at[:, :, lanes(colour, half)]

    send, arrived = ring_units(y, z, x, core, own, Absolute(y, z), part, usend_sem, urecv_sem)
    ring_start(send)
    copies = [pltpu.make_async_copy(units_ref, ubuf.at[:, me], own_sem.at[0])]
    for n, (src, dst) in enumerate(((wd_ref, dbuf), (wo_ref, obuf))):
        copies.append(pltpu.make_async_copy(src, dst.at[core], w_sem.at[3 * n]))
        copies.append(pltpu.make_async_remote_copy(
            src_ref=src, dst_ref=dst.at[core], send_sem=w_sem.at[3 * n + 1],
            recv_sem=w_sem.at[3 * n + 2], device_id=(me, 2 * x + mate), device_id_type=MESH,
        ))
    for copy in copies:
        copy.start()
    slot = me % 8

    @pl.when(goal == core)
    def _():
        @pl.loop(1, 16)
        def _(i):
            row = lax.rem(y + i // SIDE, SIDE) * SIDE + lax.rem(z + i % SIDE, SIDE)
            pltpu.make_async_remote_copy(
                src_ref=rest_ref.at[row], dst_ref=rest.at[slot],
                send_sem=hsend_sem, recv_sem=hrecv_sem,
                device_id=(row, 2 * x + core), device_id_type=MESH,
            ).start()
        pltpu.make_async_copy(rest_ref.at[me], rest.at[slot], hrecv_sem).start()

    heads = HEADS_HERE
    keep = (vkeep, qexp, sbuf)

    def key_block(n, at):
        fetch(n, k_hbm, kbuf, ksem).wait()
        return kbuf[at, :]

    def value_block(n, at):
        fetch(n, v_hbm, vbuf, vsem).wait()
        return vbuf[at, :]

    top = attention_scores(
        heads, len_ref[0], qkv_ref, qbias_ref, cos_ref, sin_ref, nk_ref, nv_ref, keep, key_block)
    ring_first(send, arrived)
    attention_mix(heads, top, keep, att_ref, value_block)
    att_own = pltpu.make_async_copy(att_ref, aring.at[me], own_sem.at[1])
    att_own.start()
    ring_start(asend)
    for copy in copies:
        copy.wait()

    def turn(first, count):
        @pl.loop(first, first + count)
        def _(n):
            h, at = n // 12, pl.ds(pl.multiple_of((n % 12) * 128, 128), 128)
            dturn[h, :, at] = dbuf[h, at, :].T

    ring_second(send, arrived, 0)
    turn(0, 12)
    ring_first(asend, aarrived)
    ring_second(send, arrived, 1)
    turn(12, 12)
    ring_second(asend, aarrived, 0)
    ring_second(asend, aarrived, 1)
    ring_second(send, arrived, 2)
    ring_second(asend, aarrived, 2)
    ring_second(asend, aarrived, 3)
    att_own.wait()
    pair = pltpu.make_async_remote_copy(
        src_ref=aring.at[pl.ds(8 * mate, 8)], dst_ref=amate,
        send_sem=amate_sem.at[0], recv_sem=amate_sem.at[1],
        device_id=(me, 2 * x + mate), device_id_type=MESH,
    )
    pair.start()
    ring_second(send, arrived, 3)
    pair.wait_recv()

    def rcopy(q, step):
        to = lax.rem(x + step, SIDE)
        return pltpu.make_async_remote_copy(
            src_ref=tsend.at[q, pl.ds(pl.multiple_of(32 * to, 32), 32)],
            dst_ref=rsum.at[step - 1, q],
            send_sem=rsend_sem.at[step - 1], recv_sem=rrecv_sem.at[step - 1],
            device_id=(me, 2 * to + core), device_id_type=MESH,
        )

    @pl.loop(0, 4)
    def _(p):
        at = pl.ds(pl.multiple_of(2 * p * NEW, 2 * NEW), 2 * NEW)
        turned = jnp.zeros((384, 2 * NEW), jnp.float32)
        for h in (0, 1):
            turned += jnp.dot(
                dturn[h], ubuf[h, :, :, at].reshape(PART, 2 * NEW),
                preferred_element_type=jnp.float32,
            )
        for n in (0, 1):
            q = 2 * p + n
            value = turned[:, n * NEW:(n + 1) * NEW].T
            value += jnp.dot(
                aring[8 * core + q], obuf[core], preferred_element_type=jnp.float32
            ) + jnp.dot(amate[q], obuf[mate], preferred_element_type=jnp.float32)
            total[q] = value
            tsend[q] = value.astype(jnp.bfloat16)
        for n in (0, 1):
            for step in (2, 1, 3):
                rcopy(2 * p + n, step).start()

    pltpu.make_async_copy(rest, rest, hrecv_sem).wait()
    for step in (1, 3, 2):
        some = rsum.at[step - 1]
        pltpu.make_async_copy(some, some, rrecv_sem.at[step - 1]).wait()
    rows = pl.ds(pl.multiple_of(32 * x, 32), 32)
    mine = pl.ds(pl.multiple_of(384 * me, 384), 384)

    @pl.loop(0, 8)
    def _(q):
        value = total[q, rows, :] + rsum[0, q].astype(jnp.float32)
        value += rsum[1, q].astype(jnp.float32) + rsum[2, q].astype(jnp.float32)
        share[q] = (rest[q].astype(jnp.float32) + (value + bias_ref[...])).astype(jnp.bfloat16)
        row = 8 * core + q

        @pl.when(row != me)
        def _():
            pltpu.make_async_remote_copy(
                src_ref=share.at[q], dst_ref=fout.at[rows, mine],
                send_sem=fsend_sem, recv_sem=frecv_sem,
                device_id=(row, 2 * x + goal), device_id_type=MESH,
            ).start()

        @pl.when(row == me)
        def _():
            pltpu.make_async_copy(share.at[q], fout.at[rows, mine], frecv_sem).start()

    def piece(owner, c):
        return fout.at[
            pl.ds(pl.multiple_of(32 * owner, 32), 32), pl.ds(pl.multiple_of(c * HALF, HALF), HALF)
        ]

    def gcopy(step):
        to = lax.rem(x + step + SIDE, SIDE)
        way = (1 - step) // 2
        return pltpu.make_async_remote_copy(
            src_ref=piece(x, core), dst_ref=piece(x, core), send_sem=gsend_sem.at[0, way],
            recv_sem=grecv_sem.at[0, way], device_id=(me, 2 * to + core), device_id_type=MESH,
        )

    def strip(owner, way):
        return fout.at[
            pl.ds(pl.multiple_of(32 * owner + 16 * way, 16), 16),
            pl.ds(pl.multiple_of(core * HALF, HALF), HALF),
        ]

    def grelay(step):
        to = lax.rem(x + step + SIDE, SIDE)
        owner = lax.rem(x - step + SIDE, SIDE)
        way = (1 - step) // 2
        return pltpu.make_async_remote_copy(
            src_ref=strip(owner, way), dst_ref=strip(owner, way), send_sem=gsend_sem.at[0, 2 + way],
            recv_sem=grecv_sem.at[0, 2 + way], device_id=(me, 2 * to + core), device_id_type=MESH,
        )

    def pass_on(step):
        owner = lax.rem(x - step + SIDE, SIDE)
        return pltpu.make_async_remote_copy(
            src_ref=piece(owner, core), dst_ref=piece(owner, core), send_sem=gsend_sem.at[1, step],
            recv_sem=grecv_sem.at[1, step], device_id=(me, 2 * x + mate), device_id_type=MESH,
        )

    def landed(kind, n, ref):
        pltpu.make_async_copy(ref, ref, grecv_sem.at[kind, n]).wait()

    def owner_at(step):
        return lax.rem(x - step + SIDE, SIDE)

    pltpu.make_async_copy(piece(x, core), piece(x, core), frecv_sem).wait()
    for step in (1, -1):
        gcopy(step).start()
    pass_on(0).start()
    for step in (1, -1):
        landed(0, (1 - step) // 2, piece(owner_at(step), core))
        grelay(step).start()
        pass_on(step % SIDE).start()
    for way in (0, 1):
        landed(0, 2 + way, strip(owner_at(2), way))
    pass_on(2).start()
    for step in (0, 1, 3, 2):
        landed(1, step, piece(owner_at(step), mate))
    out_ref[...] = fout[...]

    for step in (1, -1):
        gcopy(step).wait_send()
        grelay(step).wait_send()
    for step in (1, 2, 3):
        some = rsum.at[step - 1]
        pltpu.make_async_copy(some, some, rsend_sem.at[step - 1]).wait()
    for step in range(4):
        pass_on(step).wait_send()
    pair.wait_send()

    @pl.when(goal == core)
    def _():
        some = share.at[pl.ds(0, 7)]
        pltpu.make_async_copy(some, some, fsend_sem).wait()
        some = rest_ref.at[pl.ds(0, 15)]
        pltpu.make_async_copy(some, some, hsend_sem).wait()

    @pl.when(goal != core)
    def _():
        pltpu.make_async_copy(share, share, fsend_sem).wait()

    for colour in (0, 1):
        some = ubuf.at[:, pl.ds(0, 15), :, pl.ds(512 * colour, 512)]
        pltpu.make_async_copy(some, some, usend_sem.at[colour]).wait()
        some = aring.at[pl.ds(0, 15), pl.ds(64 * colour, 64)]
        pltpu.make_async_copy(some, some, asend_sem.at[colour]).wait()


def back(units, qkv, qkv_bias, length, keys_old, values_old, hidden, out_weight, down_weight, bias_total):
    cosine, sine = rotation_tables(length[0])
    req, x = lax.axis_index("req"), lax.axis_index("head") // 2
    rest = lax.dynamic_slice_in_dim(hidden, 32 * x, 32, 0)
    rest = rest.reshape(32, 16, 384).transpose(1, 0, 2)
    bias = lax.dynamic_slice_in_dim(bias_total, req * 384, 384, 0)[None, :]
    vmem = pl.BlockSpec(memory_space=pltpu.VMEM)
    hbm = pl.BlockSpec(memory_space=pl.ANY)
    dma = pltpu.SemaphoreType.DMA
    return pl.pallas_call(
        back_kernel,
        out_shape=(
            jax.ShapeDtypeStruct((NEW, 2 * HALF), jnp.bfloat16),
            jax.ShapeDtypeStruct((NEW, 384), jnp.bfloat16),
            jax.ShapeDtypeStruct((NEW, 384), jnp.bfloat16),
        ),
        in_specs=[
            pl.BlockSpec(memory_space=pltpu.SMEM), hbm, vmem, vmem, vmem, vmem, hbm, hbm,
            hbm, hbm, hbm, vmem,
        ],
        out_specs=(vmem, vmem, vmem),
        scratch_shapes=[
            pltpu.VMEM((2, 16, 96, 1024), jnp.bfloat16),
            pltpu.VMEM((16, NEW, 384), jnp.bfloat16),
            pltpu.VMEM((8, NEW, 384), jnp.bfloat16),
            pltpu.VMEM((2, PART, 384), jnp.bfloat16),
            pltpu.VMEM((2, 384, 384), jnp.bfloat16),
            pltpu.VMEM((2, 384, PART), jnp.bfloat16),
            pltpu.VMEM((8, NEW, 384), jnp.float32),
            pltpu.VMEM((8, NEW, 384), jnp.bfloat16),
            pltpu.VMEM((3, 8, 32, 384), jnp.bfloat16),
            pltpu.VMEM((8, 32, 384), jnp.bfloat16),
            pltpu.VMEM((8, 32, 384), jnp.bfloat16),
            pltpu.VMEM((NEW, 2 * HALF), jnp.bfloat16),
            pltpu.VMEM((CACHE, 384), jnp.bfloat16),
            pltpu.VMEM((CACHE, 384), jnp.bfloat16),
            pltpu.VMEM((HEADS_HERE * NEW, CACHE + NEW), jnp.float32),
            pltpu.VMEM((HEADS_HERE * NEW, 384), jnp.bfloat16),
            pltpu.VMEM((NEW, 384), jnp.bfloat16),
            pltpu.VMEM((NEW, 384), jnp.bfloat16),
            dma((CACHE // KB,)), dma((CACHE // KB,)),
            dma((2,)), dma((2, 2, 16)), dma((2,)), dma((2,)), dma((2, 2, 16)), dma((2,)), dma((6,)),
            dma, dma, dma((3,)), dma((3,)), dma, dma, dma((2, 4)), dma((2, 4)),
        ],
        compiler_params=pltpu.CompilerParams(
            collective_id=1, has_side_effects=True, vmem_limit_bytes=VMEM_LIMIT
        ),
        name="back",
    )(length, units, qkv, qkv_bias[:, None], cosine, sine, keys_old, values_old,
      down_weight, out_weight, rest, bias)


def body(
    hidden,
    attn_norm_gain,
    attn_norm_bias,
    mlp_norm_gain,
    mlp_norm_bias,
    qkv_weight,
    qkv_bias,
    out_weight,
    out_bias,
    up_weight,
    up_bias,
    down_weight,
    down_bias,
    cache_keys,
    cache_values,
    cached_len,
):
    gains = (attn_norm_gain, attn_norm_bias, mlp_norm_gain, mlp_norm_bias)
    qkv, units = front(hidden, gains, qkv_weight, up_weight, up_bias)
    result, key_rows, value_rows = back(
        units, qkv, qkv_bias, cached_len, cache_keys[0], cache_values[0],
        hidden, out_weight, down_weight, out_bias + down_bias,
    )
    return (result, key_rows[None], value_rows[None])


def solution(mesh):
    return jax.shard_map(
        body,
        mesh=mesh,
        in_specs=(
            P("req", None),
            P(),
            P(),
            P(),
            P(),
            P("req", "head"),
            P("head"),
            P("head", "req"),
            P(),
            P("req", "head"),
            P("head"),
            P("head", "req"),
            P(),
            P("req", None, "head"),
            P("req", None, "head"),
            P("req"),
        ),
        out_specs=(P("req", None), P("req", None, "head"), P("req", None, "head")),
        check_vma=False,
    )
```

```python
import functools
import math

import jax
import jax.numpy as jnp
from jax import lax
from jax.experimental import pallas as pl
from jax.experimental.pallas import tpu as pltpu
from jax.sharding import PartitionSpec as P

DH = 96
ROT = 24
NEW = 128
CACHE = 4096
KB = 512
NT = (((1,), (1,)), ((), ()))


def rotation_tables(length):
    position = length.astype(jnp.float32) + jnp.arange(NEW, dtype=jnp.float32)
    halfway = ROT // 2
    exponent = jnp.arange(halfway, dtype=jnp.float32) * (2.0 / ROT)
    frequency = jnp.power(10000.0, -exponent)
    angle = position[None, :] * frequency[:, None]
    cosine, sine = jnp.cos(angle), jnp.sin(angle)
    return jnp.concatenate([cosine, cosine], 0), jnp.concatenate([-sine, sine], 0)


def fetch(n, hbm, buf, sem):
    rows = pl.ds(pl.multiple_of(n * KB, KB), KB)
    return pltpu.make_async_copy(hbm.at[rows], buf.at[rows], sem.at[n])


def attention_scores(heads, length, qkv_ref, bias_ref, cos_ref, sin_ref, nk_ref, nv_ref, keep, key_block):
    scale = 1.0 / math.sqrt(DH)
    width = heads * DH
    vkeep, qexp, sbuf = keep
    cosine, sine = cos_ref[...], sin_ref[...]

    def turned(rows):
        low = rows[:ROT]
        swapped = jnp.concatenate([low[ROT // 2:], low[: ROT // 2]], axis=0)
        return jnp.concatenate([low * cosine + swapped * sine, rows[ROT:]], axis=0)

    bias = jnp.broadcast_to(bias_ref[...], (8, 3 * width)).T

    def block(j, part):
        first = (3 * j + part) * DH
        return qkv_ref[pl.ds(first, DH), :] + bias[first:first + DH, 0:1]

    queries = jnp.concatenate([turned(block(j, 0)) for j in range(heads)], 0).T.astype(jnp.bfloat16)
    keys = jnp.concatenate([turned(block(j, 1)) for j in range(heads)], 0).T.astype(jnp.bfloat16)
    values = jnp.concatenate([block(j, 2) for j in range(heads)], 0).T.astype(jnp.bfloat16)
    nk_ref[...] = keys
    nv_ref[...] = values
    vkeep[...] = values
    lane_head = lax.broadcasted_iota(jnp.int32, (NEW, width), 1) // DH
    for j in range(heads):
        qexp[pl.ds(j * NEW, NEW), :] = jnp.where(lane_head == j, queries, jnp.zeros_like(queries))
    rows = heads * NEW
    fresh = lax.dot_general(qexp[...], keys, NT, preferred_element_type=jnp.float32) * scale
    row_at = lax.broadcasted_iota(jnp.int32, (rows, NEW), 0) % NEW
    col_at = lax.broadcasted_iota(jnp.int32, (rows, NEW), 1)
    fresh = jnp.where(col_at <= row_at, fresh, -1e30)
    sbuf[:, CACHE:] = fresh

    def score(n, top):
        at = pl.ds(pl.multiple_of(n * KB, KB), KB)
        part = lax.dot_general(
            qexp[...], key_block(n, at), NT, preferred_element_type=jnp.float32) * scale
        col = lax.broadcasted_iota(jnp.int32, (rows, KB), 1) + n * KB
        part = jnp.where(col < length, part, -1e30)
        sbuf[:, at] = part
        for t in range(KB // NEW):
            top = jnp.maximum(top, part[:, t * NEW:(t + 1) * NEW])
        return top

    return lax.fori_loop(0, CACHE // KB, score, fresh)


def attention_mix(heads, top, keep, att_ref, value_block):
    width = heads * DH
    vkeep, _, sbuf = keep
    highest = jnp.max(top, axis=1, keepdims=True)
    fresh_weights = jnp.exp(sbuf[:, CACHE:] - highest)
    mixed = jnp.dot(
        fresh_weights.astype(jnp.bfloat16), vkeep[...], preferred_element_type=jnp.float32)

    def weigh(n, carry):
        mixed, total = carry
        at = pl.ds(pl.multiple_of(n * KB, KB), KB)
        weights = jnp.exp(sbuf[:, at] - highest)
        for t in range(KB // NEW):
            total = total + weights[:, t * NEW:(t + 1) * NEW]
        mixed = mixed + jnp.dot(
            weights.astype(jnp.bfloat16), value_block(n, at), preferred_element_type=jnp.float32)
        return mixed, total

    mixed, total = lax.fori_loop(0, CACHE // KB, weigh, (mixed, fresh_weights))
    total = jnp.sum(total, axis=1, keepdims=True)
    lane_head = lax.broadcasted_iota(jnp.int32, (NEW, width), 1) // DH
    out = jnp.zeros((NEW, width), jnp.float32)
    for j in range(heads):
        at = slice(j * NEW, (j + 1) * NEW)
        out = jnp.where(lane_head == j, mixed[at] / total[at], out)
    att_ref[...] = out.astype(jnp.bfloat16)


MESH = pl.DeviceIdType.MESH
SIDE = 4
HALF = 3072
PART = 1536
DIRECT = 512
HEADS_HERE = 4
VMEM_LIMIT = 62 * 2**20


def place():
    req, head = lax.axis_index("req"), lax.axis_index("head")
    return req // SIDE, req % SIDE, head // 2, head % 2


def meet(barrier, others):
    for count, target, alone in others:
        @pl.loop(0, count)
        def _(i):
            @pl.when(alone(i))
            def _():
                pl.semaphore_signal(barrier, inc=1, device_id=target(i), device_id_type=MESH)


def ring_units(y, z, x, core, own, slot, part, send_sem, recv_sem):
    def send(colour, dp, ds, half, along, step):
        to = [dp, ds]
        to[along] = (to[along] + step) % SIDE if isinstance(to[along], int) else lax.rem(
            to[along] + step + SIDE, SIDE)
        on_z = (colour == 0) == (along == 0)
        dev_y = y if on_z else lax.rem(y + step + SIDE, SIDE)
        dev_z = lax.rem(z + step + SIDE, SIDE) if on_z else z
        is_own = isinstance(dp, int) and isinstance(ds, int) and dp == 0 and ds == 0
        src = own(colour, half) if is_own else part(slot(colour, dp, ds, 0), colour, half)
        source = (colour, dp, ds)
        dst = part(slot(*source, 0), colour, half) if slot.absolute else part(
            slot(colour, to[0], to[1], 0), colour, half)
        return pltpu.make_async_remote_copy(
            src_ref=src, dst_ref=dst, send_sem=send_sem.at[colour],
            recv_sem=recv_sem.at[colour, half, to[0] * SIDE + to[1]],
            device_id=(dev_y * SIDE + dev_z, 2 * x + core), device_id_type=MESH,
        )

    def arrived(colour, dp, ds, half):
        ref = part(slot(colour, dp, ds, 0), colour, half)
        pltpu.make_async_copy(ref, ref, recv_sem.at[colour, half, dp * SIDE + ds]).wait()

    return send, arrived


FIRST = ((1, 0), (3, 1), (1, 1), (3, 0), (2, 0), (2, 1))


def ring_start(send):
    for along in (0, 1):
        for half in (0, 1):
            for colour in (0, 1):
                for step in (1, -1):
                    send(colour, 0, 0, half, along, step).start()


def ring_spread(send, dp):
    for half in (0, 1):
        for colour in (0, 1):
            for step in (1, -1):
                send(colour, dp, 0, half, 1, step).start()


def ring_first(send, arrived, eager=False):
    for dp, half in FIRST:
        if (dp, half) == (2, 0) and not eager:
            ring_spread(send, 1)
        for colour in (0, 1):
            arrived(colour, dp, 0, half)
            if (dp, half) in ((1, 0), (3, 1)):
                send(colour, dp, 0, half, 0, 1 if dp == 1 else -1).start()
            if eager:
                for step in (1, -1):
                    send(colour, dp, 0, half, 1, step).start()


def ring_second(send, arrived, i, eager=False):
    dp = gray(i)
    for ds, half in FIRST:
        if (ds, half) == (2, 0) and not eager:
            if i < 2:
                ring_spread(send, gray(i + 2))
        for colour in (0, 1):
            arrived(colour, dp, ds, half)
            if (ds, half) in ((1, 0), (3, 1)):
                send(colour, dp, ds, half, 1, 1 if ds == 1 else -1).start()


def gray(i):
    return i + (i // 2) * (1 - 2 * (i % 2))


class Relative:
    absolute = False

    def __call__(self, colour, dp, ds, _):
        return dp * SIDE + ds


class Absolute:
    absolute = True

    def __init__(self, y, z):
        self.y, self.z = y, z

    def __call__(self, colour, dp, ds, _):
        dy, dz = (ds, dp) if colour == 0 else (dp, ds)
        return lax.rem(self.y - dy + SIDE, SIDE) * SIDE + lax.rem(self.z - dz + SIDE, SIDE)


def front_kernel(
    hid_ref, stat_ref, wt_ref, gain_ref, ub_ref, qkv_ref, units_ref,
    xbuf, sbuf, stats, wbuf, nbuf, pbuf, rbuf, bbuf, qsend, qrecv,
    xsend_sem, xrecv_sem, own_sem, side_send, side_recv, stat_send, stat_recv,
    wsend_sem, wrecv_sem, wself_sem, bias_sem, pair_sem, qsend_sem, qrecv_sem,
):
    y, z, x, core = place()
    me = y * SIDE + z
    mate = 1 - core
    own_copies = []
    for colour in (0, 1):
        base = core * HALF + colour * PART

        def take(lane, width, dst, n):
            at = pl.ds(pl.multiple_of(base + lane, 256), width)
            own_copies.append(
                pltpu.make_async_copy(hid_ref.at[:, at], dst, own_sem.at[colour, n]))

        take(0, DIRECT, xbuf.at[colour, 0, :, pl.ds(0, DIRECT)], 0)
        take(DIRECT + 256 * x, 256, xbuf.at[colour, 0, :, pl.ds(DIRECT, 256)], 1)
        for dx in (1, 2, 3):
            plane_at = lax.rem(x - dx + SIDE, SIDE)
            take(DIRECT + 256 * plane_at, 256, sbuf.at[colour, dx - 1, 0], 1 + dx)
    for copy in own_copies:
        copy.start()
    barrier = pltpu.get_barrier_semaphore()

    def plane(i):
        return (i // 2, 2 * x + i % 2)

    def line(i):
        return (me, i)

    meet(barrier, [
        (32, plane, lambda i: i != 2 * me + core),
        (8, line, lambda i: i // 2 != x),
    ])
    for copy in own_copies:
        copy.wait()
    pl.semaphore_wait(barrier, 37)

    goal = y // 2
    kat = pl.ds(pl.multiple_of(((y % 2) * SIDE + z) * 384, 384), 384)

    def part(s, colour, half):
        return xbuf.at[colour, s, pl.ds(64 * half, 64)]

    def own(colour, half):
        return part(0, colour, half)

    send, arrived = ring_units(y, z, x, core, own, Relative(), part, xsend_sem, xrecv_sem)
    ring_start(send)

    def other(i):
        return lax.rem(y + i // SIDE, SIDE) * SIDE + lax.rem(z + i % SIDE, SIDE)

    @pl.loop(1, 16)
    def _(i):
        pltpu.make_async_remote_copy(
            src_ref=stat_ref, dst_ref=stats.at[me], send_sem=stat_send, recv_sem=stat_recv,
            device_id=(other(i), 2 * x + core), device_id_type=MESH,
        ).start()
    pltpu.make_async_copy(stat_ref, stats.at[me], stat_recv).start()
    bias_own = pltpu.make_async_copy(ub_ref, bbuf.at[core], bias_sem.at[0])
    bias_mate = pltpu.make_async_remote_copy(
        src_ref=ub_ref, dst_ref=bbuf.at[core], send_sem=bias_sem.at[1], recv_sem=bias_sem.at[2],
        device_id=(me, 2 * x + mate), device_id_type=MESH,
    )
    bias_own.start()
    bias_mate.start()

    def mate_w():
        return pltpu.make_async_remote_copy(
            src_ref=wt_ref.at[me], dst_ref=wbuf.at[:, core, :, kat],
            send_sem=wself_sem, recv_sem=wrecv_sem,
            device_id=(me, 2 * x + mate), device_id_type=MESH,
        )

    @pl.when(goal != core)
    def _():
        mate_w().start()

    @pl.when(goal == core)
    def _():
        pltpu.make_async_copy(wt_ref.at[me], wbuf.at[:, core, :, kat], wrecv_sem).start()

    def weights_out(first, count):
        @pl.loop(first, first + count)
        def _(i):
            pltpu.make_async_remote_copy(
                src_ref=wt_ref.at[other(i)], dst_ref=wbuf.at[:, core, :, kat],
                send_sem=wsend_sem, recv_sem=wrecv_sem,
                device_id=(other(i), 2 * x + goal), device_id_type=MESH,
            ).start()

    def slots(kind, dp):
        return pl.ds(dp * SIDE, 1) if kind == 0 else pl.ds(dp * SIDE + 1, 3)

    def side_full(colour, kind, dp, step):
        way = (1 - step) // 2
        return pltpu.make_async_remote_copy(
            src_ref=xbuf.at[colour, slots(kind, dp), :, pl.ds(DIRECT, 256)],
            dst_ref=sbuf.at[colour, 2 * way, slots(kind, dp)],
            send_sem=side_send.at[colour], recv_sem=side_recv.at[colour, kind, dp, way],
            device_id=(me, 2 * lax.rem(x + step + SIDE, SIDE) + core), device_id_type=MESH,
        )

    def side_relay(colour, kind, dp, step):
        way = (1 - step) // 2
        rows = pl.ds(64 * way, 64)
        return pltpu.make_async_remote_copy(
            src_ref=sbuf.at[colour, 2 * way, slots(kind, dp), rows],
            dst_ref=sbuf.at[colour, 1, slots(kind, dp), rows],
            send_sem=side_send.at[colour], recv_sem=side_recv.at[colour, kind, dp, 2 + way],
            device_id=(me, 2 * lax.rem(x + step + SIDE, SIDE) + core), device_id_type=MESH,
        )

    def side_wait(colour, kind, dp, n):
        if n < 2:
            ref = sbuf.at[colour, 2 * n, slots(kind, dp)]
        else:
            ref = sbuf.at[colour, 1, slots(kind, dp), pl.ds(64 * (n - 2), 64)]
        pltpu.make_async_copy(ref, ref, side_recv.at[colour, kind, dp, n]).wait()

    def side_out(kind, dp):
        for colour in (0, 1):
            for step in (1, -1):
                side_full(colour, kind, dp, step).start()

    def side_on(kind, dp):
        for colour in (0, 1):
            for way in (0, 1):
                side_wait(colour, kind, dp, way)
                side_relay(colour, kind, dp, 1 - 2 * way).start()

    pbuf[...] = jnp.zeros_like(pbuf)
    ring_first(send, arrived)
    for dp in (1, 3, 2):
        side_out(0, dp)

    def origin(colour, dp, ds):
        dy = colour * dp + (1 - colour) * ds
        dz = colour * ds + (1 - colour) * dp
        return lax.rem(y - dy + SIDE, SIDE) * SIDE + lax.rem(z - dz + SIDE, SIDE)

    def norm(colour, dp, pieces):
        base = core * HALF + colour * PART

        @pl.loop(0, SIDE)
        def _(ds):
            turned = stats[origin(colour, dp, ds)].T
            center, spread = turned[:, 0:1], turned[:, 1:2]
            rows = pl.ds(pl.multiple_of(ds * NEW, NEW), NEW)
            for raw, lane, width in pieces(colour, dp * SIDE + ds):
                value = (raw.astype(jnp.float32) - center) * spread
                at = pl.ds(pl.multiple_of(base + lane, 256), width)
                to = pl.ds(pl.multiple_of(lane, 256), width)
                for kind in (0, 1):
                    nbuf[colour, dp, kind, rows, to] = (
                        value * gain_ref[2 * kind:2 * kind + 1, at]
                        + gain_ref[2 * kind + 1:2 * kind + 2, at]
                    ).astype(jnp.bfloat16)

    def side_lane(dx):
        return DIRECT + 256 * lax.rem(x - dx + SIDE, SIDE)

    def early(colour, s):
        yield xbuf[colour, s, :, 0:DIRECT], 0, DIRECT
        yield xbuf[colour, s, :, DIRECT:DIRECT + 256], DIRECT + 256 * x, 256
        for dx in (1, 3):
            yield sbuf[colour, dx - 1, s], side_lane(dx), 256

    def late(colour, s):
        yield sbuf[colour, 1, s], side_lane(2), 256

    def compute(colour, dp):
        norm(colour, dp, late)
        for kind in (0, 1):
            left = wbuf[kind, :, :, pl.ds(pl.multiple_of(colour * PART, PART), PART)]
            product = lax.dot_general(
                left.reshape(192, PART), nbuf[colour, dp, kind], NT,
                preferred_element_type=jnp.float32,
            )
            for ds in range(SIDE):
                row = origin(colour, dp, ds)
                pbuf[row, 192 * kind:192 * (kind + 1), :] += product[:, ds * NEW:(ds + 1) * NEW]

    for i in range(SIDE):
        ring_second(send, arrived, i)
        side_out(1, gray(i))

    weights_out(1, 15)
    pltpu.make_async_copy(stats, stats, stat_recv).wait()
    for dp in (1, 3, 2):
        side_on(0, dp)

    @pl.loop(0, SIDE)
    def _(i):
        side_on(1, gray(i))

        @pl.loop(0, 2)
        def _(colour):
            norm(colour, gray(i), early)

    pltpu.make_async_copy(wbuf, wbuf, wrecv_sem).wait()

    @pl.loop(0, SIDE)
    def _(i):
        dp = gray(i)
        for colour in (0, 1):
            for n in (2, 3):
                side_wait(colour, 1, dp, n)

            @pl.when(i > 0)
            def _():
                for n in (2, 3):
                    side_wait(colour, 0, dp, n)

        @pl.loop(0, 2)
        def _(colour):
            compute(colour, dp)

    pair = pltpu.make_async_remote_copy(
        src_ref=pbuf.at[pl.ds(8 * mate, 8)], dst_ref=rbuf,
        send_sem=pair_sem.at[0], recv_sem=pair_sem.at[1],
        device_id=(me, 2 * x + mate), device_id_type=MESH,
    )
    pair.start()
    bias_own.wait()
    bias_mate.wait()
    pair.wait_recv()
    mine = pl.ds(pl.multiple_of(me * 72, 8), 72)

    @pl.loop(0, 8)
    def _(q):
        row = 8 * core + q
        total = pbuf[row] + rbuf[q]
        for h in (0, 1):
            qsend[2 * q + h] = total[96 * h:96 * h + 72]
            remote = pltpu.make_async_remote_copy(
                src_ref=qsend.at[2 * q + h], dst_ref=qrecv.at[mine],
                send_sem=qsend_sem, recv_sem=qrecv_sem,
                device_id=(row, 2 * x + h), device_id_type=MESH,
            )
            away = jnp.logical_or(row != me, core != h)

            @pl.when(away)
            def _():
                remote.start()

            @pl.when(jnp.logical_not(away))
            def _():
                pltpu.make_async_copy(qsend.at[2 * q + h], qrecv.at[mine], qrecv_sem).start()
        at = pl.ds(pl.multiple_of(q * NEW, NEW), NEW)
        for h in (0, 1):
            u = total[192 + 96 * h:288 + 96 * h] + bbuf[h]
            inner = 0.7978845608028654 * (u + 0.044715 * (u * u * u))
            units_ref[h, :, at] = (0.5 * u * (1.0 + jnp.tanh(inner))).astype(jnp.bfloat16)

    pltpu.make_async_copy(qrecv, qrecv, qrecv_sem).wait()
    qkv_ref[...] = qrecv[...]
    pair.wait_send()

    @pl.when(goal == core)
    def _():
        some = qsend.at[pl.ds(0, 15)]
        pltpu.make_async_copy(some, some, qsend_sem).wait()

    @pl.when(goal != core)
    def _():
        pltpu.make_async_copy(qsend, qsend, qsend_sem).wait()
        mate_w().wait_send()

    some = wt_ref.at[pl.ds(0, 15)]
    pltpu.make_async_copy(some, some, wsend_sem).wait()
    for colour in (0, 1):
        some = xbuf.at[colour, pl.ds(1, 15)]
        pltpu.make_async_copy(some, some, xsend_sem.at[colour]).wait()
        some = sbuf.at[colour, :, pl.ds(1, 15)]
        pltpu.make_async_copy(some, some, side_send.at[colour]).wait()
    some = stats.at[pl.ds(0, 15)]
    pltpu.make_async_copy(some, some, stat_send).wait()


def front(hidden, gains, qkv_weight, up_weight, up_bias):
    req = lax.axis_index("req")
    widened = hidden.astype(jnp.float32)
    center = jnp.mean(widened, axis=-1)
    spread = lax.rsqrt(jnp.mean(jnp.square(widened - center[:, None]), axis=-1) + 1e-05)
    stat = jnp.pad(jnp.stack([center, spread]), ((0, 6), (0, 0)))
    depth = qkv_weight.shape[0]
    wq = jnp.pad(qkv_weight.T.reshape(16, 72, depth), ((0, 0), (0, 24), (0, 0)))
    wt = jnp.stack([wq, up_weight.T.reshape(16, 96, depth)], axis=1)
    gain = jnp.stack(gains)
    bias = lax.dynamic_slice_in_dim(up_bias, req * 96, 96, 0)
    bias = jnp.broadcast_to(bias[:, None], (96, 128))
    vmem = pl.BlockSpec(memory_space=pltpu.VMEM)
    hbm = pl.BlockSpec(memory_space=pl.ANY)
    dma = pltpu.SemaphoreType.DMA
    return pl.pallas_call(
        front_kernel,
        out_shape=(
            jax.ShapeDtypeStruct((1152, NEW), jnp.float32),
            jax.ShapeDtypeStruct((2, 96, 1024), jnp.bfloat16),
        ),
        in_specs=[hbm, hbm, hbm, vmem, hbm],
        out_specs=(vmem, vmem),
        scratch_shapes=[
            pltpu.VMEM((2, 16, NEW, DIRECT + 256), jnp.bfloat16),
            pltpu.VMEM((2, 3, 16, NEW, 256), jnp.bfloat16),
            pltpu.VMEM((16, 8, NEW), jnp.float32),
            pltpu.VMEM((2, 2, 96, HALF), jnp.bfloat16),
            pltpu.VMEM((2, SIDE, 2, 512, PART), jnp.bfloat16),
            pltpu.VMEM((16, 384, NEW), jnp.float32),
            pltpu.VMEM((8, 384, NEW), jnp.float32),
            pltpu.VMEM((2, 96, NEW), jnp.float32),
            pltpu.VMEM((16, 72, NEW), jnp.float32),
            pltpu.VMEM((1152, NEW), jnp.float32),
            dma((2,)), dma((2, 2, 16)), dma((2, 5)), dma((2,)), dma((2, 2, 4, 4)), dma, dma,
            dma, dma, dma, dma((3,)), dma((2,)), dma, dma,
        ],
        compiler_params=pltpu.CompilerParams(
            collective_id=0, has_side_effects=True, vmem_limit_bytes=VMEM_LIMIT
        ),
        name="front",
    )(hidden, stat, wt, gain, bias)


def back_kernel(
    len_ref, units_ref, qkv_ref, qbias_ref, cos_ref, sin_ref, k_hbm, v_hbm,
    wd_ref, wo_ref, rest_ref, bias_ref, out_ref, nk_ref, nv_ref,
    ubuf, aring, amate, dbuf, obuf, dturn, total, tsend, rsum, share, rest, fout,
    kbuf, vbuf, sbuf, qexp, vkeep, att_ref, ksem, vsem,
    usend_sem, urecv_sem, own_sem, asend_sem, arecv_sem, amate_sem, w_sem,
    hsend_sem, hrecv_sem, rsend_sem, rrecv_sem, fsend_sem, frecv_sem, gsend_sem, grecv_sem,
):
    for hbm, buf, sem in ((k_hbm, kbuf, ksem), (v_hbm, vbuf, vsem)):
        for n in range(CACHE // KB):
            fetch(n, hbm, buf, sem).start()
    y, z, x, core = place()
    me = y * SIDE + z
    mate = 1 - core
    goal = y // 2
    barrier = pltpu.get_barrier_semaphore()

    def plane(i):
        return (i // 2, 2 * x + i % 2)

    def line(i):
        return (me, i)

    meet(barrier, [
        (32, plane, lambda i: i != 2 * me + core),
        (8, line, lambda i: i // 2 != x),
    ])
    pl.semaphore_wait(barrier, 37)

    def apart(s, colour, half):
        return aring.at[s, pl.ds(32 * (2 * colour + half), 32)]

    def aown(colour, half):
        return att_ref.at[pl.ds(32 * (2 * colour + half), 32)]

    asend, aarrived = ring_units(y, z, x, core, aown, Absolute(y, z), apart, asend_sem, arecv_sem)

    def lanes(colour, half):
        return pl.ds((2 * colour + half) * 256, 256)

    def part(s, colour, half):
        return ubuf.at[:, s, :, lanes(colour, half)]

    def own(colour, half):
        return units_ref.at[:, :, lanes(colour, half)]

    send, arrived = ring_units(y, z, x, core, own, Absolute(y, z), part, usend_sem, urecv_sem)
    ring_start(send)
    copies = [pltpu.make_async_copy(units_ref, ubuf.at[:, me], own_sem.at[0])]
    for n, (src, dst) in enumerate(((wd_ref, dbuf), (wo_ref, obuf))):
        copies.append(pltpu.make_async_copy(src, dst.at[core], w_sem.at[3 * n]))
        copies.append(pltpu.make_async_remote_copy(
            src_ref=src, dst_ref=dst.at[core], send_sem=w_sem.at[3 * n + 1],
            recv_sem=w_sem.at[3 * n + 2], device_id=(me, 2 * x + mate), device_id_type=MESH,
        ))
    for copy in copies:
        copy.start()
    slot = me % 8

    def tile(row):
        return rest_ref.at[
            pl.ds(pl.multiple_of(32 * x, 32), 32), pl.ds(pl.multiple_of(384 * row, 384), 384)
        ]

    @pl.when(goal == core)
    def _():
        @pl.loop(1, 16)
        def _(i):
            row = lax.rem(y + i // SIDE, SIDE) * SIDE + lax.rem(z + i % SIDE, SIDE)
            pltpu.make_async_remote_copy(
                src_ref=tile(row), dst_ref=rest.at[slot],
                send_sem=hsend_sem, recv_sem=hrecv_sem,
                device_id=(row, 2 * x + core), device_id_type=MESH,
            ).start()
        pltpu.make_async_copy(tile(me), rest.at[slot], hrecv_sem).start()

    heads = HEADS_HERE
    keep = (vkeep, qexp, sbuf)

    def key_block(n, at):
        fetch(n, k_hbm, kbuf, ksem).wait()
        return kbuf[at, :]

    def value_block(n, at):
        fetch(n, v_hbm, vbuf, vsem).wait()
        return vbuf[at, :]

    top = attention_scores(
        heads, len_ref[0], qkv_ref, qbias_ref, cos_ref, sin_ref, nk_ref, nv_ref, keep, key_block)
    ring_first(send, arrived, True)
    attention_mix(heads, top, keep, att_ref, value_block)
    att_own = pltpu.make_async_copy(att_ref, aring.at[me], own_sem.at[1])
    att_own.start()
    ring_start(asend)
    for copy in copies:
        copy.wait()

    def turn(first, count):
        @pl.loop(first, first + count)
        def _(n):
            h, at = n // 12, pl.ds(pl.multiple_of((n % 12) * 128, 128), 128)
            dturn[h, :, at] = dbuf[h, at, :].T

    ring_second(send, arrived, 0, True)
    turn(0, 12)
    ring_second(send, arrived, 1, True)
    turn(12, 12)
    ring_first(asend, aarrived, True)
    ring_second(send, arrived, 2, True)
    ring_second(asend, aarrived, 0, True)
    ring_second(asend, aarrived, 1, True)
    ring_second(send, arrived, 3, True)
    ring_second(asend, aarrived, 2, True)
    ring_second(asend, aarrived, 3, True)
    att_own.wait()
    pair = pltpu.make_async_remote_copy(
        src_ref=aring.at[pl.ds(8 * mate, 8)], dst_ref=amate,
        send_sem=amate_sem.at[0], recv_sem=amate_sem.at[1],
        device_id=(me, 2 * x + mate), device_id_type=MESH,
    )
    pair.start()
    pair.wait_recv()

    def rcopy(q, step):
        to = lax.rem(x + step, SIDE)
        return pltpu.make_async_remote_copy(
            src_ref=tsend.at[q, pl.ds(pl.multiple_of(32 * to, 32), 32)],
            dst_ref=rsum.at[step - 1, q],
            send_sem=rsend_sem.at[step - 1], recv_sem=rrecv_sem.at[step - 1],
            device_id=(me, 2 * to + core), device_id_type=MESH,
        )

    @pl.loop(0, 4)
    def _(p):
        at = pl.ds(pl.multiple_of(2 * p * NEW, 2 * NEW), 2 * NEW)
        turned = jnp.zeros((384, 2 * NEW), jnp.float32)
        for h in (0, 1):
            turned += jnp.dot(
                dturn[h], ubuf[h, :, :, at].reshape(PART, 2 * NEW),
                preferred_element_type=jnp.float32,
            )
        for n in (0, 1):
            q = 2 * p + n
            value = turned[:, n * NEW:(n + 1) * NEW].T
            value += jnp.dot(
                aring[8 * core + q], obuf[core], preferred_element_type=jnp.float32
            ) + jnp.dot(amate[q], obuf[mate], preferred_element_type=jnp.float32)
            total[q] = value
            tsend[q] = value.astype(jnp.bfloat16)
        for n in (0, 1):
            for step in (2, 1, 3):
                rcopy(2 * p + n, step).start()

    pltpu.make_async_copy(rest, rest, hrecv_sem).wait()
    for step in (1, 3, 2):
        some = rsum.at[step - 1]
        pltpu.make_async_copy(some, some, rrecv_sem.at[step - 1]).wait()
    rows = pl.ds(pl.multiple_of(32 * x, 32), 32)
    mine = pl.ds(pl.multiple_of(384 * me, 384), 384)

    @pl.loop(0, 8)
    def _(q):
        value = total[q, rows, :] + rsum[0, q].astype(jnp.float32)
        value += rsum[1, q].astype(jnp.float32) + rsum[2, q].astype(jnp.float32)
        share[q] = (rest[q].astype(jnp.float32) + (value + bias_ref[...])).astype(jnp.bfloat16)
        row = 8 * core + q

        @pl.when(row != me)
        def _():
            pltpu.make_async_remote_copy(
                src_ref=share.at[q], dst_ref=fout.at[rows, mine],
                send_sem=fsend_sem, recv_sem=frecv_sem,
                device_id=(row, 2 * x + goal), device_id_type=MESH,
            ).start()

        @pl.when(row == me)
        def _():
            pltpu.make_async_copy(share.at[q], fout.at[rows, mine], frecv_sem).start()

    def piece(owner, c):
        return fout.at[
            pl.ds(pl.multiple_of(32 * owner, 32), 32), pl.ds(pl.multiple_of(c * HALF, HALF), HALF)
        ]

    def gcopy(step):
        to = lax.rem(x + step + SIDE, SIDE)
        way = (1 - step) // 2
        return pltpu.make_async_remote_copy(
            src_ref=piece(x, core), dst_ref=piece(x, core), send_sem=gsend_sem.at[0, way],
            recv_sem=grecv_sem.at[0, way], device_id=(me, 2 * to + core), device_id_type=MESH,
        )

    def strip(owner, way):
        return fout.at[
            pl.ds(pl.multiple_of(32 * owner + 16 * way, 16), 16),
            pl.ds(pl.multiple_of(core * HALF, HALF), HALF),
        ]

    def grelay(step):
        to = lax.rem(x + step + SIDE, SIDE)
        owner = lax.rem(x - step + SIDE, SIDE)
        way = (1 - step) // 2
        return pltpu.make_async_remote_copy(
            src_ref=strip(owner, way), dst_ref=strip(owner, way), send_sem=gsend_sem.at[0, 2 + way],
            recv_sem=grecv_sem.at[0, 2 + way], device_id=(me, 2 * to + core), device_id_type=MESH,
        )

    def pass_on(step):
        owner = lax.rem(x - step + SIDE, SIDE)
        return pltpu.make_async_remote_copy(
            src_ref=piece(owner, core), dst_ref=piece(owner, core), send_sem=gsend_sem.at[1, step],
            recv_sem=grecv_sem.at[1, step], device_id=(me, 2 * x + mate), device_id_type=MESH,
        )

    def landed(kind, n, ref):
        pltpu.make_async_copy(ref, ref, grecv_sem.at[kind, n]).wait()

    def owner_at(step):
        return lax.rem(x - step + SIDE, SIDE)

    pltpu.make_async_copy(piece(x, core), piece(x, core), frecv_sem).wait()
    for step in (1, -1):
        gcopy(step).start()
    pass_on(0).start()
    for step in (1, -1):
        landed(0, (1 - step) // 2, piece(owner_at(step), core))
        grelay(step).start()
        pass_on(step % SIDE).start()
    for way in (0, 1):
        landed(0, 2 + way, strip(owner_at(2), way))
    pass_on(2).start()
    for step in (0, 1, 3, 2):
        landed(1, step, piece(owner_at(step), mate))
    out_ref[...] = fout[...]

    for step in (1, -1):
        gcopy(step).wait_send()
        grelay(step).wait_send()
    for step in (1, 2, 3):
        some = rsum.at[step - 1]
        pltpu.make_async_copy(some, some, rsend_sem.at[step - 1]).wait()
    for step in range(4):
        pass_on(step).wait_send()
    pair.wait_send()

    @pl.when(goal == core)
    def _():
        some = share.at[pl.ds(0, 7)]
        pltpu.make_async_copy(some, some, fsend_sem).wait()
        some = rest_ref.at[pl.ds(0, 32), pl.ds(0, 15 * 384)]
        pltpu.make_async_copy(some, some, hsend_sem).wait()

    @pl.when(goal != core)
    def _():
        pltpu.make_async_copy(share, share, fsend_sem).wait()

    for colour in (0, 1):
        some = ubuf.at[:, pl.ds(0, 15), :, pl.ds(512 * colour, 512)]
        pltpu.make_async_copy(some, some, usend_sem.at[colour]).wait()
        some = aring.at[pl.ds(0, 15), pl.ds(64 * colour, 64)]
        pltpu.make_async_copy(some, some, asend_sem.at[colour]).wait()


def back(units, qkv, qkv_bias, length, keys_old, values_old, hidden, out_weight, down_weight, bias_total):
    cosine, sine = rotation_tables(length[0])
    req = lax.axis_index("req")
    bias = lax.dynamic_slice_in_dim(bias_total, req * 384, 384, 0)[None, :]
    vmem = pl.BlockSpec(memory_space=pltpu.VMEM)
    hbm = pl.BlockSpec(memory_space=pl.ANY)
    dma = pltpu.SemaphoreType.DMA
    return pl.pallas_call(
        back_kernel,
        out_shape=(
            jax.ShapeDtypeStruct((NEW, 2 * HALF), jnp.bfloat16),
            jax.ShapeDtypeStruct((NEW, 384), jnp.bfloat16),
            jax.ShapeDtypeStruct((NEW, 384), jnp.bfloat16),
        ),
        in_specs=[
            pl.BlockSpec(memory_space=pltpu.SMEM), hbm, vmem, vmem, vmem, vmem, hbm, hbm,
            hbm, hbm, hbm, vmem,
        ],
        out_specs=(vmem, vmem, vmem),
        scratch_shapes=[
            pltpu.VMEM((2, 16, 96, 1024), jnp.bfloat16),
            pltpu.VMEM((16, NEW, 384), jnp.bfloat16),
            pltpu.VMEM((8, NEW, 384), jnp.bfloat16),
            pltpu.VMEM((2, PART, 384), jnp.bfloat16),
            pltpu.VMEM((2, 384, 384), jnp.bfloat16),
            pltpu.VMEM((2, 384, PART), jnp.bfloat16),
            pltpu.VMEM((8, NEW, 384), jnp.float32),
            pltpu.VMEM((8, NEW, 384), jnp.bfloat16),
            pltpu.VMEM((3, 8, 32, 384), jnp.bfloat16),
            pltpu.VMEM((8, 32, 384), jnp.bfloat16),
            pltpu.VMEM((8, 32, 384), jnp.bfloat16),
            pltpu.VMEM((NEW, 2 * HALF), jnp.bfloat16),
            pltpu.VMEM((CACHE, 384), jnp.bfloat16),
            pltpu.VMEM((CACHE, 384), jnp.bfloat16),
            pltpu.VMEM((HEADS_HERE * NEW, CACHE + NEW), jnp.float32),
            pltpu.VMEM((HEADS_HERE * NEW, 384), jnp.bfloat16),
            pltpu.VMEM((NEW, 384), jnp.bfloat16),
            pltpu.VMEM((NEW, 384), jnp.bfloat16),
            dma((CACHE // KB,)), dma((CACHE // KB,)),
            dma((2,)), dma((2, 2, 16)), dma((2,)), dma((2,)), dma((2, 2, 16)), dma((2,)), dma((6,)),
            dma, dma, dma((3,)), dma((3,)), dma, dma, dma((2, 4)), dma((2, 4)),
        ],
        compiler_params=pltpu.CompilerParams(
            collective_id=1, has_side_effects=True, vmem_limit_bytes=VMEM_LIMIT
        ),
        name="back",
    )(length, units, qkv, qkv_bias[None, :], cosine, sine, keys_old, values_old,
      down_weight, out_weight, hidden, bias)


def body(
    hidden,
    attn_norm_gain,
    attn_norm_bias,
    mlp_norm_gain,
    mlp_norm_bias,
    qkv_weight,
    qkv_bias,
    out_weight,
    out_bias,
    up_weight,
    up_bias,
    down_weight,
    down_bias,
    cache_keys,
    cache_values,
    cached_len,
):
    gains = (attn_norm_gain, attn_norm_bias, mlp_norm_gain, mlp_norm_bias)
    qkv, units = front(hidden, gains, qkv_weight, up_weight, up_bias)
    result, key_rows, value_rows = back(
        units, qkv, qkv_bias, cached_len, cache_keys[0], cache_values[0],
        hidden, out_weight, down_weight, out_bias + down_bias,
    )
    return (result, key_rows[None], value_rows[None])


def solution(mesh):
    return jax.shard_map(
        body,
        mesh=mesh,
        in_specs=(
            P("req", None),
            P(),
            P(),
            P(),
            P(),
            P("req", "head"),
            P("head"),
            P("head", "req"),
            P(),
            P("req", "head"),
            P("head"),
            P("head", "req"),
            P(),
            P("req", None, "head"),
            P("req", None, "head"),
            P("req"),
        ),
        out_specs=(P("req", None), P("req", None, "head"), P("req", None, "head")),
        check_vma=False,
    )
```

```python
import functools
import math

import jax
import jax.numpy as jnp
from jax import lax
from jax.experimental import pallas as pl
from jax.experimental.pallas import tpu as pltpu
from jax.sharding import PartitionSpec as P

DH = 96
ROT = 24
NEW = 128
CACHE = 4096
KB = 512
NT = (((1,), (1,)), ((), ()))


def rotation_tables(length):
    position = length.astype(jnp.float32) + jnp.arange(NEW, dtype=jnp.float32)
    halfway = ROT // 2
    exponent = jnp.arange(halfway, dtype=jnp.float32) * (2.0 / ROT)
    frequency = jnp.power(10000.0, -exponent)
    angle = position[None, :] * frequency[:, None]
    cosine, sine = jnp.cos(angle), jnp.sin(angle)
    return jnp.concatenate([cosine, cosine], 0), jnp.concatenate([-sine, sine], 0)


def fetch(n, hbm, buf, sem):
    rows = pl.ds(pl.multiple_of(n * KB, KB), KB)
    return pltpu.make_async_copy(hbm.at[rows], buf.at[rows], sem.at[n])


def attention_scores(heads, length, qkv_ref, bias_ref, cos_ref, sin_ref, nk_ref, nv_ref, keep, key_block):
    scale = 1.0 / math.sqrt(DH)
    width = heads * DH
    vkeep, qexp, sbuf = keep
    cosine, sine = cos_ref[...], sin_ref[...]

    def turned(rows):
        low = rows[:ROT]
        swapped = jnp.concatenate([low[ROT // 2:], low[: ROT // 2]], axis=0)
        return jnp.concatenate([low * cosine + swapped * sine, rows[ROT:]], axis=0)

    bias = jnp.broadcast_to(bias_ref[...], (8, 3 * width)).T

    def block(j, part):
        first = (3 * j + part) * DH
        return qkv_ref[pl.ds(first, DH), :] + bias[first:first + DH, 0:1]

    queries = jnp.concatenate([turned(block(j, 0)) for j in range(heads)], 0).T.astype(jnp.bfloat16)
    keys = jnp.concatenate([turned(block(j, 1)) for j in range(heads)], 0).T.astype(jnp.bfloat16)
    values = jnp.concatenate([block(j, 2) for j in range(heads)], 0).T.astype(jnp.bfloat16)
    nk_ref[...] = keys
    nv_ref[...] = values
    vkeep[...] = values
    lane_head = lax.broadcasted_iota(jnp.int32, (NEW, width), 1) // DH
    for j in range(heads):
        qexp[pl.ds(j * NEW, NEW), :] = jnp.where(lane_head == j, queries, jnp.zeros_like(queries))
    rows = heads * NEW
    fresh = lax.dot_general(qexp[...], keys, NT, preferred_element_type=jnp.float32) * scale
    row_at = lax.broadcasted_iota(jnp.int32, (rows, NEW), 0) % NEW
    col_at = lax.broadcasted_iota(jnp.int32, (rows, NEW), 1)
    fresh = jnp.where(col_at <= row_at, fresh, -1e30)
    sbuf[:, CACHE:] = fresh

    def score(n, top):
        at = pl.ds(pl.multiple_of(n * KB, KB), KB)
        part = lax.dot_general(
            qexp[...], key_block(n, at), NT, preferred_element_type=jnp.float32) * scale
        col = lax.broadcasted_iota(jnp.int32, (rows, KB), 1) + n * KB
        part = jnp.where(col < length, part, -1e30)
        sbuf[:, at] = part
        for t in range(KB // NEW):
            top = jnp.maximum(top, part[:, t * NEW:(t + 1) * NEW])
        return top

    return lax.fori_loop(0, CACHE // KB, score, fresh)


def attention_mix(heads, top, keep, att_ref, value_block):
    width = heads * DH
    vkeep, _, sbuf = keep
    highest = jnp.max(top, axis=1, keepdims=True)
    fresh_weights = jnp.exp(sbuf[:, CACHE:] - highest)
    mixed = jnp.dot(
        fresh_weights.astype(jnp.bfloat16), vkeep[...], preferred_element_type=jnp.float32)

    def weigh(n, carry):
        mixed, total = carry
        at = pl.ds(pl.multiple_of(n * KB, KB), KB)
        weights = jnp.exp(sbuf[:, at] - highest)
        for t in range(KB // NEW):
            total = total + weights[:, t * NEW:(t + 1) * NEW]
        mixed = mixed + jnp.dot(
            weights.astype(jnp.bfloat16), value_block(n, at), preferred_element_type=jnp.float32)
        return mixed, total

    mixed, total = lax.fori_loop(0, CACHE // KB, weigh, (mixed, fresh_weights))
    total = jnp.sum(total, axis=1, keepdims=True)
    lane_head = lax.broadcasted_iota(jnp.int32, (NEW, width), 1) // DH
    out = jnp.zeros((NEW, width), jnp.float32)
    for j in range(heads):
        at = slice(j * NEW, (j + 1) * NEW)
        out = jnp.where(lane_head == j, mixed[at] / total[at], out)
    att_ref[...] = out.astype(jnp.bfloat16)


MESH = pl.DeviceIdType.MESH
SIDE = 4
HALF = 3072
PART = 1536
DIRECT = 512
HEADS_HERE = 4
VMEM_LIMIT = 62 * 2**20


def place():
    req, head = lax.axis_index("req"), lax.axis_index("head")
    return req // SIDE, req % SIDE, head // 2, head % 2


def meet(barrier, others):
    for count, target, alone in others:
        @pl.loop(0, count)
        def _(i):
            @pl.when(alone(i))
            def _():
                pl.semaphore_signal(barrier, inc=1, device_id=target(i), device_id_type=MESH)


def ring_units(y, z, x, core, own, slot, part, send_sem, recv_sem):
    def send(colour, dp, ds, half, along, step):
        to = [dp, ds]
        to[along] = (to[along] + step) % SIDE if isinstance(to[along], int) else lax.rem(
            to[along] + step + SIDE, SIDE)
        on_z = (colour == 0) == (along == 0)
        dev_y = y if on_z else lax.rem(y + step + SIDE, SIDE)
        dev_z = lax.rem(z + step + SIDE, SIDE) if on_z else z
        is_own = isinstance(dp, int) and isinstance(ds, int) and dp == 0 and ds == 0
        src = own(colour, half) if is_own else part(slot(colour, dp, ds, 0), colour, half)
        source = (colour, dp, ds)
        dst = part(slot(*source, 0), colour, half) if slot.absolute else part(
            slot(colour, to[0], to[1], 0), colour, half)
        return pltpu.make_async_remote_copy(
            src_ref=src, dst_ref=dst, send_sem=send_sem.at[colour],
            recv_sem=recv_sem.at[colour, half, to[0] * SIDE + to[1]],
            device_id=(dev_y * SIDE + dev_z, 2 * x + core), device_id_type=MESH,
        )

    def arrived(colour, dp, ds, half):
        ref = part(slot(colour, dp, ds, 0), colour, half)
        pltpu.make_async_copy(ref, ref, recv_sem.at[colour, half, dp * SIDE + ds]).wait()

    return send, arrived


FIRST = ((1, 0), (3, 1), (1, 1), (3, 0), (2, 0), (2, 1))


def ring_start(send):
    for along in (0, 1):
        for half in (0, 1):
            for colour in (0, 1):
                for step in (1, -1):
                    send(colour, 0, 0, half, along, step).start()


def ring_spread(send, dp):
    for half in (0, 1):
        for colour in (0, 1):
            for step in (1, -1):
                send(colour, dp, 0, half, 1, step).start()


def ring_first(send, arrived):
    for dp, half in FIRST:
        if (dp, half) == (2, 0):
            ring_spread(send, 1)
        for colour in (0, 1):
            arrived(colour, dp, 0, half)
            if (dp, half) in ((1, 0), (3, 1)):
                send(colour, dp, 0, half, 0, 1 if dp == 1 else -1).start()


def ring_second(send, arrived, i):
    dp = gray(i)
    for ds, half in FIRST:
        if (ds, half) == (2, 0) and i < 2:
            ring_spread(send, gray(i + 2))
        for colour in (0, 1):
            arrived(colour, dp, ds, half)
            if (ds, half) in ((1, 0), (3, 1)):
                send(colour, dp, ds, half, 1, 1 if ds == 1 else -1).start()


def two_start(send):
    for along in (0, 1):
        for half in (0, 1):
            for colour in (0, 1):
                for step in (1, -1, 2):
                    send(colour, 0, 0, half, along, step).start()


def two_first(send, arrived):
    for dp, half in FIRST:
        for colour in (0, 1):
            arrived(colour, dp, 0, half)
            for step in (1, -1, 2):
                send(colour, dp, 0, half, 1, step).start()


def two_second(arrived):
    for dp in (0, 1, 3, 2):
        for ds, half in FIRST:
            for colour in (0, 1):
                arrived(colour, dp, ds, half)


def gray(i):
    return i + (i // 2) * (1 - 2 * (i % 2))


class Relative:
    absolute = False

    def __call__(self, colour, dp, ds, _):
        return dp * SIDE + ds


class Absolute:
    absolute = True

    def __init__(self, y, z):
        self.y, self.z = y, z

    def __call__(self, colour, dp, ds, _):
        dy, dz = (ds, dp) if colour == 0 else (dp, ds)
        return lax.rem(self.y - dy + SIDE, SIDE) * SIDE + lax.rem(self.z - dz + SIDE, SIDE)


def front_kernel(
    hid_ref, wq_ref, wu_ref, gain0, gain1, gain2, gain3, ub_in, qkv_ref, units_ref,
    wturn, wt_ref, stat_ref, bturn, ub_ref, xbuf, sbuf, stats, wbuf, nbuf, pbuf, rbuf, bbuf, qsend, qrecv,
    xsend_sem, xrecv_sem, own_sem, side_send, side_recv, stat_send, stat_recv,
    wsend_sem, wrecv_sem, wself_sem, bias_sem, pair_sem, qsend_sem, qrecv_sem,
):
    y, z, x, core = place()
    me = y * SIDE + z
    mate = 1 - core
    own_copies = []
    for colour in (0, 1):
        base = core * HALF + colour * PART

        def take(lane, width, dst, n):
            at = pl.ds(pl.multiple_of(base + lane, 256), width)
            own_copies.append(
                pltpu.make_async_copy(hid_ref.at[:, at], dst, own_sem.at[colour, n]))

        take(0, DIRECT, xbuf.at[colour, 0, :, pl.ds(0, DIRECT)], 0)
        take(DIRECT + 256 * x, 256, xbuf.at[colour, 0, :, pl.ds(DIRECT, 256)], 1)
        for dx in (1, 2, 3):
            plane_at = lax.rem(x - dx + SIDE, SIDE)
            take(DIRECT + 256 * plane_at, 256, sbuf.at[colour, dx - 1, 0], 1 + dx)
    for copy in own_copies:
        copy.start()
    barrier = pltpu.get_barrier_semaphore()

    def plane(i):
        return (i // 2, 2 * x + i % 2)

    def line(i):
        return (me, i)

    meet(barrier, [
        (32, plane, lambda i: i != 2 * me + core),
        (8, line, lambda i: i // 2 != x),
    ])
    for copy in own_copies:
        copy.wait()
    pl.semaphore_wait(barrier, 37)

    goal = y // 2
    kat = pl.ds(pl.multiple_of(((y % 2) * SIDE + z) * 384, 384), 384)

    def part(s, colour, half):
        return xbuf.at[colour, s, pl.ds(64 * half, 64)]

    def own(colour, half):
        return part(0, colour, half)

    send, arrived = ring_units(y, z, x, core, own, Relative(), part, xsend_sem, xrecv_sem)
    ring_start(send)

    def other(i):
        return lax.rem(y + i // SIDE, SIDE) * SIDE + lax.rem(z + i % SIDE, SIDE)

    def mate_w():
        return pltpu.make_async_remote_copy(
            src_ref=wt_ref.at[me], dst_ref=wbuf.at[:, core, :, kat],
            send_sem=wself_sem, recv_sem=wrecv_sem,
            device_id=(me, 2 * x + mate), device_id_type=MESH,
        )

    def weights_out(first, count):
        @pl.loop(first, first + count)
        def _(i):
            pltpu.make_async_remote_copy(
                src_ref=wt_ref.at[other(i)], dst_ref=wbuf.at[:, core, :, kat],
                send_sem=wsend_sem, recv_sem=wrecv_sem,
                device_id=(other(i), 2 * x + goal), device_id_type=MESH,
            ).start()

    def slots(kind, dp):
        return pl.ds(dp * SIDE, 1) if kind == 0 else pl.ds(dp * SIDE + 1, 3)

    def side_full(colour, kind, dp, step):
        way = (1 - step) // 2
        return pltpu.make_async_remote_copy(
            src_ref=xbuf.at[colour, slots(kind, dp), :, pl.ds(DIRECT, 256)],
            dst_ref=sbuf.at[colour, 2 * way, slots(kind, dp)],
            send_sem=side_send.at[colour], recv_sem=side_recv.at[colour, kind, dp, way],
            device_id=(me, 2 * lax.rem(x + step + SIDE, SIDE) + core), device_id_type=MESH,
        )

    def side_relay(colour, kind, dp, step):
        way = (1 - step) // 2
        rows = pl.ds(64 * way, 64)
        return pltpu.make_async_remote_copy(
            src_ref=sbuf.at[colour, 2 * way, slots(kind, dp), rows],
            dst_ref=sbuf.at[colour, 1, slots(kind, dp), rows],
            send_sem=side_send.at[colour], recv_sem=side_recv.at[colour, kind, dp, 2 + way],
            device_id=(me, 2 * lax.rem(x + step + SIDE, SIDE) + core), device_id_type=MESH,
        )

    def side_wait(colour, kind, dp, n):
        if n < 2:
            ref = sbuf.at[colour, 2 * n, slots(kind, dp)]
        else:
            ref = sbuf.at[colour, 1, slots(kind, dp), pl.ds(64 * (n - 2), 64)]
        pltpu.make_async_copy(ref, ref, side_recv.at[colour, kind, dp, n]).wait()

    def side_out(kind, dp):
        for colour in (0, 1):
            for step in (1, -1):
                side_full(colour, kind, dp, step).start()

    def side_on(kind, dp):
        for colour in (0, 1):
            for way in (0, 1):
                side_wait(colour, kind, dp, way)
                side_relay(colour, kind, dp, 1 - 2 * way).start()

    pbuf[...] = jnp.zeros_like(pbuf)
    ring_first(send, arrived)
    for dp in (1, 3, 2):
        side_out(0, dp)

    def lane_sum(tile):
        total = jnp.zeros((NEW, NEW), jnp.float32)
        for k in range(2 * HALF // 512):
            value = tile(hid_ref[:, 512 * k:512 * (k + 1)].astype(jnp.float32))
            for n in range(4):
                total += value[:, NEW * n:NEW * (n + 1)]
        return jnp.sum(total, axis=1, keepdims=True) * (1.0 / (2 * HALF))

    mean = lane_sum(lambda value: value)
    scatter = lax.rsqrt(lane_sum(lambda value: jnp.square(value - mean)) + 1e-05)
    lane = lax.broadcasted_iota(jnp.int32, (NEW, NEW), 1)
    stat_ref[...] = jnp.where(lane == 0, mean, jnp.where(lane == 1, scatter, 0.0)).T[0:8]
    bturn[...] = jnp.broadcast_to(ub_in[...], (8, PART)).T
    ub_ref[...] = jnp.broadcast_to(
        bturn[pl.ds(pl.multiple_of(96 * me, 8), 96), 0:1], (96, NEW))

    def turn(src, count):
        @pl.loop(0, count)
        def _(k):
            at = pl.ds(pl.multiple_of(k * NEW, NEW), NEW)
            wturn[at, :] = src[:, at].astype(jnp.float32).T

    turn(wq_ref, 9)

    @pl.loop(0, 16)
    def _(r):
        block = wturn[pl.ds(pl.multiple_of(72 * r, 8), 72), :]
        wt_ref[r, 0] = jnp.concatenate(
            [block, jnp.zeros((24, 384), jnp.float32)], axis=0).astype(jnp.bfloat16)

    turn(wu_ref, 12)

    @pl.loop(0, 16)
    def _(r):
        wt_ref[r, 1] = wturn[pl.ds(pl.multiple_of(96 * r, 8), 96), :].astype(jnp.bfloat16)

    @pl.loop(1, 16)
    def _(i):
        pltpu.make_async_remote_copy(
            src_ref=stat_ref, dst_ref=stats.at[me], send_sem=stat_send, recv_sem=stat_recv,
            device_id=(other(i), 2 * x + core), device_id_type=MESH,
        ).start()
    pltpu.make_async_copy(stat_ref, stats.at[me], stat_recv).start()
    bias_own = pltpu.make_async_copy(ub_ref, bbuf.at[core], bias_sem.at[0])
    bias_mate = pltpu.make_async_remote_copy(
        src_ref=ub_ref, dst_ref=bbuf.at[core], send_sem=bias_sem.at[1], recv_sem=bias_sem.at[2],
        device_id=(me, 2 * x + mate), device_id_type=MESH,
    )
    bias_own.start()
    bias_mate.start()

    @pl.when(goal != core)
    def _():
        mate_w().start()

    @pl.when(goal == core)
    def _():
        pltpu.make_async_copy(wt_ref.at[me], wbuf.at[:, core, :, kat], wrecv_sem).start()


    def origin(colour, dp, ds):
        dy = colour * dp + (1 - colour) * ds
        dz = colour * ds + (1 - colour) * dp
        return lax.rem(y - dy + SIDE, SIDE) * SIDE + lax.rem(z - dz + SIDE, SIDE)

    def norm(colour, dp, pieces):
        base = core * HALF + colour * PART

        @pl.loop(0, SIDE)
        def _(ds):
            turned = stats[origin(colour, dp, ds)].T
            center, spread = turned[:, 0:1], turned[:, 1:2]
            rows = pl.ds(pl.multiple_of(ds * NEW, NEW), NEW)
            for raw, lane, width in pieces(colour, dp * SIDE + ds):
                value = (raw.astype(jnp.float32) - center) * spread
                at = pl.ds(pl.multiple_of(base + lane, 256), width)
                to = pl.ds(pl.multiple_of(lane, 256), width)
                for kind, (gain, shift) in enumerate(((gain0, gain1), (gain2, gain3))):
                    nbuf[colour, dp, kind, rows, to] = (
                        value * gain[:, at] + shift[:, at]
                    ).astype(jnp.bfloat16)

    def side_lane(dx):
        return DIRECT + 256 * lax.rem(x - dx + SIDE, SIDE)

    def early(colour, s):
        yield xbuf[colour, s, :, 0:DIRECT], 0, DIRECT
        yield xbuf[colour, s, :, DIRECT:DIRECT + 256], DIRECT + 256 * x, 256
        for dx in (1, 3):
            yield sbuf[colour, dx - 1, s], side_lane(dx), 256

    def late(colour, s):
        yield sbuf[colour, 1, s], side_lane(2), 256

    def compute(colour, dp):
        norm(colour, dp, late)
        for kind in (0, 1):
            left = wbuf[kind, :, :, pl.ds(pl.multiple_of(colour * PART, PART), PART)]
            product = lax.dot_general(
                left.reshape(192, PART), nbuf[colour, dp, kind], NT,
                preferred_element_type=jnp.float32,
            )
            for ds in range(SIDE):
                row = origin(colour, dp, ds)
                pbuf[row, 192 * kind:192 * (kind + 1), :] += product[:, ds * NEW:(ds + 1) * NEW]

    for i in range(SIDE):
        ring_second(send, arrived, i)
        side_out(1, gray(i))

    weights_out(1, 15)
    pltpu.make_async_copy(stats, stats, stat_recv).wait()
    for dp in (1, 3, 2):
        side_on(0, dp)

    @pl.loop(0, SIDE)
    def _(i):
        side_on(1, gray(i))

        @pl.loop(0, 2)
        def _(colour):
            norm(colour, gray(i), early)

    pltpu.make_async_copy(wbuf, wbuf, wrecv_sem).wait()

    @pl.loop(0, SIDE)
    def _(i):
        dp = gray(i)
        for colour in (0, 1):
            for n in (2, 3):
                side_wait(colour, 1, dp, n)

            @pl.when(i > 0)
            def _():
                for n in (2, 3):
                    side_wait(colour, 0, dp, n)

        @pl.loop(0, 2)
        def _(colour):
            compute(colour, dp)

    pair = pltpu.make_async_remote_copy(
        src_ref=pbuf.at[pl.ds(8 * mate, 8)], dst_ref=rbuf,
        send_sem=pair_sem.at[0], recv_sem=pair_sem.at[1],
        device_id=(me, 2 * x + mate), device_id_type=MESH,
    )
    pair.start()
    bias_own.wait()
    bias_mate.wait()
    pair.wait_recv()
    mine = pl.ds(pl.multiple_of(me * 72, 8), 72)

    @pl.loop(0, 8)
    def _(q):
        row = 8 * core + q
        total = pbuf[row] + rbuf[q]
        for h in (0, 1):
            qsend[2 * q + h] = total[96 * h:96 * h + 72]
            remote = pltpu.make_async_remote_copy(
                src_ref=qsend.at[2 * q + h], dst_ref=qrecv.at[mine],
                send_sem=qsend_sem, recv_sem=qrecv_sem,
                device_id=(row, 2 * x + h), device_id_type=MESH,
            )
            away = jnp.logical_or(row != me, core != h)

            @pl.when(away)
            def _():
                remote.start()

            @pl.when(jnp.logical_not(away))
            def _():
                pltpu.make_async_copy(qsend.at[2 * q + h], qrecv.at[mine], qrecv_sem).start()
        at = pl.ds(pl.multiple_of(q * NEW, NEW), NEW)
        for h in (0, 1):
            u = total[192 + 96 * h:288 + 96 * h] + bbuf[h]
            inner = 0.7978845608028654 * (u + 0.044715 * (u * u * u))
            units_ref[h, :, at] = (0.5 * u * (1.0 + jnp.tanh(inner))).astype(jnp.bfloat16)

    pltpu.make_async_copy(qrecv, qrecv, qrecv_sem).wait()
    qkv_ref[...] = qrecv[...]
    pair.wait_send()

    @pl.when(goal == core)
    def _():
        some = qsend.at[pl.ds(0, 15)]
        pltpu.make_async_copy(some, some, qsend_sem).wait()

    @pl.when(goal != core)
    def _():
        pltpu.make_async_copy(qsend, qsend, qsend_sem).wait()
        mate_w().wait_send()

    some = wt_ref.at[pl.ds(0, 15)]
    pltpu.make_async_copy(some, some, wsend_sem).wait()
    for colour in (0, 1):
        some = xbuf.at[colour, pl.ds(1, 15)]
        pltpu.make_async_copy(some, some, xsend_sem.at[colour]).wait()
        some = sbuf.at[colour, :, pl.ds(1, 15)]
        pltpu.make_async_copy(some, some, side_send.at[colour]).wait()
    some = stats.at[pl.ds(0, 15)]
    pltpu.make_async_copy(some, some, stat_send).wait()


def front(hidden, gains, qkv_weight, up_weight, up_bias):
    vmem = pl.BlockSpec(memory_space=pltpu.VMEM)
    hbm = pl.BlockSpec(memory_space=pl.ANY)
    dma = pltpu.SemaphoreType.DMA
    return pl.pallas_call(
        front_kernel,
        out_shape=(
            jax.ShapeDtypeStruct((1152, NEW), jnp.float32),
            jax.ShapeDtypeStruct((2, 96, 1024), jnp.bfloat16),
        ),
        in_specs=[vmem] * 8,
        out_specs=(vmem, vmem),
        scratch_shapes=[
            pltpu.VMEM((PART, 384), jnp.float32),
            pltpu.VMEM((16, 2, 96, 384), jnp.bfloat16),
            pltpu.VMEM((8, NEW), jnp.float32),
            pltpu.VMEM((PART, 8), jnp.float32),
            pltpu.VMEM((96, NEW), jnp.float32),
            pltpu.VMEM((2, 16, NEW, DIRECT + 256), jnp.bfloat16),
            pltpu.VMEM((2, 3, 16, NEW, 256), jnp.bfloat16),
            pltpu.VMEM((16, 8, NEW), jnp.float32),
            pltpu.VMEM((2, 2, 96, HALF), jnp.bfloat16),
            pltpu.VMEM((2, SIDE, 2, 512, PART), jnp.bfloat16),
            pltpu.VMEM((16, 384, NEW), jnp.float32),
            pltpu.VMEM((8, 384, NEW), jnp.float32),
            pltpu.VMEM((2, 96, NEW), jnp.float32),
            pltpu.VMEM((16, 72, NEW), jnp.float32),
            pltpu.VMEM((1152, NEW), jnp.float32),
            dma((2,)), dma((2, 2, 16)), dma((2, 5)), dma((2,)), dma((2, 2, 4, 4)), dma, dma,
            dma, dma, dma, dma((3,)), dma((2,)), dma, dma,
        ],
        compiler_params=pltpu.CompilerParams(
            collective_id=0, has_side_effects=True, vmem_limit_bytes=VMEM_LIMIT
        ),
        name="front",
    )(hidden, qkv_weight, up_weight, *(gain[None, :] for gain in gains), up_bias[None, :])


def back_kernel(
    len_ref, units_ref, qkv_ref, qbias_ref, cos_ref, sin_ref, k_hbm, v_hbm,
    wd_ref, wo_ref, rest_ref, bias_ref, out_ref, nk_ref, nv_ref,
    ubuf, aring, amate, dbuf, obuf, dturn, total, tsend, rsum, share, rest, fout,
    kbuf, vbuf, sbuf, qexp, vkeep, att_ref, ksem, vsem,
    usend_sem, urecv_sem, own_sem, asend_sem, arecv_sem, amate_sem, w_sem,
    hsend_sem, hrecv_sem, rsend_sem, rrecv_sem, fsend_sem, frecv_sem, gsend_sem, grecv_sem,
):
    for hbm, buf, sem in ((k_hbm, kbuf, ksem), (v_hbm, vbuf, vsem)):
        for n in range(CACHE // KB):
            fetch(n, hbm, buf, sem).start()
    y, z, x, core = place()
    me = y * SIDE + z
    mate = 1 - core
    goal = y // 2
    barrier = pltpu.get_barrier_semaphore()

    def plane(i):
        return (i // 2, 2 * x + i % 2)

    def line(i):
        return (me, i)

    meet(barrier, [
        (32, plane, lambda i: i != 2 * me + core),
        (8, line, lambda i: i // 2 != x),
    ])
    pl.semaphore_wait(barrier, 37)

    def apart(s, colour, half):
        return aring.at[s, pl.ds(32 * (2 * colour + half), 32)]

    def aown(colour, half):
        return att_ref.at[pl.ds(32 * (2 * colour + half), 32)]

    asend, aarrived = ring_units(y, z, x, core, aown, Absolute(y, z), apart, asend_sem, arecv_sem)

    def lanes(colour, half):
        return pl.ds((2 * colour + half) * 256, 256)

    def part(s, colour, half):
        return ubuf.at[:, s, :, lanes(colour, half)]

    def own(colour, half):
        return units_ref.at[:, :, lanes(colour, half)]

    send, arrived = ring_units(y, z, x, core, own, Absolute(y, z), part, usend_sem, urecv_sem)
    ring_start(send)
    copies = [pltpu.make_async_copy(units_ref, ubuf.at[:, me], own_sem.at[0])]
    for n, (src, dst) in enumerate(((wd_ref, dbuf), (wo_ref, obuf))):
        copies.append(pltpu.make_async_copy(src, dst.at[core], w_sem.at[3 * n]))
        copies.append(pltpu.make_async_remote_copy(
            src_ref=src, dst_ref=dst.at[core], send_sem=w_sem.at[3 * n + 1],
            recv_sem=w_sem.at[3 * n + 2], device_id=(me, 2 * x + mate), device_id_type=MESH,
        ))
    for copy in copies:
        copy.start()
    slot = me % 8

    def tile(row):
        return rest_ref.at[
            pl.ds(pl.multiple_of(32 * x, 32), 32), pl.ds(pl.multiple_of(384 * row, 384), 384)
        ]

    @pl.when(goal == core)
    def _():
        @pl.loop(1, 16)
        def _(i):
            row = lax.rem(y + i // SIDE, SIDE) * SIDE + lax.rem(z + i % SIDE, SIDE)
            pltpu.make_async_remote_copy(
                src_ref=tile(row), dst_ref=rest.at[slot],
                send_sem=hsend_sem, recv_sem=hrecv_sem,
                device_id=(row, 2 * x + core), device_id_type=MESH,
            ).start()
        pltpu.make_async_copy(tile(me), rest.at[slot], hrecv_sem).start()

    heads = HEADS_HERE
    keep = (vkeep, qexp, sbuf)

    def key_block(n, at):
        fetch(n, k_hbm, kbuf, ksem).wait()
        return kbuf[at, :]

    def value_block(n, at):
        fetch(n, v_hbm, vbuf, vsem).wait()
        return vbuf[at, :]

    top = attention_scores(
        heads, len_ref[0], qkv_ref, qbias_ref, cos_ref, sin_ref, nk_ref, nv_ref, keep, key_block)
    ring_first(send, arrived)
    attention_mix(heads, top, keep, att_ref, value_block)
    att_own = pltpu.make_async_copy(att_ref, aring.at[me], own_sem.at[1])
    att_own.start()
    two_start(asend)
    for copy in copies:
        copy.wait()

    def turn(first, count):
        @pl.loop(first, first + count)
        def _(n):
            h, at = n // 12, pl.ds(pl.multiple_of((n % 12) * 128, 128), 128)
            dturn[h, :, at] = dbuf[h, at, :].T

    ring_second(send, arrived, 0)
    turn(0, 12)
    two_first(asend, aarrived)
    ring_second(send, arrived, 1)
    turn(12, 12)
    two_second(aarrived)
    att_own.wait()
    pair = pltpu.make_async_remote_copy(
        src_ref=aring.at[pl.ds(8 * mate, 8)], dst_ref=amate,
        send_sem=amate_sem.at[0], recv_sem=amate_sem.at[1],
        device_id=(me, 2 * x + mate), device_id_type=MESH,
    )
    pair.start()
    ring_second(send, arrived, 2)
    ring_second(send, arrived, 3)
    pair.wait_recv()

    def rcopy(q, step):
        to = lax.rem(x + step, SIDE)
        return pltpu.make_async_remote_copy(
            src_ref=tsend.at[q, pl.ds(pl.multiple_of(32 * to, 32), 32)],
            dst_ref=rsum.at[step - 1, q],
            send_sem=rsend_sem.at[step - 1], recv_sem=rrecv_sem.at[step - 1],
            device_id=(me, 2 * to + core), device_id_type=MESH,
        )

    @pl.loop(0, 4)
    def _(p):
        at = pl.ds(pl.multiple_of(2 * p * NEW, 2 * NEW), 2 * NEW)
        turned = jnp.zeros((384, 2 * NEW), jnp.float32)
        for h in (0, 1):
            turned += jnp.dot(
                dturn[h], ubuf[h, :, :, at].reshape(PART, 2 * NEW),
                preferred_element_type=jnp.float32,
            )
        for n in (0, 1):
            q = 2 * p + n
            value = turned[:, n * NEW:(n + 1) * NEW].T
            value += jnp.dot(
                aring[8 * core + q], obuf[core], preferred_element_type=jnp.float32
            ) + jnp.dot(amate[q], obuf[mate], preferred_element_type=jnp.float32)
            total[q] = value
            tsend[q] = value.astype(jnp.bfloat16)
        for n in (0, 1):
            for step in (2, 1, 3):
                rcopy(2 * p + n, step).start()

    pltpu.make_async_copy(rest, rest, hrecv_sem).wait()
    for step in (1, 3, 2):
        some = rsum.at[step - 1]
        pltpu.make_async_copy(some, some, rrecv_sem.at[step - 1]).wait()
    rows = pl.ds(pl.multiple_of(32 * x, 32), 32)
    mine = pl.ds(pl.multiple_of(384 * me, 384), 384)

    @pl.loop(0, 8)
    def _(q):
        value = total[q, rows, :] + rsum[0, q].astype(jnp.float32)
        value += rsum[1, q].astype(jnp.float32) + rsum[2, q].astype(jnp.float32)
        share[q] = (rest[q].astype(jnp.float32) + (value + bias_ref[...])).astype(jnp.bfloat16)
        row = 8 * core + q

        @pl.when(row != me)
        def _():
            pltpu.make_async_remote_copy(
                src_ref=share.at[q], dst_ref=fout.at[rows, mine],
                send_sem=fsend_sem, recv_sem=frecv_sem,
                device_id=(row, 2 * x + goal), device_id_type=MESH,
            ).start()

        @pl.when(row == me)
        def _():
            pltpu.make_async_copy(share.at[q], fout.at[rows, mine], frecv_sem).start()

    def piece(owner, c):
        return fout.at[
            pl.ds(pl.multiple_of(32 * owner, 32), 32), pl.ds(pl.multiple_of(c * HALF, HALF), HALF)
        ]

    def gcopy(step):
        to = lax.rem(x + step + SIDE, SIDE)
        way = (1 - step) // 2
        return pltpu.make_async_remote_copy(
            src_ref=piece(x, core), dst_ref=piece(x, core), send_sem=gsend_sem.at[0, way],
            recv_sem=grecv_sem.at[0, way], device_id=(me, 2 * to + core), device_id_type=MESH,
        )

    def strip(owner, way):
        return fout.at[
            pl.ds(pl.multiple_of(32 * owner + 16 * way, 16), 16),
            pl.ds(pl.multiple_of(core * HALF, HALF), HALF),
        ]

    def grelay(step):
        to = lax.rem(x + step + SIDE, SIDE)
        owner = lax.rem(x - step + SIDE, SIDE)
        way = (1 - step) // 2
        return pltpu.make_async_remote_copy(
            src_ref=strip(owner, way), dst_ref=strip(owner, way), send_sem=gsend_sem.at[0, 2 + way],
            recv_sem=grecv_sem.at[0, 2 + way], device_id=(me, 2 * to + core), device_id_type=MESH,
        )

    def pass_on(step):
        owner = lax.rem(x - step + SIDE, SIDE)
        return pltpu.make_async_remote_copy(
            src_ref=piece(owner, core), dst_ref=piece(owner, core), send_sem=gsend_sem.at[1, step],
            recv_sem=grecv_sem.at[1, step], device_id=(me, 2 * x + mate), device_id_type=MESH,
        )

    def landed(kind, n, ref):
        pltpu.make_async_copy(ref, ref, grecv_sem.at[kind, n]).wait()

    def owner_at(step):
        return lax.rem(x - step + SIDE, SIDE)

    pltpu.make_async_copy(piece(x, core), piece(x, core), frecv_sem).wait()
    for step in (1, -1):
        gcopy(step).start()
    pass_on(0).start()
    for step in (1, -1):
        landed(0, (1 - step) // 2, piece(owner_at(step), core))
        grelay(step).start()
        pass_on(step % SIDE).start()
    for way in (0, 1):
        landed(0, 2 + way, strip(owner_at(2), way))
    pass_on(2).start()
    for step in (0, 1, 3, 2):
        landed(1, step, piece(owner_at(step), mate))
    out_ref[...] = fout[...]

    for step in (1, -1):
        gcopy(step).wait_send()
        grelay(step).wait_send()
    for step in (1, 2, 3):
        some = rsum.at[step - 1]
        pltpu.make_async_copy(some, some, rsend_sem.at[step - 1]).wait()
    for step in range(4):
        pass_on(step).wait_send()
    pair.wait_send()

    @pl.when(goal == core)
    def _():
        some = share.at[pl.ds(0, 7)]
        pltpu.make_async_copy(some, some, fsend_sem).wait()
        some = rest_ref.at[pl.ds(0, 32), pl.ds(0, 15 * 384)]
        pltpu.make_async_copy(some, some, hsend_sem).wait()

    @pl.when(goal != core)
    def _():
        pltpu.make_async_copy(share, share, fsend_sem).wait()

    for colour in (0, 1):
        some = ubuf.at[:, pl.ds(0, 15), :, pl.ds(512 * colour, 512)]
        pltpu.make_async_copy(some, some, usend_sem.at[colour]).wait()
        some = aring.at[pl.ds(0, 15), pl.ds(64 * colour, 64)]
        pltpu.make_async_copy(some, some, asend_sem.at[colour]).wait()


def back(units, qkv, qkv_bias, length, keys_old, values_old, hidden, out_weight, down_weight, bias_total):
    cosine, sine = rotation_tables(length[0])
    req = lax.axis_index("req")
    bias = lax.dynamic_slice_in_dim(bias_total, req * 384, 384, 0)[None, :]
    vmem = pl.BlockSpec(memory_space=pltpu.VMEM)
    hbm = pl.BlockSpec(memory_space=pl.ANY)
    dma = pltpu.SemaphoreType.DMA
    return pl.pallas_call(
        back_kernel,
        out_shape=(
            jax.ShapeDtypeStruct((NEW, 2 * HALF), jnp.bfloat16),
            jax.ShapeDtypeStruct((NEW, 384), jnp.bfloat16),
            jax.ShapeDtypeStruct((NEW, 384), jnp.bfloat16),
        ),
        in_specs=[
            pl.BlockSpec(memory_space=pltpu.SMEM), hbm, vmem, vmem, vmem, vmem, hbm, hbm,
            hbm, hbm, hbm, vmem,
        ],
        out_specs=(vmem, vmem, vmem),
        scratch_shapes=[
            pltpu.VMEM((2, 16, 96, 1024), jnp.bfloat16),
            pltpu.VMEM((16, NEW, 384), jnp.bfloat16),
            pltpu.VMEM((8, NEW, 384), jnp.bfloat16),
            pltpu.VMEM((2, PART, 384), jnp.bfloat16),
            pltpu.VMEM((2, 384, 384), jnp.bfloat16),
            pltpu.VMEM((2, 384, PART), jnp.bfloat16),
            pltpu.VMEM((8, NEW, 384), jnp.float32),
            pltpu.VMEM((8, NEW, 384), jnp.bfloat16),
            pltpu.VMEM((3, 8, 32, 384), jnp.bfloat16),
            pltpu.VMEM((8, 32, 384), jnp.bfloat16),
            pltpu.VMEM((8, 32, 384), jnp.bfloat16),
            pltpu.VMEM((NEW, 2 * HALF), jnp.bfloat16),
            pltpu.VMEM((CACHE, 384), jnp.bfloat16),
            pltpu.VMEM((CACHE, 384), jnp.bfloat16),
            pltpu.VMEM((HEADS_HERE * NEW, CACHE + NEW), jnp.float32),
            pltpu.VMEM((HEADS_HERE * NEW, 384), jnp.bfloat16),
            pltpu.VMEM((NEW, 384), jnp.bfloat16),
            pltpu.VMEM((NEW, 384), jnp.bfloat16),
            dma((CACHE // KB,)), dma((CACHE // KB,)),
            dma((2,)), dma((2, 2, 16)), dma((2,)), dma((2,)), dma((2, 2, 16)), dma((2,)), dma((6,)),
            dma, dma, dma((3,)), dma((3,)), dma, dma, dma((2, 4)), dma((2, 4)),
        ],
        compiler_params=pltpu.CompilerParams(
            collective_id=1, has_side_effects=True, vmem_limit_bytes=VMEM_LIMIT
        ),
        name="back",
    )(length, units, qkv, qkv_bias[None, :], cosine, sine, keys_old, values_old,
      down_weight, out_weight, hidden, bias)


def body(
    hidden,
    attn_norm_gain,
    attn_norm_bias,
    mlp_norm_gain,
    mlp_norm_bias,
    qkv_weight,
    qkv_bias,
    out_weight,
    out_bias,
    up_weight,
    up_bias,
    down_weight,
    down_bias,
    cache_keys,
    cache_values,
    cached_len,
):
    gains = (attn_norm_gain, attn_norm_bias, mlp_norm_gain, mlp_norm_bias)
    qkv, units = front(hidden, gains, qkv_weight, up_weight, up_bias)
    result, key_rows, value_rows = back(
        units, qkv, qkv_bias, cached_len, cache_keys[0], cache_values[0],
        hidden, out_weight, down_weight, out_bias + down_bias,
    )
    return (result, key_rows[None], value_rows[None])


def solution(mesh):
    return jax.shard_map(
        body,
        mesh=mesh,
        in_specs=(
            P("req", None),
            P(),
            P(),
            P(),
            P(),
            P("req", "head"),
            P("head"),
            P("head", "req"),
            P(),
            P("req", "head"),
            P("head"),
            P("head", "req"),
            P(),
            P("req", None, "head"),
            P("req", None, "head"),
            P("req"),
        ),
        out_specs=(P("req", None), P("req", None, "head"), P("req", None, "head")),
        check_vma=False,
    )
```

```python
import functools
import math

import jax
import jax.numpy as jnp
from jax import lax
from jax.experimental import pallas as pl
from jax.experimental.pallas import tpu as pltpu
from jax.sharding import PartitionSpec as P

DH = 96
ROT = 24
NEW = 128
CACHE = 4096
KB = 512
NT = (((1,), (1,)), ((), ()))


def rotation_tables(length):
    position = length.astype(jnp.float32) + jnp.arange(NEW, dtype=jnp.float32)
    halfway = ROT // 2
    exponent = jnp.arange(halfway, dtype=jnp.float32) * (2.0 / ROT)
    frequency = jnp.power(10000.0, -exponent)
    angle = position[None, :] * frequency[:, None]
    cosine, sine = jnp.cos(angle), jnp.sin(angle)
    return jnp.concatenate([cosine, cosine], 0), jnp.concatenate([-sine, sine], 0)


def fetch(n, hbm, buf, sem):
    rows = pl.ds(pl.multiple_of(n * KB, KB), KB)
    return pltpu.make_async_copy(hbm.at[rows], buf.at[rows], sem.at[n])


def attention_scores(heads, length, qkv_ref, bias_ref, cos_ref, sin_ref, nk_ref, nv_ref, keep, key_block):
    scale = 1.0 / math.sqrt(DH)
    width = heads * DH
    vkeep, qexp, sbuf = keep
    cosine, sine = cos_ref[...], sin_ref[...]

    def turned(rows):
        low = rows[:ROT]
        swapped = jnp.concatenate([low[ROT // 2:], low[: ROT // 2]], axis=0)
        return jnp.concatenate([low * cosine + swapped * sine, rows[ROT:]], axis=0)

    bias = jnp.broadcast_to(bias_ref[...][None, :], (8, 3 * width)).T

    def block(j, part):
        first = (3 * j + part) * DH
        return qkv_ref[pl.ds(first, DH), :] + bias[first:first + DH, 0:1]

    queries = jnp.concatenate([turned(block(j, 0)) for j in range(heads)], 0).T.astype(jnp.bfloat16)
    keys = jnp.concatenate([turned(block(j, 1)) for j in range(heads)], 0).T.astype(jnp.bfloat16)
    values = jnp.concatenate([block(j, 2) for j in range(heads)], 0).T.astype(jnp.bfloat16)
    nk_ref[...] = keys
    nv_ref[...] = values
    vkeep[...] = values
    lane_head = lax.broadcasted_iota(jnp.int32, (NEW, width), 1) // DH
    for j in range(heads):
        qexp[pl.ds(j * NEW, NEW), :] = jnp.where(lane_head == j, queries, jnp.zeros_like(queries))
    rows = heads * NEW
    fresh = lax.dot_general(qexp[...], keys, NT, preferred_element_type=jnp.float32) * scale
    row_at = lax.broadcasted_iota(jnp.int32, (rows, NEW), 0) % NEW
    col_at = lax.broadcasted_iota(jnp.int32, (rows, NEW), 1)
    fresh = jnp.where(col_at <= row_at, fresh, -1e30)
    sbuf[:, CACHE:] = fresh

    def score(n, top):
        at = pl.ds(pl.multiple_of(n * KB, KB), KB)
        part = lax.dot_general(
            qexp[...], key_block(n, at), NT, preferred_element_type=jnp.float32) * scale
        col = lax.broadcasted_iota(jnp.int32, (rows, KB), 1) + n * KB
        part = jnp.where(col < length, part, -1e30)
        sbuf[:, at] = part
        for t in range(KB // NEW):
            top = jnp.maximum(top, part[:, t * NEW:(t + 1) * NEW])
        return top

    return lax.fori_loop(0, CACHE // KB, score, fresh)


def attention_mix(heads, top, keep, att_ref, value_block):
    width = heads * DH
    vkeep, _, sbuf = keep
    highest = jnp.max(top, axis=1, keepdims=True)
    fresh_weights = jnp.exp(sbuf[:, CACHE:] - highest)
    mixed = jnp.dot(
        fresh_weights.astype(jnp.bfloat16), vkeep[...], preferred_element_type=jnp.float32)

    def weigh(n, carry):
        mixed, total = carry
        at = pl.ds(pl.multiple_of(n * KB, KB), KB)
        weights = jnp.exp(sbuf[:, at] - highest)
        for t in range(KB // NEW):
            total = total + weights[:, t * NEW:(t + 1) * NEW]
        mixed = mixed + jnp.dot(
            weights.astype(jnp.bfloat16), value_block(n, at), preferred_element_type=jnp.float32)
        return mixed, total

    mixed, total = lax.fori_loop(0, CACHE // KB, weigh, (mixed, fresh_weights))
    total = jnp.sum(total, axis=1, keepdims=True)
    lane_head = lax.broadcasted_iota(jnp.int32, (NEW, width), 1) // DH
    out = jnp.zeros((NEW, width), jnp.float32)
    for j in range(heads):
        at = slice(j * NEW, (j + 1) * NEW)
        out = jnp.where(lane_head == j, mixed[at] / total[at], out)
    att_ref[...] = out.astype(jnp.bfloat16)


MESH = pl.DeviceIdType.MESH
SIDE = 4
HALF = 3072
PART = 1536
DIRECT = 512
HEADS_HERE = 4
VMEM_LIMIT = 62 * 2**20


def place():
    req, head = lax.axis_index("req"), lax.axis_index("head")
    return req // SIDE, req % SIDE, head // 2, head % 2


def meet(barrier, others):
    for count, target, alone in others:
        @pl.loop(0, count)
        def _(i):
            @pl.when(alone(i))
            def _():
                pl.semaphore_signal(barrier, inc=1, device_id=target(i), device_id_type=MESH)


def ring_units(y, z, x, core, own, slot, part, send_sem, recv_sem):
    def send(colour, dp, ds, half, along, step):
        to = [dp, ds]
        to[along] = (to[along] + step) % SIDE if isinstance(to[along], int) else lax.rem(
            to[along] + step + SIDE, SIDE)
        on_z = (colour == 0) == (along == 0)
        dev_y = y if on_z else lax.rem(y + step + SIDE, SIDE)
        dev_z = lax.rem(z + step + SIDE, SIDE) if on_z else z
        is_own = isinstance(dp, int) and isinstance(ds, int) and dp == 0 and ds == 0
        src = own(colour, half) if is_own else part(slot(colour, dp, ds, 0), colour, half)
        source = (colour, dp, ds)
        dst = part(slot(*source, 0), colour, half) if slot.absolute else part(
            slot(colour, to[0], to[1], 0), colour, half)
        return pltpu.make_async_remote_copy(
            src_ref=src, dst_ref=dst, send_sem=send_sem.at[colour],
            recv_sem=recv_sem.at[colour, half, to[0] * SIDE + to[1]],
            device_id=(dev_y * SIDE + dev_z, 2 * x + core), device_id_type=MESH,
        )

    def arrived(colour, dp, ds, half):
        ref = part(slot(colour, dp, ds, 0), colour, half)
        pltpu.make_async_copy(ref, ref, recv_sem.at[colour, half, dp * SIDE + ds]).wait()

    return send, arrived


FIRST = ((1, 0), (3, 1), (1, 1), (3, 0), (2, 0), (2, 1))


def ring_start(send):
    for along in (0, 1):
        for half in (0, 1):
            for colour in (0, 1):
                for step in (1, -1):
                    send(colour, 0, 0, half, along, step).start()


def ring_spread(send, dp):
    for half in (0, 1):
        for colour in (0, 1):
            for step in (1, -1):
                send(colour, dp, 0, half, 1, step).start()


def ring_first(send, arrived):
    for dp, half in FIRST:
        if (dp, half) == (2, 0):
            ring_spread(send, 1)
        for colour in (0, 1):
            arrived(colour, dp, 0, half)
            if (dp, half) in ((1, 0), (3, 1)):
                send(colour, dp, 0, half, 0, 1 if dp == 1 else -1).start()


def ring_second(send, arrived, i):
    dp = gray(i)
    for ds, half in FIRST:
        if (ds, half) == (2, 0) and i < 2:
            ring_spread(send, gray(i + 2))
        for colour in (0, 1):
            arrived(colour, dp, ds, half)
            if (ds, half) in ((1, 0), (3, 1)):
                send(colour, dp, ds, half, 1, 1 if ds == 1 else -1).start()


def two_start(send):
    for along in (0, 1):
        for half in (0, 1):
            for colour in (0, 1):
                for step in (1, -1, 2):
                    send(colour, 0, 0, half, along, step).start()


def two_first(send, arrived):
    for dp, half in FIRST:
        for colour in (0, 1):
            arrived(colour, dp, 0, half)
            for step in (1, -1, 2):
                send(colour, dp, 0, half, 1, step).start()


def two_second(arrived):
    for dp in (0, 1, 3, 2):
        for ds, half in FIRST:
            for colour in (0, 1):
                arrived(colour, dp, ds, half)


def gray(i):
    return i + (i // 2) * (1 - 2 * (i % 2))


class Relative:
    absolute = False

    def __call__(self, colour, dp, ds, _):
        return dp * SIDE + ds


class Absolute:
    absolute = True

    def __init__(self, y, z):
        self.y, self.z = y, z

    def __call__(self, colour, dp, ds, _):
        dy, dz = (ds, dp) if colour == 0 else (dp, ds)
        return lax.rem(self.y - dy + SIDE, SIDE) * SIDE + lax.rem(self.z - dz + SIDE, SIDE)


def front_kernel(
    hid_ref, wq_ref, wu_ref, gain0, gain1, gain2, gain3, ub_in, qkv_ref, units_ref,
    wturn, wt_ref, stat_ref, bturn, ub_ref, xbuf, sbuf, stats, wbuf, nbuf, pbuf, rbuf, bbuf, qsend, qrecv,
    xsend_sem, xrecv_sem, own_sem, side_send, side_recv, stat_send, stat_recv,
    wsend_sem, wrecv_sem, wself_sem, bias_sem, pair_sem, qsend_sem, qrecv_sem, extra_send, extra_recv,
):
    y, z, x, core = place()
    me = y * SIDE + z
    mate = 1 - core
    own_copies = []
    for colour in (0, 1):
        base = core * HALF + colour * PART

        def take(lane, width, dst, n):
            at = pl.ds(pl.multiple_of(base + lane, 256), width)
            own_copies.append(
                pltpu.make_async_copy(hid_ref.at[:, at], dst, own_sem.at[colour, n]))

        take(0, DIRECT, xbuf.at[colour, 0, :, pl.ds(0, DIRECT)], 0)
        take(DIRECT + 256 * x, 256, xbuf.at[colour, 0, :, pl.ds(DIRECT, 256)], 1)
        for dx in (1, 2, 3):
            plane_at = lax.rem(x - dx + SIDE, SIDE)
            take(DIRECT + 256 * plane_at, 256, sbuf.at[colour, dx - 1, 0], 1 + dx)
    for copy in own_copies:
        copy.start()
    barrier = pltpu.get_barrier_semaphore()

    def plane(i):
        return (i // 2, 2 * x + i % 2)

    def line(i):
        return (me, i)

    meet(barrier, [
        (32, plane, lambda i: i != 2 * me + core),
        (8, line, lambda i: i // 2 != x),
    ])
    for copy in own_copies:
        copy.wait()
    pl.semaphore_wait(barrier, 37)

    goal = y // 2
    kat = pl.ds(pl.multiple_of(((y % 2) * SIDE + z) * 384, 384), 384)

    def part(s, colour, half):
        return xbuf.at[colour, s, pl.ds(64 * half, 64)]

    def own(colour, half):
        return part(0, colour, half)

    send, arrived = ring_units(y, z, x, core, own, Relative(), part, xsend_sem, xrecv_sem)

    def extra(colour, dp, half):
        return sbuf.at[colour, :, dp * SIDE, pl.ds(64 * half, 64)]

    def extra_out(colour, dp, half, step):
        to = (dp + step) % SIDE
        dev_y = y if colour == 0 else lax.rem(y + step + SIDE, SIDE)
        dev_z = lax.rem(z + step + SIDE, SIDE) if colour == 0 else z
        pltpu.make_async_remote_copy(
            src_ref=extra(colour, dp, half), dst_ref=extra(colour, to, half),
            send_sem=extra_send.at[colour], recv_sem=extra_recv.at[colour, half, to],
            device_id=(dev_y * SIDE + dev_z, 2 * x + core), device_id_type=MESH,
        ).start()

    def extra_wait(colour, dp, half):
        ref = extra(colour, dp, half)
        pltpu.make_async_copy(ref, ref, extra_recv.at[colour, half, dp]).wait()

    ring_start(send)
    for half in (0, 1):
        for colour in (0, 1):
            for step in (1, -1):
                extra_out(colour, 0, half, step)

    def other(i):
        return lax.rem(y + i // SIDE, SIDE) * SIDE + lax.rem(z + i % SIDE, SIDE)

    def mate_w():
        return pltpu.make_async_remote_copy(
            src_ref=wt_ref.at[me], dst_ref=wbuf.at[:, core, :, kat],
            send_sem=wself_sem, recv_sem=wrecv_sem,
            device_id=(me, 2 * x + mate), device_id_type=MESH,
        )

    def weights_out(first, count):
        @pl.loop(first, first + count)
        def _(i):
            pltpu.make_async_remote_copy(
                src_ref=wt_ref.at[other(i)], dst_ref=wbuf.at[:, core, :, kat],
                send_sem=wsend_sem, recv_sem=wrecv_sem,
                device_id=(other(i), 2 * x + goal), device_id_type=MESH,
            ).start()

    def slots(kind, dp):
        return pl.ds(dp * SIDE + 1, 3)

    def side_full(colour, kind, dp, step):
        way = (1 - step) // 2
        return pltpu.make_async_remote_copy(
            src_ref=xbuf.at[colour, slots(kind, dp), :, pl.ds(DIRECT, 256)],
            dst_ref=sbuf.at[colour, 2 * way, slots(kind, dp)],
            send_sem=side_send.at[colour], recv_sem=side_recv.at[colour, kind, dp, way],
            device_id=(me, 2 * lax.rem(x + step + SIDE, SIDE) + core), device_id_type=MESH,
        )

    def side_relay(colour, kind, dp, step):
        way = (1 - step) // 2
        rows = pl.ds(64 * way, 64)
        return pltpu.make_async_remote_copy(
            src_ref=sbuf.at[colour, 2 * way, slots(kind, dp), rows],
            dst_ref=sbuf.at[colour, 1, slots(kind, dp), rows],
            send_sem=side_send.at[colour], recv_sem=side_recv.at[colour, kind, dp, 2 + way],
            device_id=(me, 2 * lax.rem(x + step + SIDE, SIDE) + core), device_id_type=MESH,
        )

    def side_wait(colour, kind, dp, n):
        if n < 2:
            ref = sbuf.at[colour, 2 * n, slots(kind, dp)]
        else:
            ref = sbuf.at[colour, 1, slots(kind, dp), pl.ds(64 * (n - 2), 64)]
        pltpu.make_async_copy(ref, ref, side_recv.at[colour, kind, dp, n]).wait()

    def side_out(kind, dp):
        for colour in (0, 1):
            for step in (1, -1):
                side_full(colour, kind, dp, step).start()

    def side_on(kind, dp):
        for colour in (0, 1):
            for way in (0, 1):
                side_wait(colour, kind, dp, way)
                side_relay(colour, kind, dp, 1 - 2 * way).start()

    pbuf[...] = jnp.zeros_like(pbuf)
    ring_first(send, arrived)
    for dp, half in ((1, 0), (3, 1)):
        for colour in (0, 1):
            extra_wait(colour, dp, half)
            extra_out(colour, dp, half, 1 if dp == 1 else -1)

    def lane_sum(tile):
        total = jnp.zeros((NEW, NEW), jnp.float32)
        for k in range(2 * HALF // 512):
            value = tile(hid_ref[:, 512 * k:512 * (k + 1)].astype(jnp.float32))
            for n in range(4):
                total += value[:, NEW * n:NEW * (n + 1)]
        return jnp.sum(total, axis=1, keepdims=True) * (1.0 / (2 * HALF))

    mean = lane_sum(lambda value: value)
    scatter = lax.rsqrt(lane_sum(lambda value: jnp.square(value - mean)) + 1e-05)
    lane = lax.broadcasted_iota(jnp.int32, (NEW, NEW), 1)
    stat_ref[...] = jnp.where(lane == 0, mean, jnp.where(lane == 1, scatter, 0.0)).T[0:8]
    bturn[...] = jnp.broadcast_to(ub_in[...][None, :], (8, PART)).T
    ub_ref[...] = jnp.broadcast_to(
        bturn[pl.ds(pl.multiple_of(96 * me, 8), 96), 0:1], (96, NEW))

    def turn(src, count):
        @pl.loop(0, count)
        def _(k):
            at = pl.ds(pl.multiple_of(k * NEW, NEW), NEW)
            wturn[at, :] = src[:, at].astype(jnp.float32).T

    turn(wq_ref, 9)

    @pl.loop(0, 16)
    def _(r):
        block = wturn[pl.ds(pl.multiple_of(72 * r, 8), 72), :]
        wt_ref[r, 0] = jnp.concatenate(
            [block, jnp.zeros((24, 384), jnp.float32)], axis=0).astype(jnp.bfloat16)

    turn(wu_ref, 12)

    @pl.loop(0, 16)
    def _(r):
        wt_ref[r, 1] = wturn[pl.ds(pl.multiple_of(96 * r, 8), 96), :].astype(jnp.bfloat16)

    @pl.loop(1, 16)
    def _(i):
        pltpu.make_async_remote_copy(
            src_ref=stat_ref, dst_ref=stats.at[me], send_sem=stat_send, recv_sem=stat_recv,
            device_id=(other(i), 2 * x + core), device_id_type=MESH,
        ).start()
    pltpu.make_async_copy(stat_ref, stats.at[me], stat_recv).start()
    bias_own = pltpu.make_async_copy(ub_ref, bbuf.at[core], bias_sem.at[0])
    bias_mate = pltpu.make_async_remote_copy(
        src_ref=ub_ref, dst_ref=bbuf.at[core], send_sem=bias_sem.at[1], recv_sem=bias_sem.at[2],
        device_id=(me, 2 * x + mate), device_id_type=MESH,
    )
    bias_own.start()
    bias_mate.start()

    @pl.when(goal != core)
    def _():
        mate_w().start()

    @pl.when(goal == core)
    def _():
        pltpu.make_async_copy(wt_ref.at[me], wbuf.at[:, core, :, kat], wrecv_sem).start()


    def origin(colour, dp, ds):
        dy = colour * dp + (1 - colour) * ds
        dz = colour * ds + (1 - colour) * dp
        return lax.rem(y - dy + SIDE, SIDE) * SIDE + lax.rem(z - dz + SIDE, SIDE)

    def norm(colour, dp, pieces):
        base = core * HALF + colour * PART

        @pl.loop(0, SIDE)
        def _(ds):
            turned = stats[origin(colour, dp, ds)].T
            center, spread = turned[:, 0:1], turned[:, 1:2]
            rows = pl.ds(pl.multiple_of(ds * NEW, NEW), NEW)
            for raw, lane, width in pieces(colour, dp * SIDE + ds):
                value = (raw.astype(jnp.float32) - center) * spread
                at = pl.ds(pl.multiple_of(base + lane, 256), width)
                to = pl.ds(pl.multiple_of(lane, 256), width)
                for kind, (gain, shift) in enumerate(((gain0, gain1), (gain2, gain3))):
                    nbuf[colour, dp, kind, rows, to] = (
                        value * gain[:, at] + shift[:, at]
                    ).astype(jnp.bfloat16)

    def side_lane(dx):
        return DIRECT + 256 * lax.rem(x - dx + SIDE, SIDE)

    def early(colour, s):
        yield xbuf[colour, s, :, 0:DIRECT], 0, DIRECT
        yield xbuf[colour, s, :, DIRECT:DIRECT + 256], DIRECT + 256 * x, 256
        for dx in (1, 3):
            yield sbuf[colour, dx - 1, s], side_lane(dx), 256

    def late(colour, s):
        yield sbuf[colour, 1, s], side_lane(2), 256

    def compute(colour, dp):
        norm(colour, dp, late)
        for kind in (0, 1):
            left = wbuf[kind, :, :, pl.ds(pl.multiple_of(colour * PART, PART), PART)]
            product = lax.dot_general(
                left.reshape(192, PART), nbuf[colour, dp, kind], NT,
                preferred_element_type=jnp.float32,
            )
            for ds in range(SIDE):
                row = origin(colour, dp, ds)
                pbuf[row, 192 * kind:192 * (kind + 1), :] += product[:, ds * NEW:(ds + 1) * NEW]

    for i in range(SIDE):
        ring_second(send, arrived, i)
        side_out(1, gray(i))

    weights_out(1, 15)
    pltpu.make_async_copy(stats, stats, stat_recv).wait()
    for dp, half in FIRST[2:]:
        for colour in (0, 1):
            extra_wait(colour, dp, half)

    @pl.loop(0, SIDE)
    def _(i):
        side_on(1, gray(i))

        @pl.loop(0, 2)
        def _(colour):
            norm(colour, gray(i), early)

    pltpu.make_async_copy(wbuf, wbuf, wrecv_sem).wait()

    def pair_out(last):
        @pl.loop(0, 16)
        def _(j):
            dy, dz = j // SIDE, j % SIDE
            row = origin(0, dz, dy)
            final = jnp.logical_or(dy == 2, dz == 2)

            @pl.when(jnp.logical_and(row // 8 != core, final == last))
            def _():
                pltpu.make_async_remote_copy(
                    src_ref=pbuf.at[row], dst_ref=rbuf.at[lax.rem(row, 8)],
                    send_sem=pair_sem.at[0], recv_sem=pair_sem.at[1],
                    device_id=(me, 2 * x + mate), device_id_type=MESH,
                ).start()


    @pl.loop(0, SIDE)
    def _(i):
        dp = gray(i)
        for colour in (0, 1):
            for n in (2, 3):
                side_wait(colour, 1, dp, n)

        @pl.loop(0, 2)
        def _(colour):
            compute(colour, dp)

        @pl.when(i >= 2)
        def _():
            pair_out(i == 3)

    bias_own.wait()
    bias_mate.wait()
    pltpu.make_async_copy(rbuf, rbuf, pair_sem.at[1]).wait()
    mine = pl.ds(pl.multiple_of(me * 72, 8), 72)

    @pl.loop(0, 8)
    def _(q):
        row = 8 * core + q
        total = pbuf[row] + rbuf[q]
        for h in (0, 1):
            qsend[2 * q + h] = total[96 * h:96 * h + 72]
            remote = pltpu.make_async_remote_copy(
                src_ref=qsend.at[2 * q + h], dst_ref=qrecv.at[mine],
                send_sem=qsend_sem, recv_sem=qrecv_sem,
                device_id=(row, 2 * x + h), device_id_type=MESH,
            )
            away = jnp.logical_or(row != me, core != h)

            @pl.when(away)
            def _():
                remote.start()

            @pl.when(jnp.logical_not(away))
            def _():
                pltpu.make_async_copy(qsend.at[2 * q + h], qrecv.at[mine], qrecv_sem).start()
        at = pl.ds(pl.multiple_of(q * NEW, NEW), NEW)
        for h in (0, 1):
            u = total[192 + 96 * h:288 + 96 * h] + bbuf[h]
            inner = 0.7978845608028654 * (u + 0.044715 * (u * u * u))
            units_ref[h, :, at] = (0.5 * u * (1.0 + jnp.tanh(inner))).astype(jnp.bfloat16)

    pltpu.make_async_copy(qrecv, qrecv, qrecv_sem).wait()
    qkv_ref[...] = qrecv[...]
    some = pbuf.at[pl.ds(0, 8)]
    pltpu.make_async_copy(some, some, pair_sem.at[0]).wait()

    @pl.when(goal == core)
    def _():
        some = qsend.at[pl.ds(0, 15)]
        pltpu.make_async_copy(some, some, qsend_sem).wait()

    @pl.when(goal != core)
    def _():
        pltpu.make_async_copy(qsend, qsend, qsend_sem).wait()
        mate_w().wait_send()

    some = wt_ref.at[pl.ds(0, 15)]
    pltpu.make_async_copy(some, some, wsend_sem).wait()
    for colour in (0, 1):
        some = xbuf.at[colour, pl.ds(1, 15)]
        pltpu.make_async_copy(some, some, xsend_sem.at[colour]).wait()
        some = sbuf.at[colour, :, pl.ds(4, 12)]
        pltpu.make_async_copy(some, some, side_send.at[colour]).wait()
        some = sbuf.at[colour, :, pl.ds(1, 3)]
        pltpu.make_async_copy(some, some, extra_send.at[colour]).wait()
    some = stats.at[pl.ds(0, 15)]
    pltpu.make_async_copy(some, some, stat_send).wait()


def front(hidden, gains, qkv_weight, up_weight, up_bias):
    vmem = pl.BlockSpec(memory_space=pltpu.VMEM)
    hbm = pl.BlockSpec(memory_space=pl.ANY)
    dma = pltpu.SemaphoreType.DMA
    return pl.pallas_call(
        front_kernel,
        out_shape=(
            jax.ShapeDtypeStruct((1152, NEW), jnp.float32),
            jax.ShapeDtypeStruct((2, 96, 1024), jnp.bfloat16),
        ),
        in_specs=[vmem] * 8,
        out_specs=(vmem, vmem),
        scratch_shapes=[
            pltpu.VMEM((PART, 384), jnp.float32),
            pltpu.VMEM((16, 2, 96, 384), jnp.bfloat16),
            pltpu.VMEM((8, NEW), jnp.float32),
            pltpu.VMEM((PART, 8), jnp.float32),
            pltpu.VMEM((96, NEW), jnp.float32),
            pltpu.VMEM((2, 16, NEW, DIRECT + 256), jnp.bfloat16),
            pltpu.VMEM((2, 3, 16, NEW, 256), jnp.bfloat16),
            pltpu.VMEM((16, 8, NEW), jnp.float32),
            pltpu.VMEM((2, 2, 96, HALF), jnp.bfloat16),
            pltpu.VMEM((2, SIDE, 2, 512, PART), jnp.bfloat16),
            pltpu.VMEM((16, 384, NEW), jnp.float32),
            pltpu.VMEM((8, 384, NEW), jnp.float32),
            pltpu.VMEM((2, 96, NEW), jnp.float32),
            pltpu.VMEM((16, 72, NEW), jnp.float32),
            pltpu.VMEM((1152, NEW), jnp.float32),
            dma((2,)), dma((2, 2, 16)), dma((2, 5)), dma((2,)), dma((2, 2, 4, 4)), dma, dma,
            dma, dma, dma, dma((3,)), dma((2,)), dma, dma, dma((2,)), dma((2, 2, 4)),
        ],
        compiler_params=pltpu.CompilerParams(
            collective_id=0, has_side_effects=True, vmem_limit_bytes=VMEM_LIMIT
        ),
        name="front",
    )(hidden, qkv_weight, up_weight, *(gain[None, :] for gain in gains), up_bias)


def back_kernel(
    len_ref, units_ref, qkv_ref, qbias_ref, cos_ref, sin_ref, k_hbm, v_hbm,
    wd_ref, wo_ref, rest_ref, bias_ref, out_ref, nk_ref, nv_ref,
    ubuf, aring, amate, dbuf, obuf, dturn, total, tsend, rsum, share, rest, fout,
    kbuf, vbuf, sbuf, qexp, vkeep, att_ref, ksem, vsem,
    usend_sem, urecv_sem, own_sem, asend_sem, arecv_sem, amate_sem, w_sem,
    hsend_sem, hrecv_sem, rsend_sem, rrecv_sem, fsend_sem, frecv_sem, gsend_sem, grecv_sem, out_sem,
):
    for hbm, buf, sem in ((k_hbm, kbuf, ksem), (v_hbm, vbuf, vsem)):
        for n in range(CACHE // KB):
            fetch(n, hbm, buf, sem).start()
    y, z, x, core = place()
    me = y * SIDE + z
    mate = 1 - core
    goal = y // 2
    barrier = pltpu.get_barrier_semaphore()

    def plane(i):
        return (i // 2, 2 * x + i % 2)

    def line(i):
        return (me, i)

    meet(barrier, [
        (32, plane, lambda i: i != 2 * me + core),
        (8, line, lambda i: i // 2 != x),
    ])
    pl.semaphore_wait(barrier, 37)

    def apart(s, colour, half):
        return aring.at[s, pl.ds(32 * (2 * colour + half), 32)]

    def aown(colour, half):
        return att_ref.at[pl.ds(32 * (2 * colour + half), 32)]

    asend, aarrived = ring_units(y, z, x, core, aown, Absolute(y, z), apart, asend_sem, arecv_sem)

    def lanes(colour, half):
        return pl.ds((2 * colour + half) * 256, 256)

    def part(s, colour, half):
        return ubuf.at[:, s, :, lanes(colour, half)]

    def own(colour, half):
        return units_ref.at[:, :, lanes(colour, half)]

    send, arrived = ring_units(y, z, x, core, own, Absolute(y, z), part, usend_sem, urecv_sem)
    ring_start(send)
    copies = [pltpu.make_async_copy(units_ref, ubuf.at[:, me], own_sem.at[0])]
    for n, (src, dst) in enumerate(((wd_ref, dbuf), (wo_ref, obuf))):
        copies.append(pltpu.make_async_copy(src, dst.at[core], w_sem.at[3 * n]))
        copies.append(pltpu.make_async_remote_copy(
            src_ref=src, dst_ref=dst.at[core], send_sem=w_sem.at[3 * n + 1],
            recv_sem=w_sem.at[3 * n + 2], device_id=(me, 2 * x + mate), device_id_type=MESH,
        ))
    for copy in copies:
        copy.start()
    slot = me % 8

    def tile(row):
        return rest_ref.at[
            pl.ds(pl.multiple_of(32 * x, 32), 32), pl.ds(pl.multiple_of(384 * row, 384), 384)
        ]

    @pl.when(goal == core)
    def _():
        @pl.loop(1, 16)
        def _(i):
            row = lax.rem(y + i // SIDE, SIDE) * SIDE + lax.rem(z + i % SIDE, SIDE)
            pltpu.make_async_remote_copy(
                src_ref=tile(row), dst_ref=rest.at[slot],
                send_sem=hsend_sem, recv_sem=hrecv_sem,
                device_id=(row, 2 * x + core), device_id_type=MESH,
            ).start()
        pltpu.make_async_copy(tile(me), rest.at[slot], hrecv_sem).start()

    heads = HEADS_HERE
    keep = (vkeep, qexp, sbuf)

    def key_block(n, at):
        fetch(n, k_hbm, kbuf, ksem).wait()
        return kbuf[at, :]

    def value_block(n, at):
        fetch(n, v_hbm, vbuf, vsem).wait()
        return vbuf[at, :]

    top = attention_scores(
        heads, len_ref[0], qkv_ref, qbias_ref, cos_ref, sin_ref, nk_ref, nv_ref, keep, key_block)
    ring_first(send, arrived)
    attention_mix(heads, top, keep, att_ref, value_block)
    att_own = pltpu.make_async_copy(att_ref, aring.at[me], own_sem.at[1])
    att_own.start()
    two_start(asend)
    for copy in copies:
        copy.wait()

    def turn(first, count):
        @pl.loop(first, first + count)
        def _(n):
            h, at = n // 12, pl.ds(pl.multiple_of((n % 12) * 128, 128), 128)
            dturn[h, :, at] = dbuf[h, at, :].T

    ring_second(send, arrived, 0)
    turn(0, 12)
    two_first(asend, aarrived)
    ring_second(send, arrived, 1)
    turn(12, 12)
    two_second(aarrived)
    att_own.wait()
    pair = pltpu.make_async_remote_copy(
        src_ref=aring.at[pl.ds(8 * mate, 8)], dst_ref=amate,
        send_sem=amate_sem.at[0], recv_sem=amate_sem.at[1],
        device_id=(me, 2 * x + mate), device_id_type=MESH,
    )
    pair.start()
    ring_second(send, arrived, 2)
    ring_second(send, arrived, 3)
    pair.wait_recv()

    def rcopy(q, step):
        to = lax.rem(x + step, SIDE)
        return pltpu.make_async_remote_copy(
            src_ref=tsend.at[q, pl.ds(pl.multiple_of(32 * to, 32), 32)],
            dst_ref=rsum.at[step - 1, q],
            send_sem=rsend_sem.at[step - 1], recv_sem=rrecv_sem.at[step - 1],
            device_id=(me, 2 * to + core), device_id_type=MESH,
        )

    @pl.loop(0, 4)
    def _(p):
        at = pl.ds(pl.multiple_of(2 * p * NEW, 2 * NEW), 2 * NEW)
        turned = jnp.zeros((384, 2 * NEW), jnp.float32)
        for h in (0, 1):
            turned += jnp.dot(
                dturn[h], ubuf[h, :, :, at].reshape(PART, 2 * NEW),
                preferred_element_type=jnp.float32,
            )
        for n in (0, 1):
            q = 2 * p + n
            value = turned[:, n * NEW:(n + 1) * NEW].T
            value += jnp.dot(
                aring[8 * core + q], obuf[core], preferred_element_type=jnp.float32
            ) + jnp.dot(amate[q], obuf[mate], preferred_element_type=jnp.float32)
            total[q] = value
            tsend[q] = value.astype(jnp.bfloat16)
        for n in (0, 1):
            for step in (2, 1, 3):
                rcopy(2 * p + n, step).start()

    pltpu.make_async_copy(rest, rest, hrecv_sem).wait()
    for step in (1, 3, 2):
        some = rsum.at[step - 1]
        pltpu.make_async_copy(some, some, rrecv_sem.at[step - 1]).wait()
    rows = pl.ds(pl.multiple_of(32 * x, 32), 32)
    mine = pl.ds(pl.multiple_of(384 * me, 384), 384)

    @pl.loop(0, 8)
    def _(q):
        value = total[q, rows, :] + rsum[0, q].astype(jnp.float32)
        value += rsum[1, q].astype(jnp.float32) + rsum[2, q].astype(jnp.float32)
        share[q] = (rest[q].astype(jnp.float32) + (value + bias_ref[...])).astype(jnp.bfloat16)
        row = 8 * core + q

        @pl.when(row != me)
        def _():
            pltpu.make_async_remote_copy(
                src_ref=share.at[q], dst_ref=fout.at[rows, mine],
                send_sem=fsend_sem, recv_sem=frecv_sem,
                device_id=(row, 2 * x + goal), device_id_type=MESH,
            ).start()

        @pl.when(row == me)
        def _():
            pltpu.make_async_copy(share.at[q], fout.at[rows, mine], frecv_sem).start()

    def piece(owner, c):
        return fout.at[
            pl.ds(pl.multiple_of(32 * owner, 32), 32), pl.ds(pl.multiple_of(c * HALF, HALF), HALF)
        ]

    def gcopy(step):
        to = lax.rem(x + step + SIDE, SIDE)
        way = (1 - step) // 2
        return pltpu.make_async_remote_copy(
            src_ref=piece(x, core), dst_ref=piece(x, core), send_sem=gsend_sem.at[0, way],
            recv_sem=grecv_sem.at[0, way], device_id=(me, 2 * to + core), device_id_type=MESH,
        )

    def strip(owner, way):
        return fout.at[
            pl.ds(pl.multiple_of(32 * owner + 16 * way, 16), 16),
            pl.ds(pl.multiple_of(core * HALF, HALF), HALF),
        ]

    def grelay(step):
        to = lax.rem(x + step + SIDE, SIDE)
        owner = lax.rem(x - step + SIDE, SIDE)
        way = (1 - step) // 2
        return pltpu.make_async_remote_copy(
            src_ref=strip(owner, way), dst_ref=strip(owner, way), send_sem=gsend_sem.at[0, 2 + way],
            recv_sem=grecv_sem.at[0, 2 + way], device_id=(me, 2 * to + core), device_id_type=MESH,
        )

    def pass_on(step):
        owner = lax.rem(x - step + SIDE, SIDE)
        return pltpu.make_async_remote_copy(
            src_ref=piece(owner, core), dst_ref=piece(owner, core), send_sem=gsend_sem.at[1, step],
            recv_sem=grecv_sem.at[1, step], device_id=(me, 2 * x + mate), device_id_type=MESH,
        )

    def landed(kind, n, ref):
        pltpu.make_async_copy(ref, ref, grecv_sem.at[kind, n]).wait()

    def owner_at(step):
        return lax.rem(x - step + SIDE, SIDE)

    store = []

    def out_copy(c, step):
        owner = owner_at(step)
        whose = core if c == 0 else mate
        dst = out_ref.at[
            pl.ds(pl.multiple_of(32 * owner, 32), 32),
            pl.ds(pl.multiple_of(whose * HALF, HALF), HALF),
        ]
        return pltpu.make_async_copy(piece(owner, whose), dst, out_sem.at[c, step])

    def put(c, step):
        out_copy(c, step).start()
        store.append((c, step))

    pltpu.make_async_copy(piece(x, core), piece(x, core), frecv_sem).wait()
    for step in (1, -1):
        gcopy(step).start()
    pass_on(0).start()
    put(0, 0)
    for step in (1, -1):
        landed(0, (1 - step) // 2, piece(owner_at(step), core))
        grelay(step).start()
        pass_on(step % SIDE).start()
        put(0, step % SIDE)
    landed(1, 0, piece(owner_at(0), mate))
    put(1, 0)
    for way in (0, 1):
        landed(0, 2 + way, strip(owner_at(2), way))
    pass_on(2).start()
    put(0, 2)
    for step in (1, 3, 2):
        landed(1, step, piece(owner_at(step), mate))
        put(1, step)
    for c, step in store:
        out_copy(c, step).wait()

    for step in (1, -1):
        gcopy(step).wait_send()
        grelay(step).wait_send()
    for step in (1, 2, 3):
        some = rsum.at[step - 1]
        pltpu.make_async_copy(some, some, rsend_sem.at[step - 1]).wait()
    for step in range(4):
        pass_on(step).wait_send()
    pair.wait_send()

    @pl.when(goal == core)
    def _():
        some = share.at[pl.ds(0, 7)]
        pltpu.make_async_copy(some, some, fsend_sem).wait()
        some = rest_ref.at[pl.ds(0, 32), pl.ds(0, 15 * 384)]
        pltpu.make_async_copy(some, some, hsend_sem).wait()

    @pl.when(goal != core)
    def _():
        pltpu.make_async_copy(share, share, fsend_sem).wait()

    for colour in (0, 1):
        some = ubuf.at[:, pl.ds(0, 15), :, pl.ds(512 * colour, 512)]
        pltpu.make_async_copy(some, some, usend_sem.at[colour]).wait()
        some = aring.at[pl.ds(0, 15), pl.ds(64 * colour, 64)]
        pltpu.make_async_copy(some, some, asend_sem.at[colour]).wait()


def back(units, qkv, qkv_bias, length, keys_old, values_old, hidden, out_weight, down_weight, bias_total):
    cosine, sine = rotation_tables(length[0])
    req = lax.axis_index("req")
    bias = lax.dynamic_slice_in_dim(bias_total, req * 384, 384, 0)[None, :]
    vmem = pl.BlockSpec(memory_space=pltpu.VMEM)
    hbm = pl.BlockSpec(memory_space=pl.ANY)
    dma = pltpu.SemaphoreType.DMA
    return pl.pallas_call(
        back_kernel,
        out_shape=(
            jax.ShapeDtypeStruct((NEW, 2 * HALF), jnp.bfloat16),
            jax.ShapeDtypeStruct((NEW, 384), jnp.bfloat16),
            jax.ShapeDtypeStruct((NEW, 384), jnp.bfloat16),
        ),
        in_specs=[
            pl.BlockSpec(memory_space=pltpu.SMEM), hbm, vmem, vmem, vmem, vmem, hbm, hbm,
            hbm, hbm, hbm, vmem,
        ],
        out_specs=(hbm, vmem, vmem),
        scratch_shapes=[
            pltpu.VMEM((2, 16, 96, 1024), jnp.bfloat16),
            pltpu.VMEM((16, NEW, 384), jnp.bfloat16),
            pltpu.VMEM((8, NEW, 384), jnp.bfloat16),
            pltpu.VMEM((2, PART, 384), jnp.bfloat16),
            pltpu.VMEM((2, 384, 384), jnp.bfloat16),
            pltpu.VMEM((2, 384, PART), jnp.bfloat16),
            pltpu.VMEM((8, NEW, 384), jnp.float32),
            pltpu.VMEM((8, NEW, 384), jnp.bfloat16),
            pltpu.VMEM((3, 8, 32, 384), jnp.bfloat16),
            pltpu.VMEM((8, 32, 384), jnp.bfloat16),
            pltpu.VMEM((8, 32, 384), jnp.bfloat16),
            pltpu.VMEM((NEW, 2 * HALF), jnp.bfloat16),
            pltpu.VMEM((CACHE, 384), jnp.bfloat16),
            pltpu.VMEM((CACHE, 384), jnp.bfloat16),
            pltpu.VMEM((HEADS_HERE * NEW, CACHE + NEW), jnp.float32),
            pltpu.VMEM((HEADS_HERE * NEW, 384), jnp.bfloat16),
            pltpu.VMEM((NEW, 384), jnp.bfloat16),
            pltpu.VMEM((NEW, 384), jnp.bfloat16),
            dma((CACHE // KB,)), dma((CACHE // KB,)),
            dma((2,)), dma((2, 2, 16)), dma((2,)), dma((2,)), dma((2, 2, 16)), dma((2,)), dma((6,)),
            dma, dma, dma((3,)), dma((3,)), dma, dma, dma((2, 4)), dma((2, 4)), dma((2, 4)),
        ],
        compiler_params=pltpu.CompilerParams(
            collective_id=1, has_side_effects=True, vmem_limit_bytes=VMEM_LIMIT
        ),
        name="back",
    )(length, units, qkv, qkv_bias, cosine, sine, keys_old, values_old,
      down_weight, out_weight, hidden, bias)


def body(
    hidden,
    attn_norm_gain,
    attn_norm_bias,
    mlp_norm_gain,
    mlp_norm_bias,
    qkv_weight,
    qkv_bias,
    out_weight,
    out_bias,
    up_weight,
    up_bias,
    down_weight,
    down_bias,
    cache_keys,
    cache_values,
    cached_len,
):
    gains = (attn_norm_gain, attn_norm_bias, mlp_norm_gain, mlp_norm_bias)
    qkv, units = front(hidden, gains, qkv_weight, up_weight, up_bias)
    result, key_rows, value_rows = back(
        units, qkv, qkv_bias, cached_len, cache_keys[0], cache_values[0],
        hidden, out_weight, down_weight, out_bias + down_bias,
    )
    return (result, key_rows[None], value_rows[None])


def solution(mesh):
    return jax.shard_map(
        body,
        mesh=mesh,
        in_specs=(
            P("req", None),
            P(),
            P(),
            P(),
            P(),
            P("req", "head"),
            P("head"),
            P("head", "req"),
            P(),
            P("req", "head"),
            P("head"),
            P("head", "req"),
            P(),
            P("req", None, "head"),
            P("req", None, "head"),
            P("req"),
        ),
        out_specs=(P("req", None), P("req", None, "head"), P("req", None, "head")),
        check_vma=False,
    )
```

```python
import functools
import math

import jax
import jax.numpy as jnp
from jax import lax
from jax.experimental import pallas as pl
from jax.experimental.pallas import tpu as pltpu
from jax.sharding import PartitionSpec as P

DH = 96
ROT = 24
NEW = 128
CACHE = 4096
KB = 512
NT = (((1,), (1,)), ((), ()))


def rotation_tables(length):
    position = length.astype(jnp.float32) + jnp.arange(NEW, dtype=jnp.float32)
    halfway = ROT // 2
    exponent = jnp.arange(halfway, dtype=jnp.float32) * (2.0 / ROT)
    frequency = jnp.power(10000.0, -exponent)
    angle = position[None, :] * frequency[:, None]
    cosine, sine = jnp.cos(angle), jnp.sin(angle)
    return jnp.concatenate([cosine, cosine], 0), jnp.concatenate([-sine, sine], 0)


def fetch(n, hbm, buf, sem):
    rows = pl.ds(pl.multiple_of(n * KB, KB), KB)
    return pltpu.make_async_copy(hbm.at[rows], buf.at[rows], sem.at[n])


def attention_scores(heads, length, qkv_ref, bias_ref, cos_ref, sin_ref, nk_ref, nv_ref, keep, key_block):
    scale = 1.0 / math.sqrt(DH)
    width = heads * DH
    vkeep, qexp, sbuf = keep
    cosine, sine = cos_ref[...], sin_ref[...]

    def turned(rows):
        low = rows[:ROT]
        swapped = jnp.concatenate([low[ROT // 2:], low[: ROT // 2]], axis=0)
        return jnp.concatenate([low * cosine + swapped * sine, rows[ROT:]], axis=0)

    bias = jnp.broadcast_to(bias_ref[...][None, :], (8, 3 * width)).T

    def block(j, part):
        first = (3 * j + part) * DH
        return qkv_ref[pl.ds(first, DH), :] + bias[first:first + DH, 0:1]

    queries = jnp.concatenate([turned(block(j, 0)) for j in range(heads)], 0).T.astype(jnp.bfloat16)
    keys = jnp.concatenate([turned(block(j, 1)) for j in range(heads)], 0).T.astype(jnp.bfloat16)
    values = jnp.concatenate([block(j, 2) for j in range(heads)], 0).T.astype(jnp.bfloat16)
    nk_ref[...] = keys
    nv_ref[...] = values
    vkeep[...] = values
    lane_head = lax.broadcasted_iota(jnp.int32, (NEW, width), 1) // DH
    for j in range(heads):
        qexp[pl.ds(j * NEW, NEW), :] = jnp.where(lane_head == j, queries, jnp.zeros_like(queries))
    rows = heads * NEW
    fresh = lax.dot_general(qexp[...], keys, NT, preferred_element_type=jnp.float32) * scale
    row_at = lax.broadcasted_iota(jnp.int32, (rows, NEW), 0) % NEW
    col_at = lax.broadcasted_iota(jnp.int32, (rows, NEW), 1)
    fresh = jnp.where(col_at <= row_at, fresh, -1e30)
    sbuf[:, CACHE:] = fresh

    def score(n, top):
        at = pl.ds(pl.multiple_of(n * KB, KB), KB)
        part = lax.dot_general(
            qexp[...], key_block(n, at), NT, preferred_element_type=jnp.float32) * scale
        col = lax.broadcasted_iota(jnp.int32, (rows, KB), 1) + n * KB
        part = jnp.where(col < length, part, -1e30)
        sbuf[:, at] = part
        for t in range(KB // NEW):
            top = jnp.maximum(top, part[:, t * NEW:(t + 1) * NEW])
        return top

    return lax.fori_loop(0, CACHE // KB, score, fresh)


def attention_mix(heads, top, keep, att_ref, value_block):
    width = heads * DH
    vkeep, _, sbuf = keep
    highest = jnp.max(top, axis=1, keepdims=True)
    fresh_weights = jnp.exp(sbuf[:, CACHE:] - highest)
    mixed = jnp.dot(
        fresh_weights.astype(jnp.bfloat16), vkeep[...], preferred_element_type=jnp.float32)

    def weigh(n, carry):
        mixed, total = carry
        at = pl.ds(pl.multiple_of(n * KB, KB), KB)
        weights = jnp.exp(sbuf[:, at] - highest)
        for t in range(KB // NEW):
            total = total + weights[:, t * NEW:(t + 1) * NEW]
        mixed = mixed + jnp.dot(
            weights.astype(jnp.bfloat16), value_block(n, at), preferred_element_type=jnp.float32)
        return mixed, total

    mixed, total = lax.fori_loop(0, CACHE // KB, weigh, (mixed, fresh_weights))
    total = jnp.sum(total, axis=1, keepdims=True)
    lane_head = lax.broadcasted_iota(jnp.int32, (NEW, width), 1) // DH
    out = jnp.zeros((NEW, width), jnp.float32)
    for j in range(heads):
        at = slice(j * NEW, (j + 1) * NEW)
        out = jnp.where(lane_head == j, mixed[at] / total[at], out)
    att_ref[...] = out.astype(jnp.bfloat16)


MESH = pl.DeviceIdType.MESH
SIDE = 4
HALF = 3072
PART = 1536
DIRECT = 512
HEADS_HERE = 4
VMEM_LIMIT = 62 * 2**20


def place():
    req, head = lax.axis_index("req"), lax.axis_index("head")
    return req // SIDE, req % SIDE, head // 2, head % 2


def meet(barrier, others):
    for count, target, alone in others:
        @pl.loop(0, count)
        def _(i):
            @pl.when(alone(i))
            def _():
                pl.semaphore_signal(barrier, inc=1, device_id=target(i), device_id_type=MESH)


def ring_units(y, z, x, core, own, slot, part, send_sem, recv_sem):
    def send(colour, dp, ds, half, along, step):
        to = [dp, ds]
        to[along] = (to[along] + step) % SIDE if isinstance(to[along], int) else lax.rem(
            to[along] + step + SIDE, SIDE)
        on_z = (colour == 0) == (along == 0)
        dev_y = y if on_z else lax.rem(y + step + SIDE, SIDE)
        dev_z = lax.rem(z + step + SIDE, SIDE) if on_z else z
        is_own = isinstance(dp, int) and isinstance(ds, int) and dp == 0 and ds == 0
        src = own(colour, half) if is_own else part(slot(colour, dp, ds, 0), colour, half)
        source = (colour, dp, ds)
        dst = part(slot(*source, 0), colour, half) if slot.absolute else part(
            slot(colour, to[0], to[1], 0), colour, half)
        return pltpu.make_async_remote_copy(
            src_ref=src, dst_ref=dst, send_sem=send_sem.at[colour],
            recv_sem=recv_sem.at[colour, half, to[0] * SIDE + to[1]],
            device_id=(dev_y * SIDE + dev_z, 2 * x + core), device_id_type=MESH,
        )

    def arrived(colour, dp, ds, half):
        ref = part(slot(colour, dp, ds, 0), colour, half)
        pltpu.make_async_copy(ref, ref, recv_sem.at[colour, half, dp * SIDE + ds]).wait()

    return send, arrived


FIRST = ((1, 0), (3, 1), (1, 1), (3, 0), (2, 0), (2, 1))


def ring_start(send):
    for along in (0, 1):
        for half in (0, 1):
            for colour in (0, 1):
                for step in (1, -1):
                    send(colour, 0, 0, half, along, step).start()


def ring_spread(send, dp):
    for half in (0, 1):
        for colour in (0, 1):
            for step in (1, -1):
                send(colour, dp, 0, half, 1, step).start()


def ring_first(send, arrived):
    for dp, half in FIRST:
        if (dp, half) == (2, 0):
            ring_spread(send, 1)
        for colour in (0, 1):
            arrived(colour, dp, 0, half)
            if (dp, half) in ((1, 0), (3, 1)):
                send(colour, dp, 0, half, 0, 1 if dp == 1 else -1).start()


def ring_second(send, arrived, i):
    dp = gray(i)
    for ds, half in FIRST:
        if (ds, half) == (2, 0) and i < 2:
            ring_spread(send, gray(i + 2))
        for colour in (0, 1):
            arrived(colour, dp, ds, half)
            if (ds, half) in ((1, 0), (3, 1)):
                send(colour, dp, ds, half, 1, 1 if ds == 1 else -1).start()


def two_start(send):
    for along in (0, 1):
        for half in (0, 1):
            for colour in (0, 1):
                for step in (1, -1, 2):
                    send(colour, 0, 0, half, along, step).start()


def two_first(send, arrived):
    for dp, half in FIRST:
        for colour in (0, 1):
            arrived(colour, dp, 0, half)
            for step in (1, -1, 2):
                send(colour, dp, 0, half, 1, step).start()


def two_second(arrived):
    for dp in (0, 1, 3, 2):
        for ds, half in FIRST:
            for colour in (0, 1):
                arrived(colour, dp, ds, half)


def gray(i):
    return i + (i // 2) * (1 - 2 * (i % 2))


class Relative:
    absolute = False

    def __call__(self, colour, dp, ds, _):
        return dp * SIDE + ds


class Absolute:
    absolute = True

    def __init__(self, y, z):
        self.y, self.z = y, z

    def __call__(self, colour, dp, ds, _):
        dy, dz = (ds, dp) if colour == 0 else (dp, ds)
        return lax.rem(self.y - dy + SIDE, SIDE) * SIDE + lax.rem(self.z - dz + SIDE, SIDE)


def front_kernel(
    hid_ref, wq_ref, wu_ref, gain0, gain1, gain2, gain3, ub_in, qkv_ref, units_ref,
    wturn, wt_ref, stat_ref, bturn, ub_ref, xbuf, sbuf, stats, wbuf, nbuf, pbuf, rbuf, bbuf, qsend, qrecv,
    xsend_sem, xrecv_sem, own_sem, side_send, side_recv, stat_send, stat_recv,
    wsend_sem, wrecv_sem, wself_sem, bias_sem, pair_sem, qsend_sem, qrecv_sem,
):
    y, z, x, core = place()
    me = y * SIDE + z
    mate = 1 - core
    own_copies = []
    for colour in (0, 1):
        base = core * HALF + colour * PART

        def take(lane, width, dst, n):
            at = pl.ds(pl.multiple_of(base + lane, 256), width)
            own_copies.append(
                pltpu.make_async_copy(hid_ref.at[:, at], dst, own_sem.at[colour, n]))

        take(0, DIRECT, xbuf.at[colour, 0, :, pl.ds(0, DIRECT)], 0)
        take(DIRECT + 256 * x, 256, xbuf.at[colour, 0, :, pl.ds(DIRECT, 256)], 1)
        for dx in (1, 2, 3):
            plane_at = lax.rem(x - dx + SIDE, SIDE)
            take(DIRECT + 256 * plane_at, 256, sbuf.at[colour, dx - 1, 0], 1 + dx)
    for copy in own_copies:
        copy.start()
    barrier = pltpu.get_barrier_semaphore()

    def plane(i):
        return (i // 2, 2 * x + i % 2)

    def line(i):
        return (me, i)

    meet(barrier, [
        (32, plane, lambda i: i != 2 * me + core),
        (8, line, lambda i: i // 2 != x),
    ])
    for copy in own_copies:
        copy.wait()
    pl.semaphore_wait(barrier, 37)

    goal = y // 2
    kat = pl.ds(pl.multiple_of(((y % 2) * SIDE + z) * 384, 384), 384)

    def part(s, colour, half):
        return xbuf.at[colour, s, pl.ds(64 * half, 64)]

    def own(colour, half):
        return part(0, colour, half)

    send, arrived = ring_units(y, z, x, core, own, Relative(), part, xsend_sem, xrecv_sem)
    ring_start(send)

    def other(i):
        return lax.rem(y + i // SIDE, SIDE) * SIDE + lax.rem(z + i % SIDE, SIDE)

    def mate_w():
        return pltpu.make_async_remote_copy(
            src_ref=wt_ref.at[me], dst_ref=wbuf.at[:, core, :, kat],
            send_sem=wself_sem, recv_sem=wrecv_sem,
            device_id=(me, 2 * x + mate), device_id_type=MESH,
        )

    def weights_out(first, count):
        @pl.loop(first, first + count)
        def _(i):
            pltpu.make_async_remote_copy(
                src_ref=wt_ref.at[other(i)], dst_ref=wbuf.at[:, core, :, kat],
                send_sem=wsend_sem, recv_sem=wrecv_sem,
                device_id=(other(i), 2 * x + goal), device_id_type=MESH,
            ).start()

    def slots(kind, dp):
        return pl.ds(dp * SIDE, 1) if kind == 0 else pl.ds(dp * SIDE + 1, 3)

    def side_full(colour, kind, dp, step):
        way = (1 - step) // 2
        return pltpu.make_async_remote_copy(
            src_ref=xbuf.at[colour, slots(kind, dp), :, pl.ds(DIRECT, 256)],
            dst_ref=sbuf.at[colour, 2 * way, slots(kind, dp)],
            send_sem=side_send.at[colour], recv_sem=side_recv.at[colour, kind, dp, way],
            device_id=(me, 2 * lax.rem(x + step + SIDE, SIDE) + core), device_id_type=MESH,
        )

    def side_relay(colour, kind, dp, step):
        way = (1 - step) // 2
        rows = pl.ds(64 * way, 64)
        return pltpu.make_async_remote_copy(
            src_ref=sbuf.at[colour, 2 * way, slots(kind, dp), rows],
            dst_ref=sbuf.at[colour, 1, slots(kind, dp), rows],
            send_sem=side_send.at[colour], recv_sem=side_recv.at[colour, kind, dp, 2 + way],
            device_id=(me, 2 * lax.rem(x + step + SIDE, SIDE) + core), device_id_type=MESH,
        )

    def side_wait(colour, kind, dp, n):
        if n < 2:
            ref = sbuf.at[colour, 2 * n, slots(kind, dp)]
        else:
            ref = sbuf.at[colour, 1, slots(kind, dp), pl.ds(64 * (n - 2), 64)]
        pltpu.make_async_copy(ref, ref, side_recv.at[colour, kind, dp, n]).wait()

    def side_out(kind, dp):
        for colour in (0, 1):
            for step in (1, -1):
                side_full(colour, kind, dp, step).start()

    def side_on(kind, dp):
        for colour in (0, 1):
            for way in (0, 1):
                side_wait(colour, kind, dp, way)
                side_relay(colour, kind, dp, 1 - 2 * way).start()

    pbuf[...] = jnp.zeros_like(pbuf)
    ring_first(send, arrived)
    for dp in (1, 3, 2):
        side_out(0, dp)

    def lane_sum(tile):
        total = jnp.zeros((NEW, NEW), jnp.float32)
        for k in range(2 * HALF // 512):
            value = tile(hid_ref[:, 512 * k:512 * (k + 1)].astype(jnp.float32))
            for n in range(4):
                total += value[:, NEW * n:NEW * (n + 1)]
        return jnp.sum(total, axis=1, keepdims=True) * (1.0 / (2 * HALF))

    mean = lane_sum(lambda value: value)
    scatter = lax.rsqrt(lane_sum(lambda value: jnp.square(value - mean)) + 1e-05)
    lane = lax.broadcasted_iota(jnp.int32, (NEW, NEW), 1)
    stat_ref[...] = jnp.where(lane == 0, mean, jnp.where(lane == 1, scatter, 0.0)).T[0:8]
    bturn[...] = jnp.broadcast_to(ub_in[...][None, :], (8, PART)).T
    ub_ref[...] = jnp.broadcast_to(
        bturn[pl.ds(pl.multiple_of(96 * me, 8), 96), 0:1], (96, NEW))

    def turn(src, count):
        @pl.loop(0, count)
        def _(k):
            at = pl.ds(pl.multiple_of(k * NEW, NEW), NEW)
            wturn[at, :] = src[:, at].astype(jnp.float32).T

    turn(wq_ref, 9)

    @pl.loop(0, 16)
    def _(r):
        block = wturn[pl.ds(pl.multiple_of(72 * r, 8), 72), :]
        wt_ref[r, 0] = jnp.concatenate(
            [block, jnp.zeros((24, 384), jnp.float32)], axis=0).astype(jnp.bfloat16)

    turn(wu_ref, 12)

    @pl.loop(0, 16)
    def _(r):
        wt_ref[r, 1] = wturn[pl.ds(pl.multiple_of(96 * r, 8), 96), :].astype(jnp.bfloat16)

    @pl.loop(1, 16)
    def _(i):
        pltpu.make_async_remote_copy(
            src_ref=stat_ref, dst_ref=stats.at[me], send_sem=stat_send, recv_sem=stat_recv,
            device_id=(other(i), 2 * x + core), device_id_type=MESH,
        ).start()
    pltpu.make_async_copy(stat_ref, stats.at[me], stat_recv).start()
    bias_own = pltpu.make_async_copy(ub_ref, bbuf.at[core], bias_sem.at[0])
    bias_mate = pltpu.make_async_remote_copy(
        src_ref=ub_ref, dst_ref=bbuf.at[core], send_sem=bias_sem.at[1], recv_sem=bias_sem.at[2],
        device_id=(me, 2 * x + mate), device_id_type=MESH,
    )
    bias_own.start()
    bias_mate.start()

    @pl.when(goal != core)
    def _():
        mate_w().start()

    @pl.when(goal == core)
    def _():
        pltpu.make_async_copy(wt_ref.at[me], wbuf.at[:, core, :, kat], wrecv_sem).start()


    def origin(colour, dp, ds):
        dy = colour * dp + (1 - colour) * ds
        dz = colour * ds + (1 - colour) * dp
        return lax.rem(y - dy + SIDE, SIDE) * SIDE + lax.rem(z - dz + SIDE, SIDE)

    def norm(colour, dp, pieces):
        base = core * HALF + colour * PART

        @pl.loop(0, SIDE)
        def _(ds):
            turned = stats[origin(colour, dp, ds)].T
            center, spread = turned[:, 0:1], turned[:, 1:2]
            rows = pl.ds(pl.multiple_of(ds * NEW, NEW), NEW)
            for raw, lane, width in pieces(colour, dp * SIDE + ds):
                value = (raw.astype(jnp.float32) - center) * spread
                at = pl.ds(pl.multiple_of(base + lane, 256), width)
                to = pl.ds(pl.multiple_of(lane, 256), width)
                for kind, (gain, shift) in enumerate(((gain0, gain1), (gain2, gain3))):
                    nbuf[colour, dp, kind, rows, to] = (
                        value * gain[:, at] + shift[:, at]
                    ).astype(jnp.bfloat16)

    def side_lane(dx):
        return DIRECT + 256 * lax.rem(x - dx + SIDE, SIDE)

    def early(colour, s):
        yield xbuf[colour, s, :, 0:DIRECT], 0, DIRECT
        yield xbuf[colour, s, :, DIRECT:DIRECT + 256], DIRECT + 256 * x, 256
        for dx in (1, 3):
            yield sbuf[colour, dx - 1, s], side_lane(dx), 256

    def late(colour, s):
        yield sbuf[colour, 1, s], side_lane(2), 256

    def compute(colour, dp):
        norm(colour, dp, late)
        for kind in (0, 1):
            left = wbuf[kind, :, :, pl.ds(pl.multiple_of(colour * PART, PART), PART)]
            product = lax.dot_general(
                left.reshape(192, PART), nbuf[colour, dp, kind], NT,
                preferred_element_type=jnp.float32,
            )
            for ds in range(SIDE):
                row = origin(colour, dp, ds)
                pbuf[row, 192 * kind:192 * (kind + 1), :] += product[:, ds * NEW:(ds + 1) * NEW]

    for i in range(SIDE):
        ring_second(send, arrived, i)
        side_out(1, gray(i))

    weights_out(1, 15)
    pltpu.make_async_copy(stats, stats, stat_recv).wait()
    for dp in (1, 3, 2):
        side_on(0, dp)

    @pl.loop(0, SIDE)
    def _(i):
        side_on(1, gray(i))

        @pl.loop(0, 2)
        def _(colour):
            norm(colour, gray(i), early)

    pltpu.make_async_copy(wbuf, wbuf, wrecv_sem).wait()

    def pair_out(last):
        @pl.loop(0, 16)
        def _(j):
            dy, dz = j // SIDE, j % SIDE
            row = origin(0, dz, dy)
            final = jnp.logical_or(dy == 2, dz == 2)

            @pl.when(jnp.logical_and(row // 8 != core, final == last))
            def _():
                pltpu.make_async_remote_copy(
                    src_ref=pbuf.at[row], dst_ref=rbuf.at[lax.rem(row, 8)],
                    send_sem=pair_sem.at[0], recv_sem=pair_sem.at[1],
                    device_id=(me, 2 * x + mate), device_id_type=MESH,
                ).start()


    @pl.loop(0, SIDE)
    def _(i):
        dp = gray(i)
        for colour in (0, 1):
            for n in (2, 3):
                side_wait(colour, 1, dp, n)

            @pl.when(i > 0)
            def _():
                for n in (2, 3):
                    side_wait(colour, 0, dp, n)

        @pl.loop(0, 2)
        def _(colour):
            compute(colour, dp)

        @pl.when(i >= 2)
        def _():
            pair_out(i == 3)

    bias_own.wait()
    bias_mate.wait()
    pltpu.make_async_copy(rbuf, rbuf, pair_sem.at[1]).wait()
    mine = pl.ds(pl.multiple_of(me * 72, 8), 72)

    @pl.loop(0, 8)
    def _(q):
        row = 8 * core + q
        total = pbuf[row] + rbuf[q]
        for h in (0, 1):
            qsend[2 * q + h] = total[96 * h:96 * h + 72]
            remote = pltpu.make_async_remote_copy(
                src_ref=qsend.at[2 * q + h], dst_ref=qrecv.at[mine],
                send_sem=qsend_sem, recv_sem=qrecv_sem,
                device_id=(row, 2 * x + h), device_id_type=MESH,
            )
            away = jnp.logical_or(row != me, core != h)

            @pl.when(away)
            def _():
                remote.start()

            @pl.when(jnp.logical_not(away))
            def _():
                pltpu.make_async_copy(qsend.at[2 * q + h], qrecv.at[mine], qrecv_sem).start()
        at = pl.ds(pl.multiple_of(q * NEW, NEW), NEW)
        for h in (0, 1):
            u = total[192 + 96 * h:288 + 96 * h] + bbuf[h]
            inner = 0.7978845608028654 * (u + 0.044715 * (u * u * u))
            units_ref[h, :, at] = (0.5 * u * (1.0 + jnp.tanh(inner))).astype(jnp.bfloat16)

    pltpu.make_async_copy(qrecv, qrecv, qrecv_sem).wait()
    qkv_ref[...] = qrecv[...]
    some = pbuf.at[pl.ds(0, 8)]
    pltpu.make_async_copy(some, some, pair_sem.at[0]).wait()

    @pl.when(goal == core)
    def _():
        some = qsend.at[pl.ds(0, 15)]
        pltpu.make_async_copy(some, some, qsend_sem).wait()

    @pl.when(goal != core)
    def _():
        pltpu.make_async_copy(qsend, qsend, qsend_sem).wait()
        mate_w().wait_send()

    some = wt_ref.at[pl.ds(0, 15)]
    pltpu.make_async_copy(some, some, wsend_sem).wait()
    for colour in (0, 1):
        some = xbuf.at[colour, pl.ds(1, 15)]
        pltpu.make_async_copy(some, some, xsend_sem.at[colour]).wait()
        some = sbuf.at[colour, :, pl.ds(1, 15)]
        pltpu.make_async_copy(some, some, side_send.at[colour]).wait()
    some = stats.at[pl.ds(0, 15)]
    pltpu.make_async_copy(some, some, stat_send).wait()


def front(hidden, gains, qkv_weight, up_weight, up_bias):
    vmem = pl.BlockSpec(memory_space=pltpu.VMEM)
    hbm = pl.BlockSpec(memory_space=pl.ANY)
    dma = pltpu.SemaphoreType.DMA
    return pl.pallas_call(
        front_kernel,
        out_shape=(
            jax.ShapeDtypeStruct((1152, NEW), jnp.float32),
            jax.ShapeDtypeStruct((2, 96, 1024), jnp.bfloat16),
        ),
        in_specs=[vmem] * 8,
        out_specs=(vmem, vmem),
        scratch_shapes=[
            pltpu.VMEM((PART, 384), jnp.float32),
            pltpu.VMEM((16, 2, 96, 384), jnp.bfloat16),
            pltpu.VMEM((8, NEW), jnp.float32),
            pltpu.VMEM((PART, 8), jnp.float32),
            pltpu.VMEM((96, NEW), jnp.float32),
            pltpu.VMEM((2, 16, NEW, DIRECT + 256), jnp.bfloat16),
            pltpu.VMEM((2, 3, 16, NEW, 256), jnp.bfloat16),
            pltpu.VMEM((16, 8, NEW), jnp.float32),
            pltpu.VMEM((2, 2, 96, HALF), jnp.bfloat16),
            pltpu.VMEM((2, SIDE, 2, 512, PART), jnp.bfloat16),
            pltpu.VMEM((16, 384, NEW), jnp.float32),
            pltpu.VMEM((8, 384, NEW), jnp.float32),
            pltpu.VMEM((2, 96, NEW), jnp.float32),
            pltpu.VMEM((16, 72, NEW), jnp.float32),
            pltpu.VMEM((1152, NEW), jnp.float32),
            dma((2,)), dma((2, 2, 16)), dma((2, 5)), dma((2,)), dma((2, 2, 4, 4)), dma, dma,
            dma, dma, dma, dma((3,)), dma((2,)), dma, dma,
        ],
        compiler_params=pltpu.CompilerParams(
            collective_id=0, has_side_effects=True, vmem_limit_bytes=VMEM_LIMIT
        ),
        name="front",
    )(hidden, qkv_weight, up_weight, *(gain[None, :] for gain in gains), up_bias)


def back_kernel(
    len_ref, units_ref, qkv_ref, qbias_ref, cos_ref, sin_ref, k_hbm, v_hbm,
    wd_ref, wo_ref, rest_ref, bias_ref, out_ref, nk_ref, nv_ref,
    ubuf, aring, amate, dbuf, obuf, dturn, total, tsend, rsum, share, rest, fout,
    kbuf, vbuf, sbuf, qexp, vkeep, att_ref, ksem, vsem,
    usend_sem, urecv_sem, own_sem, asend_sem, arecv_sem, amate_sem, w_sem,
    hsend_sem, hrecv_sem, rsend_sem, rrecv_sem, fsend_sem, frecv_sem, gsend_sem, grecv_sem,
):
    for hbm, buf, sem in ((k_hbm, kbuf, ksem), (v_hbm, vbuf, vsem)):
        for n in range(CACHE // KB):
            fetch(n, hbm, buf, sem).start()
    y, z, x, core = place()
    me = y * SIDE + z
    mate = 1 - core
    goal = y // 2
    barrier = pltpu.get_barrier_semaphore()

    def plane(i):
        return (i // 2, 2 * x + i % 2)

    def line(i):
        return (me, i)

    meet(barrier, [
        (32, plane, lambda i: i != 2 * me + core),
        (8, line, lambda i: i // 2 != x),
    ])
    pl.semaphore_wait(barrier, 37)

    def apart(s, colour, half):
        return aring.at[s, pl.ds(32 * (2 * colour + half), 32)]

    def aown(colour, half):
        return att_ref.at[pl.ds(32 * (2 * colour + half), 32)]

    asend, aarrived = ring_units(y, z, x, core, aown, Absolute(y, z), apart, asend_sem, arecv_sem)

    def lanes(colour, half):
        return pl.ds((2 * colour + half) * 256, 256)

    def part(s, colour, half):
        return ubuf.at[:, s, :, lanes(colour, half)]

    def own(colour, half):
        return units_ref.at[:, :, lanes(colour, half)]

    send, arrived = ring_units(y, z, x, core, own, Absolute(y, z), part, usend_sem, urecv_sem)
    ring_start(send)
    copies = [pltpu.make_async_copy(units_ref, ubuf.at[:, me], own_sem.at[0])]
    for n, (src, dst) in enumerate(((wd_ref, dbuf), (wo_ref, obuf))):
        copies.append(pltpu.make_async_copy(src, dst.at[core], w_sem.at[3 * n]))
        copies.append(pltpu.make_async_remote_copy(
            src_ref=src, dst_ref=dst.at[core], send_sem=w_sem.at[3 * n + 1],
            recv_sem=w_sem.at[3 * n + 2], device_id=(me, 2 * x + mate), device_id_type=MESH,
        ))
    for copy in copies:
        copy.start()
    slot = me % 8

    def tile(row):
        return rest_ref.at[
            pl.ds(pl.multiple_of(32 * x, 32), 32), pl.ds(pl.multiple_of(384 * row, 384), 384)
        ]

    @pl.when(goal == core)
    def _():
        @pl.loop(1, 16)
        def _(i):
            row = lax.rem(y + i // SIDE, SIDE) * SIDE + lax.rem(z + i % SIDE, SIDE)
            pltpu.make_async_remote_copy(
                src_ref=tile(row), dst_ref=rest.at[slot],
                send_sem=hsend_sem, recv_sem=hrecv_sem,
                device_id=(row, 2 * x + core), device_id_type=MESH,
            ).start()
        pltpu.make_async_copy(tile(me), rest.at[slot], hrecv_sem).start()

    heads = HEADS_HERE
    keep = (vkeep, qexp, sbuf)

    def key_block(n, at):
        fetch(n, k_hbm, kbuf, ksem).wait()
        return kbuf[at, :]

    def value_block(n, at):
        fetch(n, v_hbm, vbuf, vsem).wait()
        return vbuf[at, :]

    top = attention_scores(
        heads, len_ref[0], qkv_ref, qbias_ref, cos_ref, sin_ref, nk_ref, nv_ref, keep, key_block)
    ring_first(send, arrived)
    attention_mix(heads, top, keep, att_ref, value_block)
    att_own = pltpu.make_async_copy(att_ref, aring.at[me], own_sem.at[1])
    att_own.start()
    two_start(asend)
    for copy in copies:
        copy.wait()

    def turn(first, count):
        @pl.loop(first, first + count)
        def _(n):
            h, at = n // 12, pl.ds(pl.multiple_of((n % 12) * 128, 128), 128)
            dturn[h, :, at] = dbuf[h, at, :].T

    ring_second(send, arrived, 0)
    turn(0, 12)
    two_first(asend, aarrived)
    ring_second(send, arrived, 1)
    turn(12, 12)
    two_second(aarrived)
    att_own.wait()
    pair = pltpu.make_async_remote_copy(
        src_ref=aring.at[pl.ds(8 * mate, 8)], dst_ref=amate,
        send_sem=amate_sem.at[0], recv_sem=amate_sem.at[1],
        device_id=(me, 2 * x + mate), device_id_type=MESH,
    )
    pair.start()
    ring_second(send, arrived, 2)
    ring_second(send, arrived, 3)
    pair.wait_recv()

    def rcopy(q, step):
        to = lax.rem(x + step, SIDE)
        return pltpu.make_async_remote_copy(
            src_ref=tsend.at[q, pl.ds(pl.multiple_of(32 * to, 32), 32)],
            dst_ref=rsum.at[step - 1, q],
            send_sem=rsend_sem.at[step - 1], recv_sem=rrecv_sem.at[step - 1],
            device_id=(me, 2 * to + core), device_id_type=MESH,
        )

    @pl.loop(0, 4)
    def _(p):
        at = pl.ds(pl.multiple_of(2 * p * NEW, 2 * NEW), 2 * NEW)
        turned = jnp.zeros((384, 2 * NEW), jnp.float32)
        for h in (0, 1):
            turned += jnp.dot(
                dturn[h], ubuf[h, :, :, at].reshape(PART, 2 * NEW),
                preferred_element_type=jnp.float32,
            )
        for n in (0, 1):
            q = 2 * p + n
            value = turned[:, n * NEW:(n + 1) * NEW].T
            value += jnp.dot(
                aring[8 * core + q], obuf[core], preferred_element_type=jnp.float32
            ) + jnp.dot(amate[q], obuf[mate], preferred_element_type=jnp.float32)
            total[q] = value
            tsend[q] = value.astype(jnp.bfloat16)
        for n in (0, 1):
            for step in (2, 1, 3):
                rcopy(2 * p + n, step).start()

    pltpu.make_async_copy(rest, rest, hrecv_sem).wait()
    for step in (1, 3, 2):
        some = rsum.at[step - 1]
        pltpu.make_async_copy(some, some, rrecv_sem.at[step - 1]).wait()
    rows = pl.ds(pl.multiple_of(32 * x, 32), 32)
    mine = pl.ds(pl.multiple_of(384 * me, 384), 384)

    @pl.loop(0, 8)
    def _(q):
        value = total[q, rows, :] + rsum[0, q].astype(jnp.float32)
        value += rsum[1, q].astype(jnp.float32) + rsum[2, q].astype(jnp.float32)
        share[q] = (rest[q].astype(jnp.float32) + (value + bias_ref[...])).astype(jnp.bfloat16)
        row = 8 * core + q

        @pl.when(row != me)
        def _():
            pltpu.make_async_remote_copy(
                src_ref=share.at[q], dst_ref=fout.at[rows, mine],
                send_sem=fsend_sem, recv_sem=frecv_sem,
                device_id=(row, 2 * x + goal), device_id_type=MESH,
            ).start()

        @pl.when(row == me)
        def _():
            pltpu.make_async_copy(share.at[q], fout.at[rows, mine], frecv_sem).start()

    def piece(owner, c):
        return fout.at[
            pl.ds(pl.multiple_of(32 * owner, 32), 32), pl.ds(pl.multiple_of(c * HALF, HALF), HALF)
        ]

    def gcopy(step):
        to = lax.rem(x + step + SIDE, SIDE)
        way = (1 - step) // 2
        return pltpu.make_async_remote_copy(
            src_ref=piece(x, core), dst_ref=piece(x, core), send_sem=gsend_sem.at[0, way],
            recv_sem=grecv_sem.at[0, way], device_id=(me, 2 * to + core), device_id_type=MESH,
        )

    def strip(owner, way):
        return fout.at[
            pl.ds(pl.multiple_of(32 * owner + 16 * way, 16), 16),
            pl.ds(pl.multiple_of(core * HALF, HALF), HALF),
        ]

    def grelay(step):
        to = lax.rem(x + step + SIDE, SIDE)
        owner = lax.rem(x - step + SIDE, SIDE)
        way = (1 - step) // 2
        return pltpu.make_async_remote_copy(
            src_ref=strip(owner, way), dst_ref=strip(owner, way), send_sem=gsend_sem.at[0, 2 + way],
            recv_sem=grecv_sem.at[0, 2 + way], device_id=(me, 2 * to + core), device_id_type=MESH,
        )

    def pass_on(step):
        owner = lax.rem(x - step + SIDE, SIDE)
        return pltpu.make_async_remote_copy(
            src_ref=piece(owner, core), dst_ref=piece(owner, core), send_sem=gsend_sem.at[1, step],
            recv_sem=grecv_sem.at[1, step], device_id=(me, 2 * x + mate), device_id_type=MESH,
        )

    def landed(kind, n, ref):
        pltpu.make_async_copy(ref, ref, grecv_sem.at[kind, n]).wait()

    def owner_at(step):
        return lax.rem(x - step + SIDE, SIDE)

    pltpu.make_async_copy(piece(x, core), piece(x, core), frecv_sem).wait()
    for step in (1, -1):
        gcopy(step).start()
    pass_on(0).start()
    for step in (1, -1):
        landed(0, (1 - step) // 2, piece(owner_at(step), core))
        grelay(step).start()
        pass_on(step % SIDE).start()
    for way in (0, 1):
        landed(0, 2 + way, strip(owner_at(2), way))
    pass_on(2).start()
    for step in (0, 1, 3, 2):
        landed(1, step, piece(owner_at(step), mate))
    out_ref[...] = fout[...]

    for step in (1, -1):
        gcopy(step).wait_send()
        grelay(step).wait_send()
    for step in (1, 2, 3):
        some = rsum.at[step - 1]
        pltpu.make_async_copy(some, some, rsend_sem.at[step - 1]).wait()
    for step in range(4):
        pass_on(step).wait_send()
    pair.wait_send()

    @pl.when(goal == core)
    def _():
        some = share.at[pl.ds(0, 7)]
        pltpu.make_async_copy(some, some, fsend_sem).wait()
        some = rest_ref.at[pl.ds(0, 32), pl.ds(0, 15 * 384)]
        pltpu.make_async_copy(some, some, hsend_sem).wait()

    @pl.when(goal != core)
    def _():
        pltpu.make_async_copy(share, share, fsend_sem).wait()

    for colour in (0, 1):
        some = ubuf.at[:, pl.ds(0, 15), :, pl.ds(512 * colour, 512)]
        pltpu.make_async_copy(some, some, usend_sem.at[colour]).wait()
        some = aring.at[pl.ds(0, 15), pl.ds(64 * colour, 64)]
        pltpu.make_async_copy(some, some, asend_sem.at[colour]).wait()


def back(units, qkv, qkv_bias, length, keys_old, values_old, hidden, out_weight, down_weight, bias_total):
    cosine, sine = rotation_tables(length[0])
    req = lax.axis_index("req")
    bias = lax.dynamic_slice_in_dim(bias_total, req * 384, 384, 0)[None, :]
    vmem = pl.BlockSpec(memory_space=pltpu.VMEM)
    hbm = pl.BlockSpec(memory_space=pl.ANY)
    dma = pltpu.SemaphoreType.DMA
    return pl.pallas_call(
        back_kernel,
        out_shape=(
            jax.ShapeDtypeStruct((NEW, 2 * HALF), jnp.bfloat16),
            jax.ShapeDtypeStruct((NEW, 384), jnp.bfloat16),
            jax.ShapeDtypeStruct((NEW, 384), jnp.bfloat16),
        ),
        in_specs=[
            pl.BlockSpec(memory_space=pltpu.SMEM), hbm, vmem, vmem, vmem, vmem, hbm, hbm,
            hbm, hbm, hbm, vmem,
        ],
        out_specs=(vmem, vmem, vmem),
        scratch_shapes=[
            pltpu.VMEM((2, 16, 96, 1024), jnp.bfloat16),
            pltpu.VMEM((16, NEW, 384), jnp.bfloat16),
            pltpu.VMEM((8, NEW, 384), jnp.bfloat16),
            pltpu.VMEM((2, PART, 384), jnp.bfloat16),
            pltpu.VMEM((2, 384, 384), jnp.bfloat16),
            pltpu.VMEM((2, 384, PART), jnp.bfloat16),
            pltpu.VMEM((8, NEW, 384), jnp.float32),
            pltpu.VMEM((8, NEW, 384), jnp.bfloat16),
            pltpu.VMEM((3, 8, 32, 384), jnp.bfloat16),
            pltpu.VMEM((8, 32, 384), jnp.bfloat16),
            pltpu.VMEM((8, 32, 384), jnp.bfloat16),
            pltpu.VMEM((NEW, 2 * HALF), jnp.bfloat16),
            pltpu.VMEM((CACHE, 384), jnp.bfloat16),
            pltpu.VMEM((CACHE, 384), jnp.bfloat16),
            pltpu.VMEM((HEADS_HERE * NEW, CACHE + NEW), jnp.float32),
            pltpu.VMEM((HEADS_HERE * NEW, 384), jnp.bfloat16),
            pltpu.VMEM((NEW, 384), jnp.bfloat16),
            pltpu.VMEM((NEW, 384), jnp.bfloat16),
            dma((CACHE // KB,)), dma((CACHE // KB,)),
            dma((2,)), dma((2, 2, 16)), dma((2,)), dma((2,)), dma((2, 2, 16)), dma((2,)), dma((6,)),
            dma, dma, dma((3,)), dma((3,)), dma, dma, dma((2, 4)), dma((2, 4)),
        ],
        compiler_params=pltpu.CompilerParams(
            collective_id=1, has_side_effects=True, vmem_limit_bytes=VMEM_LIMIT
        ),
        name="back",
    )(length, units, qkv, qkv_bias, cosine, sine, keys_old, values_old,
      down_weight, out_weight, hidden, bias)


def body(
    hidden,
    attn_norm_gain,
    attn_norm_bias,
    mlp_norm_gain,
    mlp_norm_bias,
    qkv_weight,
    qkv_bias,
    out_weight,
    out_bias,
    up_weight,
    up_bias,
    down_weight,
    down_bias,
    cache_keys,
    cache_values,
    cached_len,
):
    gains = (attn_norm_gain, attn_norm_bias, mlp_norm_gain, mlp_norm_bias)
    qkv, units = front(hidden, gains, qkv_weight, up_weight, up_bias)
    result, key_rows, value_rows = back(
        units, qkv, qkv_bias, cached_len, cache_keys[0], cache_values[0],
        hidden, out_weight, down_weight, out_bias + down_bias,
    )
    return (result, key_rows[None], value_rows[None])


def solution(mesh):
    return jax.shard_map(
        body,
        mesh=mesh,
        in_specs=(
            P("req", None),
            P(),
            P(),
            P(),
            P(),
            P("req", "head"),
            P("head"),
            P("head", "req"),
            P(),
            P("req", "head"),
            P("head"),
            P("head", "req"),
            P(),
            P("req", None, "head"),
            P("req", None, "head"),
            P("req"),
        ),
        out_specs=(P("req", None), P("req", None, "head"), P("req", None, "head")),
        check_vma=False,
    )
```

```python
import functools
import math

import jax
import jax.numpy as jnp
from jax import lax
from jax.experimental import pallas as pl
from jax.experimental.pallas import tpu as pltpu
from jax.sharding import PartitionSpec as P

DH = 96
ROT = 24
NEW = 128
CACHE = 4096
KB = 512
NT = (((1,), (1,)), ((), ()))


def rotation_tables(length):
    position = length.astype(jnp.float32) + jnp.arange(NEW, dtype=jnp.float32)
    halfway = ROT // 2
    exponent = jnp.arange(halfway, dtype=jnp.float32) * (2.0 / ROT)
    frequency = jnp.power(10000.0, -exponent)
    angle = position[None, :] * frequency[:, None]
    cosine, sine = jnp.cos(angle), jnp.sin(angle)
    return jnp.concatenate([cosine, cosine], 0), jnp.concatenate([-sine, sine], 0)


def fetch(n, hbm, buf, sem):
    rows = pl.ds(pl.multiple_of(n * KB, KB), KB)
    return pltpu.make_async_copy(hbm.at[rows], buf.at[rows], sem.at[n])


def attention_scores(heads, length, qkv_ref, bias_ref, cos_ref, sin_ref, nk_ref, nv_ref, keep, key_block):
    scale = 1.0 / math.sqrt(DH)
    width = heads * DH
    vkeep, qexp, sbuf = keep
    cosine, sine = cos_ref[...], sin_ref[...]

    def turned(rows):
        low = rows[:ROT]
        swapped = jnp.concatenate([low[ROT // 2:], low[: ROT // 2]], axis=0)
        return jnp.concatenate([low * cosine + swapped * sine, rows[ROT:]], axis=0)

    bias = jnp.broadcast_to(bias_ref[...][None, :], (8, 3 * width)).T

    def block(j, part):
        first = (3 * j + part) * DH
        return qkv_ref[pl.ds(first, DH), :] + bias[first:first + DH, 0:1]

    queries = jnp.concatenate([turned(block(j, 0)) for j in range(heads)], 0).T.astype(jnp.bfloat16)
    keys = jnp.concatenate([turned(block(j, 1)) for j in range(heads)], 0).T.astype(jnp.bfloat16)
    values = jnp.concatenate([block(j, 2) for j in range(heads)], 0).T.astype(jnp.bfloat16)
    nk_ref[...] = keys
    nv_ref[...] = values
    vkeep[...] = values
    lane_head = lax.broadcasted_iota(jnp.int32, (NEW, width), 1) // DH
    for j in range(heads):
        qexp[pl.ds(j * NEW, NEW), :] = jnp.where(lane_head == j, queries, jnp.zeros_like(queries))
    rows = heads * NEW
    fresh = lax.dot_general(qexp[...], keys, NT, preferred_element_type=jnp.float32) * scale
    row_at = lax.broadcasted_iota(jnp.int32, (rows, NEW), 0) % NEW
    col_at = lax.broadcasted_iota(jnp.int32, (rows, NEW), 1)
    fresh = jnp.where(col_at <= row_at, fresh, -1e30)
    sbuf[:, CACHE:] = fresh

    def score(n, top):
        at = pl.ds(pl.multiple_of(n * KB, KB), KB)
        part = lax.dot_general(
            qexp[...], key_block(n, at), NT, preferred_element_type=jnp.float32) * scale
        col = lax.broadcasted_iota(jnp.int32, (rows, KB), 1) + n * KB
        part = jnp.where(col < length, part, -1e30)
        sbuf[:, at] = part
        for t in range(KB // NEW):
            top = jnp.maximum(top, part[:, t * NEW:(t + 1) * NEW])
        return top

    return lax.fori_loop(0, CACHE // KB, score, fresh)


def attention_mix(heads, top, keep, att_ref, value_block):
    width = heads * DH
    vkeep, _, sbuf = keep
    highest = jnp.max(top, axis=1, keepdims=True)
    fresh_weights = jnp.exp(sbuf[:, CACHE:] - highest)
    mixed = jnp.dot(
        fresh_weights.astype(jnp.bfloat16), vkeep[...], preferred_element_type=jnp.float32)

    def weigh(n, carry):
        mixed, total = carry
        at = pl.ds(pl.multiple_of(n * KB, KB), KB)
        weights = jnp.exp(sbuf[:, at] - highest)
        for t in range(KB // NEW):
            total = total + weights[:, t * NEW:(t + 1) * NEW]
        mixed = mixed + jnp.dot(
            weights.astype(jnp.bfloat16), value_block(n, at), preferred_element_type=jnp.float32)
        return mixed, total

    mixed, total = lax.fori_loop(0, CACHE // KB, weigh, (mixed, fresh_weights))
    total = jnp.sum(total, axis=1, keepdims=True)
    lane_head = lax.broadcasted_iota(jnp.int32, (NEW, width), 1) // DH
    out = jnp.zeros((NEW, width), jnp.float32)
    for j in range(heads):
        at = slice(j * NEW, (j + 1) * NEW)
        out = jnp.where(lane_head == j, mixed[at] / total[at], out)
    att_ref[...] = out.astype(jnp.bfloat16)


MESH = pl.DeviceIdType.MESH
SIDE = 4
HALF = 3072
PART = 1536
DIRECT = 512
HEADS_HERE = 4
VMEM_LIMIT = 62 * 2**20


def place():
    req, head = lax.axis_index("req"), lax.axis_index("head")
    return req // SIDE, req % SIDE, head // 2, head % 2


def meet(barrier, others):
    for count, target, alone in others:
        @pl.loop(0, count)
        def _(i):
            @pl.when(alone(i))
            def _():
                pl.semaphore_signal(barrier, inc=1, device_id=target(i), device_id_type=MESH)


def ring_units(y, z, x, core, own, slot, part, send_sem, recv_sem):
    def send(colour, dp, ds, half, along, step):
        to = [dp, ds]
        to[along] = (to[along] + step) % SIDE if isinstance(to[along], int) else lax.rem(
            to[along] + step + SIDE, SIDE)
        on_z = (colour == 0) == (along == 0)
        dev_y = y if on_z else lax.rem(y + step + SIDE, SIDE)
        dev_z = lax.rem(z + step + SIDE, SIDE) if on_z else z
        is_own = isinstance(dp, int) and isinstance(ds, int) and dp == 0 and ds == 0
        src = own(colour, half) if is_own else part(slot(colour, dp, ds, 0), colour, half)
        source = (colour, dp, ds)
        dst = part(slot(*source, 0), colour, half) if slot.absolute else part(
            slot(colour, to[0], to[1], 0), colour, half)
        return pltpu.make_async_remote_copy(
            src_ref=src, dst_ref=dst, send_sem=send_sem.at[colour],
            recv_sem=recv_sem.at[colour, half, to[0] * SIDE + to[1]],
            device_id=(dev_y * SIDE + dev_z, 2 * x + core), device_id_type=MESH,
        )

    def arrived(colour, dp, ds, half):
        ref = part(slot(colour, dp, ds, 0), colour, half)
        pltpu.make_async_copy(ref, ref, recv_sem.at[colour, half, dp * SIDE + ds]).wait()

    return send, arrived


FIRST = ((1, 0), (3, 1), (1, 1), (3, 0), (2, 0), (2, 1))


def ring_start(send):
    for along in (0, 1):
        for half in (0, 1):
            for colour in (0, 1):
                for step in (1, -1):
                    send(colour, 0, 0, half, along, step).start()


def ring_spread(send, dp):
    for half in (0, 1):
        for colour in (0, 1):
            for step in (1, -1):
                send(colour, dp, 0, half, 1, step).start()


def ring_first(send, arrived):
    for dp, half in FIRST:
        if (dp, half) == (2, 0):
            ring_spread(send, 1)
        for colour in (0, 1):
            arrived(colour, dp, 0, half)
            if (dp, half) in ((1, 0), (3, 1)):
                send(colour, dp, 0, half, 0, 1 if dp == 1 else -1).start()


def ring_second(send, arrived, i):
    dp = gray(i)
    for ds, half in FIRST:
        if (ds, half) == (2, 0) and i < 2:
            ring_spread(send, gray(i + 2))
        for colour in (0, 1):
            arrived(colour, dp, ds, half)
            if (ds, half) in ((1, 0), (3, 1)):
                send(colour, dp, ds, half, 1, 1 if ds == 1 else -1).start()


def two_start(send):
    for along in (0, 1):
        for half in (0, 1):
            for colour in (0, 1):
                for step in (1, -1, 2):
                    send(colour, 0, 0, half, along, step).start()


def two_first(send, arrived):
    for dp, half in FIRST:
        for colour in (0, 1):
            arrived(colour, dp, 0, half)
            for step in (1, -1, 2):
                send(colour, dp, 0, half, 1, step).start()


def two_second(arrived):
    for dp in (0, 1, 3, 2):
        for ds, half in FIRST:
            for colour in (0, 1):
                arrived(colour, dp, ds, half)


def gray(i):
    return i + (i // 2) * (1 - 2 * (i % 2))


class Relative:
    absolute = False

    def __call__(self, colour, dp, ds, _):
        return dp * SIDE + ds


class Absolute:
    absolute = True

    def __init__(self, y, z):
        self.y, self.z = y, z

    def __call__(self, colour, dp, ds, _):
        dy, dz = (ds, dp) if colour == 0 else (dp, ds)
        return lax.rem(self.y - dy + SIDE, SIDE) * SIDE + lax.rem(self.z - dz + SIDE, SIDE)


def front_kernel(
    hid_ref, wq_ref, wu_ref, gain0, gain1, gain2, gain3, ub_in, qkv_ref, units_ref,
    wturn, wt_ref, stat_ref, bturn, ub_ref, xbuf, sbuf, stats, wbuf, nbuf, pbuf, rbuf, bbuf, qsend, qrecv,
    xsend_sem, xrecv_sem, own_sem, side_send, side_recv, stat_send, stat_recv,
    wsend_sem, wrecv_sem, wself_sem, bias_sem, pair_sem, qsend_sem, qrecv_sem,
):
    y, z, x, core = place()
    me = y * SIDE + z
    mate = 1 - core
    own_copies = []
    for colour in (0, 1):
        base = core * HALF + colour * PART

        def take(lane, width, dst, n):
            at = pl.ds(pl.multiple_of(base + lane, 256), width)
            own_copies.append(
                pltpu.make_async_copy(hid_ref.at[:, at], dst, own_sem.at[colour, n]))

        take(0, DIRECT, xbuf.at[colour, 0, :, pl.ds(0, DIRECT)], 0)
        take(DIRECT + 256 * x, 256, xbuf.at[colour, 0, :, pl.ds(DIRECT, 256)], 1)
        for dx in (1, 2, 3):
            plane_at = lax.rem(x - dx + SIDE, SIDE)
            take(DIRECT + 256 * plane_at, 256, sbuf.at[colour, dx - 1, 0], 1 + dx)
    for copy in own_copies:
        copy.start()
    barrier = pltpu.get_barrier_semaphore()

    def plane(i):
        return (i // 2, 2 * x + i % 2)

    def line(i):
        return (me, i)

    meet(barrier, [
        (32, plane, lambda i: i != 2 * me + core),
        (8, line, lambda i: i // 2 != x),
    ])
    for copy in own_copies:
        copy.wait()
    pl.semaphore_wait(barrier, 37)

    goal = y // 2
    kat = pl.ds(pl.multiple_of(((y % 2) * SIDE + z) * 384, 384), 384)

    def part(s, colour, half):
        return xbuf.at[colour, s, pl.ds(64 * half, 64)]

    def own(colour, half):
        return part(0, colour, half)

    send, arrived = ring_units(y, z, x, core, own, Relative(), part, xsend_sem, xrecv_sem)
    ring_start(send)

    def other(i):
        return lax.rem(y + i // SIDE, SIDE) * SIDE + lax.rem(z + i % SIDE, SIDE)

    def mate_w():
        return pltpu.make_async_remote_copy(
            src_ref=wt_ref.at[me], dst_ref=wbuf.at[:, core, :, kat],
            send_sem=wself_sem, recv_sem=wrecv_sem,
            device_id=(me, 2 * x + mate), device_id_type=MESH,
        )

    def weights_out(first, count):
        @pl.loop(first, first + count)
        def _(i):
            pltpu.make_async_remote_copy(
                src_ref=wt_ref.at[other(i)], dst_ref=wbuf.at[:, core, :, kat],
                send_sem=wsend_sem, recv_sem=wrecv_sem,
                device_id=(other(i), 2 * x + goal), device_id_type=MESH,
            ).start()

    def slots(kind, dp):
        return pl.ds(dp * SIDE, 1) if kind == 0 else pl.ds(dp * SIDE + 1, 3)

    def side_full(colour, kind, dp, step):
        way = (1 - step) // 2
        return pltpu.make_async_remote_copy(
            src_ref=xbuf.at[colour, slots(kind, dp), :, pl.ds(DIRECT, 256)],
            dst_ref=sbuf.at[colour, 2 * way, slots(kind, dp)],
            send_sem=side_send.at[colour], recv_sem=side_recv.at[colour, kind, dp, way],
            device_id=(me, 2 * lax.rem(x + step + SIDE, SIDE) + core), device_id_type=MESH,
        )

    def side_relay(colour, kind, dp, step):
        way = (1 - step) // 2
        rows = pl.ds(64 * way, 64)
        return pltpu.make_async_remote_copy(
            src_ref=sbuf.at[colour, 2 * way, slots(kind, dp), rows],
            dst_ref=sbuf.at[colour, 1, slots(kind, dp), rows],
            send_sem=side_send.at[colour], recv_sem=side_recv.at[colour, kind, dp, 2 + way],
            device_id=(me, 2 * lax.rem(x + step + SIDE, SIDE) + core), device_id_type=MESH,
        )

    def side_wait(colour, kind, dp, n):
        if n < 2:
            ref = sbuf.at[colour, 2 * n, slots(kind, dp)]
        else:
            ref = sbuf.at[colour, 1, slots(kind, dp), pl.ds(64 * (n - 2), 64)]
        pltpu.make_async_copy(ref, ref, side_recv.at[colour, kind, dp, n]).wait()

    def side_out(kind, dp):
        for colour in (0, 1):
            for step in (1, -1):
                side_full(colour, kind, dp, step).start()

    def side_on(kind, dp):
        for colour in (0, 1):
            for way in (0, 1):
                side_wait(colour, kind, dp, way)
                side_relay(colour, kind, dp, 1 - 2 * way).start()

    pbuf[...] = jnp.zeros_like(pbuf)
    ring_first(send, arrived)
    for dp in (1, 3, 2):
        side_out(0, dp)

    def lane_sum(tile):
        total = jnp.zeros((NEW, NEW), jnp.float32)
        for k in range(2 * HALF // 512):
            value = tile(hid_ref[:, 512 * k:512 * (k + 1)].astype(jnp.float32))
            for n in range(4):
                total += value[:, NEW * n:NEW * (n + 1)]
        return jnp.sum(total, axis=1, keepdims=True) * (1.0 / (2 * HALF))

    mean = lane_sum(lambda value: value)
    scatter = lax.rsqrt(lane_sum(lambda value: jnp.square(value - mean)) + 1e-05)
    lane = lax.broadcasted_iota(jnp.int32, (NEW, NEW), 1)
    stat_ref[...] = jnp.where(lane == 0, mean, jnp.where(lane == 1, scatter, 0.0)).T[0:8]
    bturn[...] = jnp.broadcast_to(ub_in[...][None, :], (8, PART)).T
    ub_ref[...] = jnp.broadcast_to(
        bturn[pl.ds(pl.multiple_of(96 * me, 8), 96), 0:1], (96, NEW))

    def turn(src, count):
        @pl.loop(0, count)
        def _(k):
            at = pl.ds(pl.multiple_of(k * NEW, NEW), NEW)
            wturn[at, :] = src[:, at].astype(jnp.float32).T

    turn(wq_ref, 9)

    @pl.loop(0, 16)
    def _(r):
        block = wturn[pl.ds(pl.multiple_of(72 * r, 8), 72), :]
        wt_ref[r, 0] = jnp.concatenate(
            [block, jnp.zeros((24, 384), jnp.float32)], axis=0).astype(jnp.bfloat16)

    turn(wu_ref, 12)

    @pl.loop(0, 16)
    def _(r):
        wt_ref[r, 1] = wturn[pl.ds(pl.multiple_of(96 * r, 8), 96), :].astype(jnp.bfloat16)

    @pl.loop(1, 16)
    def _(i):
        pltpu.make_async_remote_copy(
            src_ref=stat_ref, dst_ref=stats.at[me], send_sem=stat_send, recv_sem=stat_recv,
            device_id=(other(i), 2 * x + core), device_id_type=MESH,
        ).start()
    pltpu.make_async_copy(stat_ref, stats.at[me], stat_recv).start()
    bias_own = pltpu.make_async_copy(ub_ref, bbuf.at[core], bias_sem.at[0])
    bias_mate = pltpu.make_async_remote_copy(
        src_ref=ub_ref, dst_ref=bbuf.at[core], send_sem=bias_sem.at[1], recv_sem=bias_sem.at[2],
        device_id=(me, 2 * x + mate), device_id_type=MESH,
    )
    bias_own.start()
    bias_mate.start()

    @pl.when(goal != core)
    def _():
        mate_w().start()

    @pl.when(goal == core)
    def _():
        pltpu.make_async_copy(wt_ref.at[me], wbuf.at[:, core, :, kat], wrecv_sem).start()


    def origin(colour, dp, ds):
        dy = colour * dp + (1 - colour) * ds
        dz = colour * ds + (1 - colour) * dp
        return lax.rem(y - dy + SIDE, SIDE) * SIDE + lax.rem(z - dz + SIDE, SIDE)

    def norm(colour, dp, pieces):
        base = core * HALF + colour * PART

        @pl.loop(0, SIDE)
        def _(ds):
            turned = stats[origin(colour, dp, ds)].T
            center, spread = turned[:, 0:1], turned[:, 1:2]
            rows = pl.ds(pl.multiple_of(ds * NEW, NEW), NEW)
            for raw, lane, width in pieces(colour, dp * SIDE + ds):
                value = (raw.astype(jnp.float32) - center) * spread
                at = pl.ds(pl.multiple_of(base + lane, 256), width)
                to = pl.ds(pl.multiple_of(lane, 256), width)
                for kind, (gain, shift) in enumerate(((gain0, gain1), (gain2, gain3))):
                    nbuf[colour, dp, kind, rows, to] = (
                        value * gain[:, at] + shift[:, at]
                    ).astype(jnp.bfloat16)

    def side_lane(dx):
        return DIRECT + 256 * lax.rem(x - dx + SIDE, SIDE)

    def early(colour, s):
        yield xbuf[colour, s, :, 0:DIRECT], 0, DIRECT
        yield xbuf[colour, s, :, DIRECT:DIRECT + 256], DIRECT + 256 * x, 256
        for dx in (1, 3):
            yield sbuf[colour, dx - 1, s], side_lane(dx), 256

    def late(colour, s):
        yield sbuf[colour, 1, s], side_lane(2), 256

    def compute(colour, dp):
        norm(colour, dp, late)
        for kind in (0, 1):
            left = wbuf[kind, :, :, pl.ds(pl.multiple_of(colour * PART, PART), PART)]
            product = lax.dot_general(
                left.reshape(192, PART), nbuf[colour, dp, kind], NT,
                preferred_element_type=jnp.float32,
            )
            for ds in range(SIDE):
                row = origin(colour, dp, ds)
                pbuf[row, 192 * kind:192 * (kind + 1), :] += product[:, ds * NEW:(ds + 1) * NEW]

    for i in range(SIDE):
        ring_second(send, arrived, i)
        side_out(1, gray(i))

    weights_out(1, 15)
    pltpu.make_async_copy(stats, stats, stat_recv).wait()
    for dp in (1, 3, 2):
        side_on(0, dp)

    @pl.loop(0, SIDE)
    def _(i):
        side_on(1, gray(i))

        @pl.loop(0, 2)
        def _(colour):
            norm(colour, gray(i), early)

    pltpu.make_async_copy(wbuf, wbuf, wrecv_sem).wait()

    def pair_out(last):
        @pl.loop(0, 16)
        def _(j):
            dy, dz = j // SIDE, j % SIDE
            row = origin(0, dz, dy)
            final = jnp.logical_or(dy == 2, dz == 2)

            @pl.when(jnp.logical_and(row // 8 != core, final == last))
            def _():
                pltpu.make_async_remote_copy(
                    src_ref=pbuf.at[row], dst_ref=rbuf.at[lax.rem(row, 8)],
                    send_sem=pair_sem.at[0], recv_sem=pair_sem.at[1],
                    device_id=(me, 2 * x + mate), device_id_type=MESH,
                ).start()


    @pl.loop(0, SIDE)
    def _(i):
        dp = gray(i)
        for colour in (0, 1):
            for n in (2, 3):
                side_wait(colour, 1, dp, n)

            @pl.when(i > 0)
            def _():
                for n in (2, 3):
                    side_wait(colour, 0, dp, n)

        @pl.loop(0, 2)
        def _(colour):
            compute(colour, dp)

        @pl.when(i >= 2)
        def _():
            pair_out(i == 3)

    bias_own.wait()
    bias_mate.wait()
    pltpu.make_async_copy(rbuf, rbuf, pair_sem.at[1]).wait()
    mine = pl.ds(pl.multiple_of(me * 72, 8), 72)

    @pl.loop(0, 8)
    def _(q):
        row = 8 * core + q
        total = pbuf[row] + rbuf[q]
        for h in (0, 1):
            qsend[2 * q + h] = total[96 * h:96 * h + 72]
            remote = pltpu.make_async_remote_copy(
                src_ref=qsend.at[2 * q + h], dst_ref=qrecv.at[mine],
                send_sem=qsend_sem, recv_sem=qrecv_sem,
                device_id=(row, 2 * x + h), device_id_type=MESH,
            )
            away = jnp.logical_or(row != me, core != h)

            @pl.when(away)
            def _():
                remote.start()

            @pl.when(jnp.logical_not(away))
            def _():
                pltpu.make_async_copy(qsend.at[2 * q + h], qrecv.at[mine], qrecv_sem).start()
        at = pl.ds(pl.multiple_of(q * NEW, NEW), NEW)
        for h in (0, 1):
            u = total[192 + 96 * h:288 + 96 * h] + bbuf[h]
            inner = 0.7978845608028654 * (u + 0.044715 * (u * u * u))
            units_ref[h, :, at] = (0.5 * u * (1.0 + jnp.tanh(inner))).astype(jnp.bfloat16)

    pltpu.make_async_copy(qrecv, qrecv, qrecv_sem).wait()
    qkv_ref[...] = qrecv[...]
    some = pbuf.at[pl.ds(0, 8)]
    pltpu.make_async_copy(some, some, pair_sem.at[0]).wait()

    @pl.when(goal == core)
    def _():
        some = qsend.at[pl.ds(0, 15)]
        pltpu.make_async_copy(some, some, qsend_sem).wait()

    @pl.when(goal != core)
    def _():
        pltpu.make_async_copy(qsend, qsend, qsend_sem).wait()
        mate_w().wait_send()

    some = wt_ref.at[pl.ds(0, 15)]
    pltpu.make_async_copy(some, some, wsend_sem).wait()
    for colour in (0, 1):
        some = xbuf.at[colour, pl.ds(1, 15)]
        pltpu.make_async_copy(some, some, xsend_sem.at[colour]).wait()
        some = sbuf.at[colour, :, pl.ds(1, 15)]
        pltpu.make_async_copy(some, some, side_send.at[colour]).wait()
    some = stats.at[pl.ds(0, 15)]
    pltpu.make_async_copy(some, some, stat_send).wait()


def front(hidden, gains, qkv_weight, up_weight, up_bias):
    vmem = pl.BlockSpec(memory_space=pltpu.VMEM)
    hbm = pl.BlockSpec(memory_space=pl.ANY)
    dma = pltpu.SemaphoreType.DMA
    return pl.pallas_call(
        front_kernel,
        out_shape=(
            jax.ShapeDtypeStruct((1152, NEW), jnp.float32),
            jax.ShapeDtypeStruct((2, 96, 1024), jnp.bfloat16),
        ),
        in_specs=[vmem] * 8,
        out_specs=(vmem, vmem),
        scratch_shapes=[
            pltpu.VMEM((PART, 384), jnp.float32),
            pltpu.VMEM((16, 2, 96, 384), jnp.bfloat16),
            pltpu.VMEM((8, NEW), jnp.float32),
            pltpu.VMEM((PART, 8), jnp.float32),
            pltpu.VMEM((96, NEW), jnp.float32),
            pltpu.VMEM((2, 16, NEW, DIRECT + 256), jnp.bfloat16),
            pltpu.VMEM((2, 3, 16, NEW, 256), jnp.bfloat16),
            pltpu.VMEM((16, 8, NEW), jnp.float32),
            pltpu.VMEM((2, 2, 96, HALF), jnp.bfloat16),
            pltpu.VMEM((2, SIDE, 2, 512, PART), jnp.bfloat16),
            pltpu.VMEM((16, 384, NEW), jnp.float32),
            pltpu.VMEM((8, 384, NEW), jnp.float32),
            pltpu.VMEM((2, 96, NEW), jnp.float32),
            pltpu.VMEM((16, 72, NEW), jnp.float32),
            pltpu.VMEM((1152, NEW), jnp.float32),
            dma((2,)), dma((2, 2, 16)), dma((2, 5)), dma((2,)), dma((2, 2, 4, 4)), dma, dma,
            dma, dma, dma, dma((3,)), dma((2,)), dma, dma,
        ],
        compiler_params=pltpu.CompilerParams(
            collective_id=0, has_side_effects=True, vmem_limit_bytes=VMEM_LIMIT
        ),
        name="front",
    )(hidden, qkv_weight, up_weight, *(gain[None, :] for gain in gains), up_bias)


def back_kernel(
    len_ref, units_ref, qkv_ref, qbias_ref, cos_ref, sin_ref, k_hbm, v_hbm,
    wd_ref, wo_ref, rest_ref, bias_a, bias_b, out_ref, nk_ref, nv_ref,
    ubuf, aring, amate, dbuf, obuf, dturn, total, tsend, rsum, share, rest, fout,
    kbuf, vbuf, sbuf, qexp, vkeep, att_ref, ksem, vsem,
    usend_sem, urecv_sem, own_sem, asend_sem, arecv_sem, amate_sem, w_sem,
    hsend_sem, hrecv_sem, rsend_sem, rrecv_sem, fsend_sem, frecv_sem, gsend_sem, grecv_sem,
):
    for hbm, buf, sem in ((k_hbm, kbuf, ksem), (v_hbm, vbuf, vsem)):
        for n in range(CACHE // KB):
            fetch(n, hbm, buf, sem).start()
    y, z, x, core = place()
    me = y * SIDE + z
    mate = 1 - core
    goal = y // 2
    barrier = pltpu.get_barrier_semaphore()

    def plane(i):
        return (i // 2, 2 * x + i % 2)

    def line(i):
        return (me, i)

    meet(barrier, [
        (32, plane, lambda i: i != 2 * me + core),
        (8, line, lambda i: i // 2 != x),
    ])
    pl.semaphore_wait(barrier, 37)

    def apart(s, colour, half):
        return aring.at[s, pl.ds(32 * (2 * colour + half), 32)]

    def aown(colour, half):
        return att_ref.at[pl.ds(32 * (2 * colour + half), 32)]

    asend, aarrived = ring_units(y, z, x, core, aown, Absolute(y, z), apart, asend_sem, arecv_sem)

    def lanes(colour, half):
        return pl.ds((2 * colour + half) * 256, 256)

    def part(s, colour, half):
        return ubuf.at[:, s, :, lanes(colour, half)]

    def own(colour, half):
        return units_ref.at[:, :, lanes(colour, half)]

    send, arrived = ring_units(y, z, x, core, own, Absolute(y, z), part, usend_sem, urecv_sem)
    ring_start(send)
    copies = [pltpu.make_async_copy(units_ref, ubuf.at[:, me], own_sem.at[0])]
    for n, (src, dst) in enumerate(((wd_ref, dbuf), (wo_ref, obuf))):
        copies.append(pltpu.make_async_copy(src, dst.at[core], w_sem.at[3 * n]))
        copies.append(pltpu.make_async_remote_copy(
            src_ref=src, dst_ref=dst.at[core], send_sem=w_sem.at[3 * n + 1],
            recv_sem=w_sem.at[3 * n + 2], device_id=(me, 2 * x + mate), device_id_type=MESH,
        ))
    for copy in copies:
        copy.start()
    slot = me % 8

    def tile(row):
        return rest_ref.at[
            pl.ds(pl.multiple_of(32 * x, 32), 32), pl.ds(pl.multiple_of(384 * row, 384), 384)
        ]

    @pl.when(goal == core)
    def _():
        @pl.loop(1, 16)
        def _(i):
            row = lax.rem(y + i // SIDE, SIDE) * SIDE + lax.rem(z + i % SIDE, SIDE)
            pltpu.make_async_remote_copy(
                src_ref=tile(row), dst_ref=rest.at[slot],
                send_sem=hsend_sem, recv_sem=hrecv_sem,
                device_id=(row, 2 * x + core), device_id_type=MESH,
            ).start()
        pltpu.make_async_copy(tile(me), rest.at[slot], hrecv_sem).start()

    heads = HEADS_HERE
    keep = (vkeep, qexp, sbuf)

    def key_block(n, at):
        fetch(n, k_hbm, kbuf, ksem).wait()
        return kbuf[at, :]

    def value_block(n, at):
        fetch(n, v_hbm, vbuf, vsem).wait()
        return vbuf[at, :]

    top = attention_scores(
        heads, len_ref[0], qkv_ref, qbias_ref, cos_ref, sin_ref, nk_ref, nv_ref, keep, key_block)
    ring_first(send, arrived)
    attention_mix(heads, top, keep, att_ref, value_block)
    att_own = pltpu.make_async_copy(att_ref, aring.at[me], own_sem.at[1])
    att_own.start()
    two_start(asend)
    for copy in copies:
        copy.wait()

    def turn(first, count):
        @pl.loop(first, first + count)
        def _(n):
            h, at = n // 12, pl.ds(pl.multiple_of((n % 12) * 128, 128), 128)
            dturn[h, :, at] = dbuf[h, at, :].T

    ring_second(send, arrived, 0)
    turn(0, 12)
    two_first(asend, aarrived)
    ring_second(send, arrived, 1)
    turn(12, 12)
    two_second(aarrived)
    att_own.wait()
    pair = pltpu.make_async_remote_copy(
        src_ref=aring.at[pl.ds(8 * mate, 8)], dst_ref=amate,
        send_sem=amate_sem.at[0], recv_sem=amate_sem.at[1],
        device_id=(me, 2 * x + mate), device_id_type=MESH,
    )
    pair.start()
    ring_second(send, arrived, 2)
    ring_second(send, arrived, 3)
    pair.wait_recv()

    def rcopy(q, step):
        to = lax.rem(x + step, SIDE)
        return pltpu.make_async_remote_copy(
            src_ref=tsend.at[q, pl.ds(pl.multiple_of(32 * to, 32), 32)],
            dst_ref=rsum.at[step - 1, q],
            send_sem=rsend_sem.at[step - 1], recv_sem=rrecv_sem.at[step - 1],
            device_id=(me, 2 * to + core), device_id_type=MESH,
        )

    @pl.loop(0, 4)
    def _(p):
        at = pl.ds(pl.multiple_of(2 * p * NEW, 2 * NEW), 2 * NEW)
        turned = jnp.zeros((384, 2 * NEW), jnp.float32)
        for h in (0, 1):
            turned += jnp.dot(
                dturn[h], ubuf[h, :, :, at].reshape(PART, 2 * NEW),
                preferred_element_type=jnp.float32,
            )
        for n in (0, 1):
            q = 2 * p + n
            value = turned[:, n * NEW:(n + 1) * NEW].T
            value += jnp.dot(
                aring[8 * core + q], obuf[core], preferred_element_type=jnp.float32
            ) + jnp.dot(amate[q], obuf[mate], preferred_element_type=jnp.float32)
            total[q] = value
            tsend[q] = value.astype(jnp.bfloat16)
        for n in (0, 1):
            for step in (2, 1, 3):
                rcopy(2 * p + n, step).start()

    pltpu.make_async_copy(rest, rest, hrecv_sem).wait()
    for step in (1, 3, 2):
        some = rsum.at[step - 1]
        pltpu.make_async_copy(some, some, rrecv_sem.at[step - 1]).wait()
    rows = pl.ds(pl.multiple_of(32 * x, 32), 32)
    mine = pl.ds(pl.multiple_of(384 * me, 384), 384)
    bias_here = bias_a[:, mine] + bias_b[:, mine]

    @pl.loop(0, 8)
    def _(q):
        value = total[q, rows, :] + rsum[0, q].astype(jnp.float32)
        value += rsum[1, q].astype(jnp.float32) + rsum[2, q].astype(jnp.float32)
        share[q] = (rest[q].astype(jnp.float32) + (value + bias_here)).astype(jnp.bfloat16)
        row = 8 * core + q

        @pl.when(row != me)
        def _():
            pltpu.make_async_remote_copy(
                src_ref=share.at[q], dst_ref=fout.at[rows, mine],
                send_sem=fsend_sem, recv_sem=frecv_sem,
                device_id=(row, 2 * x + goal), device_id_type=MESH,
            ).start()

        @pl.when(row == me)
        def _():
            pltpu.make_async_copy(share.at[q], fout.at[rows, mine], frecv_sem).start()

    def piece(owner, c):
        return fout.at[
            pl.ds(pl.multiple_of(32 * owner, 32), 32), pl.ds(pl.multiple_of(c * HALF, HALF), HALF)
        ]

    def gcopy(step):
        to = lax.rem(x + step + SIDE, SIDE)
        way = (1 - step) // 2
        return pltpu.make_async_remote_copy(
            src_ref=piece(x, core), dst_ref=piece(x, core), send_sem=gsend_sem.at[0, way],
            recv_sem=grecv_sem.at[0, way], device_id=(me, 2 * to + core), device_id_type=MESH,
        )

    def strip(owner, way):
        return fout.at[
            pl.ds(pl.multiple_of(32 * owner + 16 * way, 16), 16),
            pl.ds(pl.multiple_of(core * HALF, HALF), HALF),
        ]

    def grelay(step):
        to = lax.rem(x + step + SIDE, SIDE)
        owner = lax.rem(x - step + SIDE, SIDE)
        way = (1 - step) // 2
        return pltpu.make_async_remote_copy(
            src_ref=strip(owner, way), dst_ref=strip(owner, way), send_sem=gsend_sem.at[0, 2 + way],
            recv_sem=grecv_sem.at[0, 2 + way], device_id=(me, 2 * to + core), device_id_type=MESH,
        )

    def pass_on(step):
        owner = lax.rem(x - step + SIDE, SIDE)
        return pltpu.make_async_remote_copy(
            src_ref=piece(owner, core), dst_ref=piece(owner, core), send_sem=gsend_sem.at[1, step],
            recv_sem=grecv_sem.at[1, step], device_id=(me, 2 * x + mate), device_id_type=MESH,
        )

    def landed(kind, n, ref):
        pltpu.make_async_copy(ref, ref, grecv_sem.at[kind, n]).wait()

    def owner_at(step):
        return lax.rem(x - step + SIDE, SIDE)

    pltpu.make_async_copy(piece(x, core), piece(x, core), frecv_sem).wait()
    for step in (1, -1):
        gcopy(step).start()
    pass_on(0).start()
    for step in (1, -1):
        landed(0, (1 - step) // 2, piece(owner_at(step), core))
        grelay(step).start()
        pass_on(step % SIDE).start()
    for way in (0, 1):
        landed(0, 2 + way, strip(owner_at(2), way))
    pass_on(2).start()
    for step in (0, 1, 3, 2):
        landed(1, step, piece(owner_at(step), mate))
    out_ref[...] = fout[...]

    for step in (1, -1):
        gcopy(step).wait_send()
        grelay(step).wait_send()
    for step in (1, 2, 3):
        some = rsum.at[step - 1]
        pltpu.make_async_copy(some, some, rsend_sem.at[step - 1]).wait()
    for step in range(4):
        pass_on(step).wait_send()
    pair.wait_send()

    @pl.when(goal == core)
    def _():
        some = share.at[pl.ds(0, 7)]
        pltpu.make_async_copy(some, some, fsend_sem).wait()
        some = rest_ref.at[pl.ds(0, 32), pl.ds(0, 15 * 384)]
        pltpu.make_async_copy(some, some, hsend_sem).wait()

    @pl.when(goal != core)
    def _():
        pltpu.make_async_copy(share, share, fsend_sem).wait()

    for colour in (0, 1):
        some = ubuf.at[:, pl.ds(0, 15), :, pl.ds(512 * colour, 512)]
        pltpu.make_async_copy(some, some, usend_sem.at[colour]).wait()
        some = aring.at[pl.ds(0, 15), pl.ds(64 * colour, 64)]
        pltpu.make_async_copy(some, some, asend_sem.at[colour]).wait()


def back(units, qkv, qkv_bias, length, keys_old, values_old, hidden, out_weight, down_weight, biases):
    cosine, sine = rotation_tables(length[0])
    vmem = pl.BlockSpec(memory_space=pltpu.VMEM)
    hbm = pl.BlockSpec(memory_space=pl.ANY)
    dma = pltpu.SemaphoreType.DMA
    return pl.pallas_call(
        back_kernel,
        out_shape=(
            jax.ShapeDtypeStruct((NEW, 2 * HALF), jnp.bfloat16),
            jax.ShapeDtypeStruct((NEW, 384), jnp.bfloat16),
            jax.ShapeDtypeStruct((NEW, 384), jnp.bfloat16),
        ),
        in_specs=[
            pl.BlockSpec(memory_space=pltpu.SMEM), hbm, vmem, vmem, vmem, vmem, hbm, hbm,
            hbm, hbm, hbm, vmem, vmem,
        ],
        out_specs=(vmem, vmem, vmem),
        scratch_shapes=[
            pltpu.VMEM((2, 16, 96, 1024), jnp.bfloat16),
            pltpu.VMEM((16, NEW, 384), jnp.bfloat16),
            pltpu.VMEM((8, NEW, 384), jnp.bfloat16),
            pltpu.VMEM((2, PART, 384), jnp.bfloat16),
            pltpu.VMEM((2, 384, 384), jnp.bfloat16),
            pltpu.VMEM((2, 384, PART), jnp.bfloat16),
            pltpu.VMEM((8, NEW, 384), jnp.float32),
            pltpu.VMEM((8, NEW, 384), jnp.bfloat16),
            pltpu.VMEM((3, 8, 32, 384), jnp.bfloat16),
            pltpu.VMEM((8, 32, 384), jnp.bfloat16),
            pltpu.VMEM((8, 32, 384), jnp.bfloat16),
            pltpu.VMEM((NEW, 2 * HALF), jnp.bfloat16),
            pltpu.VMEM((CACHE, 384), jnp.bfloat16),
            pltpu.VMEM((CACHE, 384), jnp.bfloat16),
            pltpu.VMEM((HEADS_HERE * NEW, CACHE + NEW), jnp.float32),
            pltpu.VMEM((HEADS_HERE * NEW, 384), jnp.bfloat16),
            pltpu.VMEM((NEW, 384), jnp.bfloat16),
            pltpu.VMEM((NEW, 384), jnp.bfloat16),
            dma((CACHE // KB,)), dma((CACHE // KB,)),
            dma((2,)), dma((2, 2, 16)), dma((2,)), dma((2,)), dma((2, 2, 16)), dma((2,)), dma((6,)),
            dma, dma, dma((3,)), dma((3,)), dma, dma, dma((2, 4)), dma((2, 4)),
        ],
        compiler_params=pltpu.CompilerParams(
            collective_id=1, has_side_effects=True, vmem_limit_bytes=VMEM_LIMIT
        ),
        name="back",
    )(length, units, qkv, qkv_bias, cosine, sine, keys_old, values_old,
      down_weight, out_weight, hidden, biases[0][None, :], biases[1][None, :])


def body(
    hidden,
    attn_norm_gain,
    attn_norm_bias,
    mlp_norm_gain,
    mlp_norm_bias,
    qkv_weight,
    qkv_bias,
    out_weight,
    out_bias,
    up_weight,
    up_bias,
    down_weight,
    down_bias,
    cache_keys,
    cache_values,
    cached_len,
):
    gains = (attn_norm_gain, attn_norm_bias, mlp_norm_gain, mlp_norm_bias)
    qkv, units = front(hidden, gains, qkv_weight, up_weight, up_bias)
    result, key_rows, value_rows = back(
        units, qkv, qkv_bias, cached_len, cache_keys[0], cache_values[0],
        hidden, out_weight, down_weight, (out_bias, down_bias),
    )
    return (result, key_rows[None], value_rows[None])


def solution(mesh):
    return jax.shard_map(
        body,
        mesh=mesh,
        in_specs=(
            P("req", None),
            P(),
            P(),
            P(),
            P(),
            P("req", "head"),
            P("head"),
            P("head", "req"),
            P(),
            P("req", "head"),
            P("head"),
            P("head", "req"),
            P(),
            P("req", None, "head"),
            P("req", None, "head"),
            P("req"),
        ),
        out_specs=(P("req", None), P("req", None, "head"), P("req", None, "head")),
        check_vma=False,
    )
```
